512 devices in a mesh: wide: 32 (over z, core), narrow: 16 (over y, x).
Axes of the slice: x: 4, y: 4, z: 16, core: 2. Of those that a mesh axis runs over, the one named last changes fastest.
Arguments:
- hidden: bfloat16 [2048, 2048], P('wide'), may hold values from -6 to 6
- attn_gain: float32 [2048], replicated, may hold values from 0.1 to 1.9
- expert_gain: float32 [2048], replicated, may hold values from 0.1 to 1.9
- query_weight: bfloat16 [2048, 2048], P('wide', 'narrow'), may hold values from -0.125 to 0.125
- key_weight: bfloat16 [2048, 2048], P('wide', 'narrow'), may hold values from -0.125 to 0.125
- value_weight: bfloat16 [2048, 2048], P('wide', 'narrow'), may hold values from -0.125 to 0.125
- output_weight: bfloat16 [2048, 2048], P('wide', 'narrow'), may hold values from -0.125 to 0.125
- router_weight: bfloat16 [2048, 64], replicated, may hold values from -0.125 to 0.125
- gate_weight: bfloat16 [64, 2048, 1024], P('wide', None, 'narrow'), may hold values from -0.125 to 0.125
- up_weight: bfloat16 [64, 2048, 1024], P('wide', None, 'narrow'), may hold values from -0.125 to 0.125
- down_weight: bfloat16 [64, 1024, 2048], P('wide', 'narrow'), may hold values from -0.1875 to 0.1875
- prefix_keys: bfloat16 [256, 8, 2048], P('wide', None, 'narrow'), may hold values from -6 to 6
- prefix_values: bfloat16 [256, 8, 2048], P('wide', None, 'narrow'), may hold values from -6 to 6
- cache_keys: bfloat16 [32, 1024, 2048], P('wide', None, 'narrow'), may hold values from -256 to 256
- cache_values: bfloat16 [32, 1024, 2048], P('wide', None, 'narrow'), may hold values from -6 to 6
- parents: int32 [32, 64], P('wide'), may hold values from 0 to 62, as said below
- cache_lengths: int32 [32], P('wide'), may hold values from 1 to 960, 15360 in all
- group_ids: int32 [32], replicated, may hold values from 0 to 7
- expert_ids: int32 [2048, 8], P('wide'), may hold values from 0 to 63, all different within a row; in each aligned block of 64 rows (0 to 63, 64 to 127, ...) at most 9 rows name the same one
- accepted: int32 [32], P('wide'), may hold values from 0 to 63
Outputs:
- layer_out: bfloat16 [2048, 2048], P('wide', 'narrow')
- new_keys: bfloat16 [32, 1024, 2048], P('wide', None, 'narrow')
- new_values: bfloat16 [32, 1024, 2048], P('wide', None, 'narrow')
The draws below stay inside these ranges and needn't reach their ends.
Inputs may be any that keep to these rules, and one draw needn't show every extreme that they name: `parents`: node 0 of each tree is the root and its own parent; node i > 0 has its parent among nodes max(0, i - 4) to i - 1; the parent of node 63 is node 62. `expert_ids`: the 8 experts of a token differ; among the tokens of one index of wide no expert is named more than 9 times, a bound that some block reaches in some of them.
All inputs are finite; a program needn't handle non-finite values. No bound on the sum of `cache_lengths` on one device may be relied on, other than what follows from the above.
Results may differ from the reference program's by a relative error of at most 0.01.
The reference program's roundings to bfloat16 on the way count: a program that leaves them out, or rounds other values in their place, can miss the bound.
Values may be sent and summed in bfloat16 or wider, within the bound.
A program may use at most 64 MiB of HBM per device.

```python
import math
import jax
import jax.numpy as jnp
import numpy as np
from jax import lax

D = 2048
HEADS = 16
HD = 128
E = 64
FF = 1024
TOPK = 8
TREE = 64
CACHE = 1024
SINK = 4
WIN = 512
G = 8
PRE = 256
REQS = 32
TOK_DEV = 64
TOKENS = 2048
CAP = 9
N_WIDE = 32
N_NARROW = 16


def draw_cache_keys(key, part):
    base = jax.random.normal(key, (REQS, CACHE, HEADS * HD), jnp.float32)
    return jnp.clip(base, -256.0, 256.0).astype(jnp.bfloat16)


def draw_parents(key, part):
    random_bits = jax.random.randint(key, (REQS, TREE), 0, 1 << 30, dtype=jnp.int32)
    node_ids = jnp.arange(TREE, dtype=jnp.int32)
    lowest = jnp.maximum(node_ids - 4, 0)
    spread = jnp.maximum(node_ids - lowest, 1)
    drawn = jnp.where(node_ids > 0, lowest + random_bits % spread, 0)
    drawn = jnp.where(node_ids == TREE - 1, TREE - 2, drawn)
    return drawn.astype(jnp.int32)


def plant(array, own_key, least, largest):
    longest = array.shape.index(max(array.shape))
    spots = []
    for shift in (0, 1):
        where = [jax.random.randint(jax.random.fold_in(own_key, axis), (), 0, length) for axis, length in enumerate(array.shape)]
        where[longest] = (where[longest] + shift) % array.shape[longest]
        spots.append(tuple(where))
    return array.at[spots[0]].set(least).at[spots[1]].set(largest)


def block_levels(stream_key, shape, split, smallest, top_value):
    loudness = 1.0
    for dim, blocks in split:
        heights = jax.random.uniform(jax.random.fold_in(jax.random.fold_in(stream_key, 6), dim), (blocks,), jnp.float32, smallest / len(split), top_value / len(split))
        loudness = loudness * jnp.repeat(jnp.exp(heights), shape[dim] // blocks).reshape((-1,) + (1,) * (len(shape) - 1 - dim))
    return loudness


def length_profile(number_of, total, limit, slope):
    weights = [(1 << 20) // math.isqrt(grade ** slope) + 1 for grade in range(2, number_of + 1)]
    spare, counts = total - limit - (number_of - 1), [1] * (number_of - 1)
    while spare > 0:
        movable = [i for i in range(number_of - 1) if counts[i] < limit]
        pool, left = sum([weights[i] for i in movable]), spare
        for i in movable:
            extra = min(limit - counts[i], max(1, left * weights[i] // pool), spare)
            counts[i] = counts[i] + extra
            spare = spare - extra
    return np.array([limit] + counts)


def ragged_sizes(stream_key, number_of, total, most, slope):
    if number_of == 2:
        one = jax.random.randint(stream_key, (), max(1, total - most), min(most, total - 1) + 1)
        return jnp.stack([one, total - one])
    tallies = jnp.asarray(length_profile(number_of, total, most, slope), jnp.int32)
    twos = (number_of - 1) // 2
    giver, sink = tallies[1:1 + 2 * twos:2], tallies[2:2 + 2 * twos:2]
    margin = jnp.minimum(giver - 1, most - sink)
    shifted = jax.random.randint(jax.random.fold_in(stream_key, 1), (twos,), 0, 1 << 20) % (margin + 1)
    tallies = tallies.at[1:1 + 2 * twos:2].set(giver - shifted).at[2:2 + 2 * twos:2].set(sink + shifted)
    return tallies[jax.random.permutation(jax.random.fold_in(stream_key, 2), number_of)]


def deal_out(stream_key, own, number, rows, amount, top, most, skew):
    order = jax.random.permutation(stream_key, amount)
    crowded, ordinary = load_shares(amount, rows * top, most, skew, True), load_shares(amount, rows * top, most, skew, False)
    places = jnp.arange(amount)

    def named(lengths, offset_by):
        used = int((lengths > 0).sum())
        fixed = max(1, used // 4)
        moved = fixed + (places - fixed + offset_by * (used - fixed)) % max(1, amount - fixed)
        return jnp.zeros((amount,), jnp.int32).at[order[jnp.where(places < fixed, places, moved)]].set(jnp.asarray(lengths, jnp.int32))

    lengths = jnp.where(number % 4 == 0, named(crowded, number // 4), named(ordinary, number - number // 4 - 1))
    mixed = jax.random.permutation(jax.random.fold_in(own, 3), amount)
    donor, taker = mixed[0:amount // 2 * 2:2], mixed[1:amount // 2 * 2:2]
    slack = jnp.minimum(lengths[donor] - 1, most - lengths[taker]) // 2
    slack = jnp.where((donor == order[0]) | (taker == order[0]) | (lengths[taker] == 0), 0, jnp.maximum(slack, 0))
    moved = jax.random.randint(jax.random.fold_in(own, 4), (amount // 2,), 0, 1 << 20) % (slack + 1)
    lengths = lengths.at[donor].add(-moved).at[taker].add(moved)
    members = jnp.searchsorted(jnp.cumsum(lengths), jnp.arange(rows * top), side="right").astype(jnp.int32)
    table = members.reshape(top, rows).T
    table = table[jax.random.permutation(jax.random.fold_in(own, 1), rows)]
    offset_by = jax.random.randint(jax.random.fold_in(own, 2), (rows, 1), 0, top)
    return jnp.take_along_axis(table, (jnp.arange(top)[None, :] + offset_by) % top, axis=1)


def load_shares(amount, total, most, skew, full):
    loads = [(1 << 20) // math.isqrt(standing ** skew) + 1 for standing in range(1, amount + 1)]
    largest = most if full else min(most, max(-(-total // amount), total * loads[0] // sum(loads)))
    least = 1 if total - largest >= amount - 1 else 0
    counts, surplus = [largest] + [least] * (amount - 1), total - largest - least * (amount - 1)
    while surplus > 0:
        free = [i for i in range(1, amount) if counts[i] < largest] or [i for i in range(1, amount) if counts[i] < most]
        mass, remaining = sum([loads[i] for i in free]), surplus
        for i in free:
            extra = min(most - counts[i], max(1, remaining * loads[i] // mass), surplus)
            counts[i] = counts[i] + extra
            surplus = surplus - extra
    return np.array(counts)


def gaussian(rng, dims, deviation, bound, cuts=(), kind=jnp.bfloat16):
    result = jax.random.normal(rng, dims, jnp.float32) * deviation
    if len(cuts) > 0:
        result = block_levels(rng, dims, cuts, -0.22, 0.18) * result
    return jnp.clip(result, min=-bound, max=bound).astype(kind)


def setup_inputs(seed: int = 0) -> dict:
    splits = jax.random.split(jax.random.key(seed), 21)
    hidden = gaussian(splits[0], (TOKENS, D), 1.0, 6.0, ((0, 32),))
    attn_gain = jnp.clip(1.0 + 0.18 * jax.random.normal(splits[1], (D,), jnp.float32), 0.1, 1.9)
    expert_gain = jnp.clip(1.0 + 0.18 * jax.random.normal(splits[2], (D,), jnp.float32), 0.1, 1.9)
    query_weight = gaussian(splits[3], (D, HEADS * HD), D ** -0.5, 0.125, ((0, 32), (1, 16)))
    key_weight = gaussian(splits[4], (D, HEADS * HD), D ** -0.5, 0.125, ((0, 32), (1, 16)))
    value_weight = gaussian(splits[5], (D, HEADS * HD), D ** -0.5, 0.125, ((0, 32), (1, 16)))
    output_weight = gaussian(splits[6], (D, HEADS * HD), (HEADS * HD) ** -0.5, 0.125, ((0, 32), (1, 16)))
    router_weight = gaussian(splits[7], (D, E), D ** -0.5, 0.125)
    gate_weight = gaussian(splits[8], (E, D, FF), D ** -0.5, 0.125, ((0, 32), (2, 16)))
    up_weight = gaussian(splits[9], (E, D, FF), D ** -0.5, 0.125, ((0, 32), (2, 16)))
    down_weight = gaussian(splits[10], (E, FF, D), FF ** -0.5, 0.1875, ((0, 32), (1, 16)))
    prefix_keys = gaussian(splits[11], (PRE, G, HEADS * HD), 1.0, 6.0, ((0, 32), (2, 16)))
    prefix_values = gaussian(splits[12], (PRE, G, HEADS * HD), 1.0, 6.0, ((0, 32), (2, 16)))
    cache_keys = draw_cache_keys(jax.random.fold_in(splits[20], 71), 0)
    cache_values = gaussian(splits[14], (REQS, CACHE, HEADS * HD), 1.0, 6.0, ((0, 32), (2, 16)))
    parents = draw_parents(jax.random.fold_in(splits[20], 71), 0)
    cache_lengths = ragged_sizes(splits[16], REQS, REQS * (CACHE - TREE) // 2, CACHE - TREE, 2).astype(jnp.int32)
    group_ids = plant(jax.random.randint(splits[17], (REQS,), 0, G), jax.random.fold_in(splits[17], 1), 0, G - 1).astype(jnp.int32)
    expert_ids_keys = jax.random.split(jax.random.fold_in(splits[18], 1), TOKENS // TOK_DEV)
    expert_ids_turns = jax.random.permutation(jax.random.fold_in(splits[18], 3), TOKENS // TOK_DEV)
    expert_ids = jax.vmap(lambda own, number: deal_out(jax.random.fold_in(splits[18], 2), own, number, TOK_DEV, E, TOPK, CAP, 2))(expert_ids_keys, expert_ids_turns).reshape((TOKENS, TOPK))
    accepted = plant(jax.random.randint(splits[19], (REQS,), 0, TREE), jax.random.fold_in(splits[19], 1), 0, TREE - 1).astype(jnp.int32)
    return {"hidden": hidden, "attn_gain": attn_gain, "expert_gain": expert_gain, "query_weight": query_weight, "key_weight": key_weight, "value_weight": value_weight, "output_weight": output_weight, "router_weight": router_weight, "gate_weight": gate_weight, "up_weight": up_weight, "down_weight": down_weight, "prefix_keys": prefix_keys, "prefix_values": prefix_values, "cache_keys": cache_keys, "cache_values": cache_values, "parents": parents, "cache_lengths": cache_lengths, "group_ids": group_ids, "expert_ids": expert_ids, "accepted": accepted}


norm_eps = 1e-06

def rms_scale(rows, row_gain):
    widened = rows.astype(jnp.float32)
    power_mean = lax.optimization_barrier(jnp.mean(widened * widened, axis=-1, keepdims=True))
    return (widened * lax.rsqrt(power_mean + norm_eps) * row_gain).astype(jnp.bfloat16)

def tree_links(parents):
    tree_size = parents.shape[-1]
    node_ids = jnp.arange(tree_size, dtype=jnp.int32)
    linked = (node_ids[:, None] == node_ids[None, :]) | (parents[..., :, None] == node_ids)
    jumper = parents
    for doubling in range(tree_size.bit_length()):
        hop_table = (jumper[..., :, None] == node_ids).astype(jnp.float32)
        through = jnp.einsum('...ij,...jk->...ik', hop_table, linked.astype(jnp.float32), precision=lax.Precision.HIGHEST)
        linked = linked | (through > 0.5)
        jumper = jnp.take_along_axis(jumper, jumper, axis=-1)
    depths = lax.optimization_barrier(jnp.sum(linked.astype(jnp.int32), axis=-1)) - 1
    return (linked, depths)

def reference(hidden, attn_gain, expert_gain, query_weight, key_weight, value_weight, output_weight, router_weight, gate_weight, up_weight, down_weight, prefix_keys, prefix_values, cache_keys, cache_values, parents, cache_lengths, group_ids, expert_ids, accepted):
    scale_factor = 1.0 / math.sqrt(HD)
    normed = rms_scale(hidden, attn_gain)
    queries = jnp.dot(normed, query_weight, preferred_element_type=jnp.float32).astype(jnp.bfloat16)
    keys_new = jnp.dot(normed, key_weight, preferred_element_type=jnp.float32).astype(jnp.bfloat16)
    values_new = jnp.dot(normed, value_weight, preferred_element_type=jnp.float32).astype(jnp.bfloat16)
    ancestry, depths = tree_links(parents)
    positions = jnp.arange(CACHE, dtype=jnp.int32)

    def attend(request):
        first_row = request * TREE
        query_rows = lax.dynamic_slice_in_dim(queries, first_row, TREE, 0).reshape(TREE, HEADS, HD).astype(jnp.float32)
        tree_keys = lax.dynamic_slice_in_dim(keys_new, first_row, TREE, 0).reshape(TREE, HEADS, HD)
        tree_values = lax.dynamic_slice_in_dim(values_new, first_row, TREE, 0).reshape(TREE, HEADS, HD)
        group_index = group_ids[request]
        shared_keys = lax.dynamic_index_in_dim(prefix_keys, group_index, 1, keepdims=False).reshape(PRE, HEADS, HD)
        shared_values = lax.dynamic_index_in_dim(prefix_values, group_index, 1, keepdims=False).reshape(PRE, HEADS, HD)
        own_keys = lax.dynamic_index_in_dim(cache_keys, request, 0, keepdims=False).reshape(CACHE, HEADS, HD)
        own_values = lax.dynamic_index_in_dim(cache_values, request, 0, keepdims=False).reshape(CACHE, HEADS, HD)
        key_rows = jnp.concatenate([shared_keys, own_keys, tree_keys], axis=0).astype(jnp.float32)
        value_rows = jnp.concatenate([shared_values, own_values, tree_values], axis=0).astype(jnp.float32)
        length = cache_lengths[request]
        cache_mask = (positions < length) & ((positions < SINK) | (positions >= length - WIN))
        tree_mask = lax.dynamic_index_in_dim(ancestry, request, 0, keepdims=False)
        allowed = jnp.concatenate([jnp.ones((TREE, PRE), dtype=jnp.bool_), jnp.broadcast_to(cache_mask[None, :], (TREE, CACHE)), tree_mask], axis=1)
        scores = jnp.einsum('qhd,khd->hqk', query_rows, key_rows, precision=lax.Precision.HIGHEST) * scale_factor
        row_top = lax.optimization_barrier(jnp.max(jnp.where(allowed, scores, -jnp.inf), axis=-1, keepdims=True))
        weights = jnp.where(allowed, jnp.exp(scores - row_top), 0.0)
        row_total = lax.optimization_barrier(jnp.sum(weights, axis=-1))
        rounded = lax.optimization_barrier(weights.astype(jnp.bfloat16)).astype(jnp.float32)
        weighted = jnp.einsum('hqk,khd->qhd', rounded, value_rows, precision=lax.Precision.HIGHEST)
        return (weighted / jnp.transpose(row_total)[:, :, None]).astype(jnp.bfloat16).reshape(TREE, HEADS * HD)
    attended = lax.map(attend, jnp.arange(REQS, dtype=jnp.int32)).reshape(TOKENS, HEADS * HD)
    projected = lax.dot_general(attended, output_weight, (((1,), (1,)), ((), ())), preferred_element_type=jnp.float32)
    mixed = (hidden.astype(jnp.float32) + projected).astype(jnp.bfloat16)
    normed_moe = rms_scale(mixed, expert_gain)
    logits = jnp.dot(normed_moe, router_weight, preferred_element_type=jnp.float32)
    chosen = jnp.take_along_axis(logits, expert_ids, axis=1)
    shares = jax.nn.softmax(chosen, axis=-1)
    assignments = TOKENS * TOPK
    flat_experts = expert_ids.reshape(-1)
    flat_tokens = jnp.arange(assignments, dtype=jnp.int32) // TOPK
    flat_shares = shares.reshape(-1)
    room = N_WIDE * CAP
    padded_rows = jnp.concatenate([normed_moe, jnp.zeros((1, D), jnp.bfloat16)], axis=0)
    block_width = FF // N_NARROW

    def expert_step(running, expert):
        picks = jnp.nonzero(flat_experts == expert, size=room, fill_value=assignments)[0].astype(jnp.int32)
        valid = picks < assignments
        safe_picks = jnp.minimum(picks, assignments - 1)
        token_rows = jnp.where(valid, flat_tokens[safe_picks], TOKENS).astype(jnp.int32)
        share_rows = jnp.where(valid, flat_shares[safe_picks], 0.0)
        inputs = padded_rows[token_rows].astype(jnp.float32)
        gate_matrix = lax.dynamic_index_in_dim(gate_weight, expert, 0, keepdims=False).astype(jnp.float32)
        up_matrix = lax.dynamic_index_in_dim(up_weight, expert, 0, keepdims=False).astype(jnp.float32)
        down_matrix = lax.dynamic_index_in_dim(down_weight, expert, 0, keepdims=False).astype(jnp.float32)
        gate_out = jnp.dot(inputs, gate_matrix, precision=lax.Precision.HIGHEST)
        up_out = jnp.dot(inputs, up_matrix, precision=lax.Precision.HIGHEST)
        activated = lax.optimization_barrier((jax.nn.silu(gate_out) * up_out).astype(jnp.bfloat16)).astype(jnp.float32)
        blocks = activated.reshape(room, N_NARROW, block_width)
        down_blocks = down_matrix.reshape(N_NARROW, block_width, D)
        pieces = jnp.einsum('rsf,sfd->rsd', blocks, down_blocks, precision=lax.Precision.HIGHEST)
        pieces = lax.optimization_barrier(pieces.astype(jnp.bfloat16)).astype(jnp.float32)
        summed = lax.optimization_barrier(jnp.sum(pieces, axis=1)) * share_rows[:, None]
        running = running.at[token_rows].add(summed, mode='drop')
        return (running, None)
    moe_total, unused = lax.scan(expert_step, jnp.zeros((TOKENS, D), jnp.float32), jnp.arange(E, dtype=jnp.int32))
    layer_out = (mixed.astype(jnp.float32) + moe_total).astype(jnp.bfloat16)
    on_path = jnp.take_along_axis(ancestry, accepted[:, None, None], axis=1)[:, 0, :]
    slots = jnp.where(on_path, cache_lengths[:, None] + depths, CACHE).astype(jnp.int32)
    request_rows = jnp.broadcast_to(jnp.arange(REQS, dtype=jnp.int32)[:, None], (REQS, TREE))
    new_keys = cache_keys.at[request_rows, slots].set(keys_new.reshape(REQS, TREE, HEADS * HD), mode='drop')
    new_values = cache_values.at[request_rows, slots].set(values_new.reshape(REQS, TREE, HEADS * HD), mode='drop')
    return (layer_out, new_keys, new_values)
```

```python
import math

import jax
import jax.numpy as jnp
from jax import lax
from jax.experimental import pallas as pl
from jax.experimental.pallas import tpu as pltpu
from jax.sharding import PartitionSpec as P

HD = 128
E = 64
SINK = 4
WIN = 512
CAP = 9
NX = 4
NY = 4
MESH = pl.DeviceIdType.MESH
F32 = jnp.float32
BF16 = jnp.bfloat16

norm_eps = 1e-06


def rms_scale(rows, row_gain):
    widened = rows.astype(F32)
    power_mean = jnp.mean(widened * widened, axis=-1, keepdims=True)
    return (widened * lax.rsqrt(power_mean + norm_eps) * row_gain).astype(BF16)


def tree_links(parents):
    tree_size = parents.shape[-1]
    node_ids = jnp.arange(tree_size, dtype=jnp.int32)
    linked = (node_ids[:, None] == node_ids[None, :]) | (parents[0][:, None] == node_ids)
    for _ in range(6):
        m = linked.astype(BF16)
        linked = jnp.dot(m, m, preferred_element_type=F32) > 0.5
    depths = jnp.sum(linked.astype(jnp.int32), axis=-1) - 1
    return linked, depths


def rcopy(src, dst, ssem, rsem, dev):
    return pltpu.make_async_remote_copy(
        src_ref=src, dst_ref=dst, send_sem=ssem, recv_sem=rsem, device_id=dev, device_id_type=MESH
    )


def wide_barrier(w, n, nw):
    barrier = pltpu.get_barrier_semaphore()

    def sig(d, _):
        pl.semaphore_signal(barrier, inc=1, device_id=(lax.rem(w + d, nw), n), device_id_type=MESH)
        return 0

    lax.fori_loop(1, nw, sig, 0)
    pl.semaphore_wait(barrier, nw - 1)


def narrow_barrier(w, n, nn):
    barrier = pltpu.get_barrier_semaphore()

    def sig(d, _):
        pl.semaphore_signal(barrier, inc=1, device_id=(w, lax.rem(n + d, nn)), device_id_type=MESH)
        return 0

    lax.fori_loop(1, nn, sig, 0)
    pl.semaphore_wait(barrier, nn - 1)


def gather_kernel(nw, q, k, v, o, ps, gq, gk, gv, go, pr, rs, rr, bs, br, fs, fr, pss, psr, ls):
    nz = nw // 2
    hops_r = nz // 2
    hops_l = nz - 1 - hops_r
    w = lax.axis_index("wide")
    n = lax.axis_index("narrow")
    z = w // 2
    c = lax.rem(w, 2)
    sib = (w + 1 - 2 * c, n)
    right = (lax.rem(z + 1, nz) * 2 + c, n)
    left = (lax.rem(z + nz - 1, nz) * 2 + c, n)
    ins = (q, k, v, o)
    outs = (gq, gk, gv, go)
    wide_barrier(w, n, nw)

    def blk(off):
        return lax.rem(z + off + nz, nz) * 2 + c

    local = []
    for i in range(4):
        cp = pltpu.make_async_copy(ins[i], outs[i].at[w], ls.at[i])
        cp.start()
        local.append(cp)
        rcopy(ins[i], outs[i].at[w], rs.at[i, 0], rr.at[i, 0], right).start()
        rcopy(ins[i], outs[i].at[w], bs.at[i, 0], br.at[i, 0], left).start()
        rcopy(ins[i], outs[i].at[w], fs.at[i, 0], fr.at[i, 0], sib).start()
    cp = pltpu.make_async_copy(ps.at[w], pr.at[w], ls.at[4])
    cp.start()
    local.append(cp)

    def psend(d, _):
        t = lax.rem(w + d, nw)
        rcopy(ps.at[t], pr.at[w], pss.at[d], psr.at[w], (t, n)).start()
        return 0

    lax.fori_loop(1, nw, psend, 0)

    def pass_right(i, s, on):
        ref = outs[i].at[blk(-s)]
        rcopy(ref, ref, rs.at[i, s - 1], rr.at[i, s - 1], right).wait_recv()
        if on:
            rcopy(ref, ref, rs.at[i, s], rr.at[i, s], right).start()
        rcopy(ref, ref, fs.at[i, s], fr.at[i, s], sib).start()

    def pass_left(i, s, on):
        ref = outs[i].at[blk(s)]
        rcopy(ref, ref, bs.at[i, s - 1], br.at[i, s - 1], left).wait_recv()
        if on:
            rcopy(ref, ref, bs.at[i, s], br.at[i, s], left).start()
        rcopy(ref, ref, fs.at[i, hops_r + s], fr.at[i, hops_r + s], sib).start()

    def step(s, _):
        for i in range(4):
            pass_right(i, s, True)
            pass_left(i, s, True)
        return 0

    lax.fori_loop(1, hops_l, step, 0)
    for i in range(4):
        pass_right(i, hops_l, True)
        pass_left(i, hops_l, False)
    for i in range(4):
        pass_right(i, hops_r, False)
    for cp in local:
        cp.wait()

    def done_sib(s, _):
        for i in range(4):
            ref = outs[i].at[0]
            d = rcopy(ref, ref, fs.at[i, s], fr.at[i, s], sib)
            d.wait_recv()
            d.wait_send()
        return 0

    lax.fori_loop(0, nz, done_sib, 0)

    def done_r(s, _):
        for i in range(4):
            ref = outs[i].at[0]
            rcopy(ref, ref, rs.at[i, s], rr.at[i, s], right).wait_send()
        return 0

    lax.fori_loop(0, hops_r, done_r, 0)

    def done_l(s, _):
        for i in range(4):
            ref = outs[i].at[0]
            rcopy(ref, ref, bs.at[i, s], br.at[i, s], left).wait_send()
        return 0

    lax.fori_loop(0, hops_l, done_l, 0)

    def pdone(d, _):
        t = lax.rem(w + d, nw)
        cp = rcopy(ps.at[t], pr.at[t], pss.at[d], psr.at[t], (t, n))
        cp.wait_recv()
        cp.wait_send()
        return 0

    lax.fori_loop(1, nw, pdone, 0)


def gather_call(nw, q, k, v, o, ps):
    nz = nw // 2
    vm = pl.BlockSpec(memory_space=pltpu.VMEM)
    hop = nz // 2
    dma = pltpu.SemaphoreType.DMA
    full = jax.ShapeDtypeStruct((nw,) + q.shape, BF16)
    return pl.pallas_call(
        lambda *refs: gather_kernel(nw, *refs),
        out_shape=(full,) * 4 + (jax.ShapeDtypeStruct(ps.shape, BF16),),
        in_specs=[vm] * 5,
        out_specs=(vm,) * 5,
        scratch_shapes=[
            dma((4, hop)), dma((4, hop)), dma((4, hop)), dma((4, hop)),
            dma((4, nz)), dma((4, nz)), dma((nw,)), dma((nw,)), dma((5,)),
        ],
        compiler_params=pltpu.CompilerParams(collective_id=0, has_side_effects=True),
        name="weights_gather",
    )(q, k, v, o, ps)


def proj_kernel(nn, part, hid, out, rbuf, mine, s1, r1, s2, r2, ls):
    w = lax.axis_index("wide")
    n = lax.axis_index("narrow")
    narrow_barrier(w, n, nn)

    def send1(d, _):
        t = lax.rem(n + d, nn)
        rcopy(part.at[t], rbuf.at[n], s1.at[d], r1.at[n], (w, t)).start()
        return 0

    lax.fori_loop(1, nn, send1, 0)

    def add(d, acc):
        t = lax.rem(n + d, nn)
        cp = rcopy(part.at[t], rbuf.at[t], s1.at[d], r1.at[t], (w, t))
        cp.wait_recv()
        cp.wait_send()
        return acc + rbuf[t].astype(F32)

    total = lax.fori_loop(1, nn, add, part[n].astype(F32))
    mine[...] = (hid[...].astype(F32) + total).astype(BF16)

    def send2(d, _):
        t = lax.rem(n + d, nn)
        rcopy(mine, out.at[n], s2.at[d], r2.at[n], (w, t)).start()
        return 0

    lax.fori_loop(1, nn, send2, 0)
    cp = pltpu.make_async_copy(mine, out.at[n], ls)
    cp.start()
    cp.wait()

    def done(d, _):
        t = lax.rem(n + d, nn)
        cp = rcopy(mine, out.at[t], s2.at[d], r2.at[t], (w, t))
        cp.wait_recv()
        cp.wait_send()
        return 0

    lax.fori_loop(1, nn, done, 0)


def proj_call(nn, part, hid):
    vm = pl.BlockSpec(memory_space=pltpu.VMEM)
    dma = pltpu.SemaphoreType.DMA
    return pl.pallas_call(
        lambda *refs: proj_kernel(nn, *refs),
        out_shape=jax.ShapeDtypeStruct(part.shape, BF16),
        in_specs=[vm] * 2,
        out_specs=vm,
        scratch_shapes=[
            pltpu.VMEM(part.shape, BF16), pltpu.VMEM(hid.shape, BF16),
            dma((nn,)), dma((nn,)), dma((nn,)), dma((nn,)), dma,
        ],
        compiler_params=pltpu.CompilerParams(collective_id=1, has_side_effects=True),
        name="proj_sum",
    )(part, hid)


def swap_kernel(nw, src, dst, ss, rr, ls):
    w = lax.axis_index("wide")
    n = lax.axis_index("narrow")
    wide_barrier(w, n, nw)

    def send(d, _):
        t = lax.rem(w + d, nw)
        rcopy(src.at[t], dst.at[w], ss.at[d], rr.at[w], (t, n)).start()
        return 0

    lax.fori_loop(1, nw, send, 0)
    cp = pltpu.make_async_copy(src.at[w], dst.at[w], ls)
    cp.start()
    cp.wait()

    def done(d, _):
        t = lax.rem(w + d, nw)
        cp = rcopy(src.at[t], dst.at[t], ss.at[d], rr.at[t], (t, n))
        cp.wait_recv()
        cp.wait_send()
        return 0

    lax.fori_loop(1, nw, done, 0)


def swap_call(nw, src, cid, name):
    vm = pl.BlockSpec(memory_space=pltpu.VMEM)
    dma = pltpu.SemaphoreType.DMA
    return pl.pallas_call(
        lambda *refs: swap_kernel(nw, *refs),
        out_shape=jax.ShapeDtypeStruct(src.shape, BF16),
        in_specs=[vm],
        out_specs=vm,
        scratch_shapes=[dma((nw,)), dma((nw,)), dma],
        compiler_params=pltpu.CompilerParams(collective_id=cid, has_side_effects=True),
        name=name,
    )(src)


CHUNKS = 4
LOW = 80


def plane_ids():
    w = lax.axis_index("wide")
    n = lax.axis_index("narrow")
    y = n // NX
    x = lax.rem(n, NX)
    return w, n, y, x


def spread_kernel(rows, src, out, ss, rr, ls):
    w, n, y, x = plane_ids()
    size = rows // CHUNKS
    barrier = pltpu.get_barrier_semaphore()

    def dev(axis, off):
        if axis == 0:
            return (w, y * NX + lax.rem(x + off + NX, NX))
        return (w, lax.rem(y + off + NY, NY) * NX + x)

    for axis in (0, 1):
        for off in (1, -1):
            pl.semaphore_signal(barrier, inc=1, device_id=dev(axis, off), device_id_type=MESH)
    pl.semaphore_wait(barrier, 4)

    def ref_at(axis, b, o, lo, ln):
        if axis == 0:
            return out.at[o, b, pl.ds(lo, ln), :]
        return out.at[b, o, pl.ds(lo, ln), :]

    def pos(axis, off):
        if axis == 0:
            return lax.rem(x + off + NX, NX)
        return lax.rem(y + off + NY, NY)

    own = []
    for j in range(CHUNKS):
        lo = j * size
        axis = j % 2
        cp = pltpu.make_async_copy(
            src.at[pl.ds(lo, size), :], out.at[y, x, pl.ds(lo, size), :], ls.at[j]
        )
        cp.start()
        own.append(cp)
        dst = out.at[y, x, pl.ds(lo, size), :]
        a = src.at[pl.ds(lo, size), :]
        rcopy(a, dst, ss.at[j, 0], rr.at[j, 0], dev(axis, 1)).start()
        rcopy(a, dst, ss.at[j, 1], rr.at[j, 1], dev(axis, -1)).start()
        rcopy(a, dst, ss.at[j, 4], rr.at[j, 4], dev(1 - axis, 1)).start()
        rcopy(a, dst, ss.at[j, 5], rr.at[j, 5], dev(1 - axis, -1)).start()

    def desc(j, slot, b, o, lo, ln, to):
        r = ref_at(j % 2, b, o, lo, ln)
        return rcopy(r, r, ss.at[j, slot], rr.at[j, slot], to)

    pending = []

    def go(d):
        d.start()
        pending.append(d)

    for j in range(CHUNKS):
        lo = j * size
        axis = j % 2
        me_o = pos(1 - axis, 0)
        bm, bp, b2 = pos(axis, -1), pos(axis, 1), pos(axis, 2)
        desc(j, 0, bm, me_o, lo, size, dev(axis, 1)).wait_recv()
        desc(j, 2, bm, me_o, lo, LOW, dev(axis, 1)).start()
        desc(j, 8, bm, me_o, lo, size, dev(1 - axis, 1)).start()
        desc(j, 9, bm, me_o, lo, size, dev(1 - axis, -1)).start()
        desc(j, 1, bp, me_o, lo, size, dev(axis, -1)).wait_recv()
        desc(j, 3, bp, me_o, lo + LOW, size - LOW, dev(axis, -1)).start()
        desc(j, 12, bp, me_o, lo, size, dev(1 - axis, 1)).start()
        desc(j, 13, bp, me_o, lo, size, dev(1 - axis, -1)).start()
    for j in range(CHUNKS):
        lo = j * size
        axis = j % 2
        me_o = pos(1 - axis, 0)
        b0, bm, bp, b2 = pos(axis, 0), pos(axis, -1), pos(axis, 1), pos(axis, 2)
        om, op, o2 = pos(1 - axis, -1), pos(1 - axis, 1), pos(1 - axis, 2)
        desc(j, 4, b0, om, lo, size, dev(1 - axis, 1)).wait_recv()
        desc(j, 6, b0, om, lo, LOW, dev(1 - axis, 1)).start()
        desc(j, 5, b0, op, lo, size, dev(1 - axis, -1)).wait_recv()
        desc(j, 7, b0, op, lo + LOW, size - LOW, dev(1 - axis, -1)).start()
        desc(j, 2, b2, me_o, lo, LOW, dev(axis, 1)).wait_recv()
        desc(j, 3, b2, me_o, lo + LOW, size - LOW, dev(axis, -1)).wait_recv()
        desc(j, 16, b2, me_o, lo, size, dev(1 - axis, 1)).start()
        desc(j, 17, b2, me_o, lo, size, dev(1 - axis, -1)).start()
        for base, b in ((8, bm), (12, bp)):
            desc(j, base, b, om, lo, size, dev(1 - axis, 1)).wait_recv()
            desc(j, base + 2, b, om, lo, LOW, dev(1 - axis, 1)).start()
            desc(j, base + 1, b, op, lo, size, dev(1 - axis, -1)).wait_recv()
            desc(j, base + 3, b, op, lo + LOW, size - LOW, dev(1 - axis, -1)).start()
    for j in range(CHUNKS):
        lo = j * size
        axis = j % 2
        b2 = pos(axis, 2)
        om, op, o2 = pos(1 - axis, -1), pos(1 - axis, 1), pos(1 - axis, 2)
        desc(j, 16, b2, om, lo, size, dev(1 - axis, 1)).wait_recv()
        desc(j, 18, b2, om, lo, LOW, dev(1 - axis, 1)).start()
        desc(j, 17, b2, op, lo, size, dev(1 - axis, -1)).wait_recv()
        desc(j, 19, b2, op, lo + LOW, size - LOW, dev(1 - axis, -1)).start()
    for j in range(CHUNKS):
        lo = j * size
        axis = j % 2
        o2 = pos(1 - axis, 2)
        for base, off in ((4, 0), (8, -1), (12, 1), (16, 2)):
            b = pos(axis, off)
            desc(j, base + 2, b, o2, lo, LOW, dev(1 - axis, 1)).wait_recv()
            desc(j, base + 3, b, o2, lo + LOW, size - LOW, dev(1 - axis, -1)).wait_recv()
    for cp in own:
        cp.wait()
    for j in range(CHUNKS):
        for slot in range(20):
            if slot < 2 or slot % 4 < 2:
                lo, ln = 0, size
            elif slot % 4 == 2:
                lo, ln = 0, LOW
            else:
                lo, ln = LOW, size - LOW
            desc(j, slot, 0, 0, lo, ln, dev(0, 1)).wait_send()


def spread_call(src):
    rows = src.shape[0]
    vm = pl.BlockSpec(memory_space=pltpu.VMEM)
    dma = pltpu.SemaphoreType.DMA
    return pl.pallas_call(
        lambda *refs: spread_kernel(rows, *refs),
        out_shape=jax.ShapeDtypeStruct((NY, NX) + src.shape, BF16),
        in_specs=[vm],
        out_specs=vm,
        scratch_shapes=[dma((CHUNKS, 20)), dma((CHUNKS, 20)), dma((CHUNKS,))],
        compiler_params=pltpu.CompilerParams(collective_id=3, has_side_effects=True),
        name="plane_spread",
    )(src)


def fold_kernel(rows, src, out, r1, f1, t1, m2, r2, f2, t2, ss, rr, ls):
    w, n, y, x = plane_ids()
    size = rows // CHUNKS
    barrier = pltpu.get_barrier_semaphore()

    def dev(axis, off):
        if axis == 0:
            return (w, y * NX + lax.rem(x + off + NX, NX))
        return (w, lax.rem(y + off + NY, NY) * NX + x)

    for axis in (0, 1):
        for off in (1, -1):
            pl.semaphore_signal(barrier, inc=1, device_id=dev(axis, off), device_id_type=MESH)
    pl.semaphore_wait(barrier, 4)

    def pos(axis, off):
        if axis == 0:
            return lax.rem(x + off + NX, NX)
        return lax.rem(y + off + NY, NY)

    def src_at(axis, b, lo, ln):
        if axis == 0:
            return src.at[:, b, pl.ds(lo, ln), :]
        return src.at[b, :, pl.ds(lo, ln), :]

    def val(axis, b, lo, ln):
        if axis == 0:
            return src[:, b, pl.ds(lo, ln), :].astype(F32)
        return src[b, :, pl.ds(lo, ln), :].astype(F32)

    for j in range(CHUNKS):
        axis, lo = j % 2, j * size
        b2 = pos(axis, 2)
        rcopy(src_at(axis, b2, lo, LOW), f1.at[j, :, pl.ds(0, LOW), :],
              ss.at[j, 0], rr.at[j, 0], dev(axis, 1)).start()
        rcopy(src_at(axis, b2, lo + LOW, size - LOW), f1.at[j, :, pl.ds(LOW, size - LOW), :],
              ss.at[j, 1], rr.at[j, 1], dev(axis, -1)).start()

    def d1(j, slot, lo, ln, to):
        r = f1.at[j, :, pl.ds(lo, ln), :]
        return rcopy(r, r, ss.at[j, slot], rr.at[j, slot], to)

    for j in range(CHUNKS):
        axis, lo = j % 2, j * size
        bp, bm = pos(axis, 1), pos(axis, -1)
        d1(j, 0, 0, LOW, dev(axis, 1)).wait_recv()
        t1[j, 0, :, pl.ds(0, LOW), :] = (
            val(axis, bp, lo, LOW) + f1[j, :, pl.ds(0, LOW), :].astype(F32)
        ).astype(BF16)
        t1[j, 0, :, pl.ds(LOW, size - LOW), :] = val(axis, bp, lo + LOW, size - LOW).astype(BF16)
        rcopy(t1.at[j, 0], r1.at[j, 0], ss.at[j, 2], rr.at[j, 2], dev(axis, 1)).start()
        d1(j, 1, LOW, size - LOW, dev(axis, -1)).wait_recv()
        t1[j, 1, :, pl.ds(LOW, size - LOW), :] = (
            val(axis, bm, lo + LOW, size - LOW) + f1[j, :, pl.ds(LOW, size - LOW), :].astype(F32)
        ).astype(BF16)
        t1[j, 1, :, pl.ds(0, LOW), :] = val(axis, bm, lo, LOW).astype(BF16)
        rcopy(t1.at[j, 1], r1.at[j, 1], ss.at[j, 3], rr.at[j, 3], dev(axis, -1)).start()

    for j in range(CHUNKS):
        axis, lo = j % 2, j * size
        for k in range(2):
            rcopy(t1.at[j, k], r1.at[j, k], ss.at[j, 2 + k], rr.at[j, 2 + k], dev(axis, 1)).wait_recv()
        m2[j] = (
            val(axis, pos(axis, 0), lo, size) + r1[j, 0].astype(F32) + r1[j, 1].astype(F32)
        ).astype(BF16)
        b2 = pos(1 - axis, 2)
        rcopy(m2.at[j, b2, pl.ds(0, LOW), :], f2.at[j, pl.ds(0, LOW), :],
              ss.at[j, 4], rr.at[j, 4], dev(1 - axis, 1)).start()
        rcopy(m2.at[j, b2, pl.ds(LOW, size - LOW), :], f2.at[j, pl.ds(LOW, size - LOW), :],
              ss.at[j, 5], rr.at[j, 5], dev(1 - axis, -1)).start()

    def d2(j, slot, lo, ln, to):
        r = f2.at[j, pl.ds(lo, ln), :]
        return rcopy(r, r, ss.at[j, slot], rr.at[j, slot], to)

    for j in range(CHUNKS):
        axis = j % 2
        bp, bm = pos(1 - axis, 1), pos(1 - axis, -1)
        d2(j, 4, 0, LOW, dev(1 - axis, 1)).wait_recv()
        t2[j, 0, pl.ds(0, LOW), :] = (
            m2[j, bp, pl.ds(0, LOW), :].astype(F32) + f2[j, pl.ds(0, LOW), :].astype(F32)
        ).astype(BF16)
        t2[j, 0, pl.ds(LOW, size - LOW), :] = m2[j, bp, pl.ds(LOW, size - LOW), :]
        rcopy(t2.at[j, 0], r2.at[j, 0], ss.at[j, 6], rr.at[j, 6], dev(1 - axis, 1)).start()
        d2(j, 5, LOW, size - LOW, dev(1 - axis, -1)).wait_recv()
        t2[j, 1, pl.ds(LOW, size - LOW), :] = (
            m2[j, bm, pl.ds(LOW, size - LOW), :].astype(F32) + f2[j, pl.ds(LOW, size - LOW), :].astype(F32)
        ).astype(BF16)
        t2[j, 1, pl.ds(0, LOW), :] = m2[j, bm, pl.ds(0, LOW), :]
        rcopy(t2.at[j, 1], r2.at[j, 1], ss.at[j, 7], rr.at[j, 7], dev(1 - axis, -1)).start()
    for j in range(CHUNKS):
        axis = j % 2
        for k in range(2):
            rcopy(t2.at[j, k], r2.at[j, k], ss.at[j, 6 + k], rr.at[j, 6 + k], dev(0, 1)).wait_recv()
        out[pl.ds(j * size, size), :] = (
            m2[j, pos(1 - axis, 0)].astype(F32) + r2[j, 0].astype(F32) + r2[j, 1].astype(F32)
        ).astype(BF16)
    for j in range(CHUNKS):
        d1(j, 0, 0, LOW, dev(0, 1)).wait_send()
        d1(j, 1, LOW, size - LOW, dev(0, 1)).wait_send()
        d2(j, 4, 0, LOW, dev(0, 1)).wait_send()
        d2(j, 5, LOW, size - LOW, dev(0, 1)).wait_send()
        for k in range(2):
            rcopy(t1.at[j, k], r1.at[j, k], ss.at[j, 2 + k], rr.at[j, 2 + k], dev(0, 1)).wait_send()
            rcopy(t2.at[j, k], r2.at[j, k], ss.at[j, 6 + k], rr.at[j, 6 + k], dev(0, 1)).wait_send()


def fold_call(src):
    rows = src.shape[2]
    size = rows // CHUNKS
    vm = pl.BlockSpec(memory_space=pltpu.VMEM)
    dma = pltpu.SemaphoreType.DMA
    return pl.pallas_call(
        lambda *refs: fold_kernel(rows, *refs),
        out_shape=jax.ShapeDtypeStruct((rows, 128), BF16),
        in_specs=[vm],
        out_specs=vm,
        scratch_shapes=[
            pltpu.VMEM((CHUNKS, 2, 4, size, 128), BF16),
            pltpu.VMEM((CHUNKS, 4, size, 128), BF16),
            pltpu.VMEM((CHUNKS, 2, 4, size, 128), BF16),
            pltpu.VMEM((CHUNKS, 4, size, 128), BF16),
            pltpu.VMEM((CHUNKS, 2, size, 128), BF16),
            pltpu.VMEM((CHUNKS, size, 128), BF16),
            pltpu.VMEM((CHUNKS, 2, size, 128), BF16),
            dma((CHUNKS, 8)), dma((CHUNKS, 8)), dma,
        ],
        compiler_params=pltpu.CompilerParams(collective_id=4, has_side_effects=True),
        name="plane_fold",
    )(src)


def body(
    hidden,
    attn_gain,
    expert_gain,
    query_weight,
    key_weight,
    value_weight,
    output_weight,
    router_weight,
    gate_weight,
    up_weight,
    down_weight,
    prefix_keys,
    prefix_values,
    cache_keys,
    cache_values,
    parents,
    cache_lengths,
    group_ids,
    expert_ids,
    accepted,
):
    tok, width = hidden.shape
    cache_size = cache_keys.shape[1]
    nn = lax.axis_size("narrow")
    nw = lax.axis_size("wide")
    n = lax.axis_index("narrow")
    slice_width = width // nn
    top = expert_ids.shape[1]
    exp_local = gate_weight.shape[0]
    per_dev = exp_local * CAP
    slots_all = nw * per_dev
    scale_factor = 1.0 / math.sqrt(HD)
    pre = jnp.concatenate([prefix_keys, prefix_values], axis=0)
    psend = jnp.transpose(jnp.take(pre, group_ids, axis=1), (1, 0, 2))
    gq, gk, gv, go, pr = gather_call(nw, query_weight, key_weight, value_weight, output_weight, psend)
    pp = prefix_keys.shape[0]
    group_keys = pr[:, :pp].reshape(nw * pp, HD)
    group_values = pr[:, pp:].reshape(nw * pp, HD)
    normed = rms_scale(hidden, attn_gain)

    def project(g):
        return jnp.dot(normed, g.reshape(width, HD), preferred_element_type=F32).astype(BF16)

    queries, keys_new, values_new = project(gq), project(gk), project(gv)
    length = cache_lengths[0]
    slot_ids = jnp.arange(cache_size, dtype=jnp.int32)
    cache_mask = (slot_ids < length) & ((slot_ids < SINK) | (slot_ids >= length - WIN))
    ancestry, depths = tree_links(parents)
    own_keys, own_values = cache_keys[0], cache_values[0]

    def score(k):
        return (
            lax.dot_general(queries, k, (((1,), (1,)), ((), ())), preferred_element_type=F32)
            * scale_factor
        )

    ps, cs, ts = score(group_keys), score(own_keys), score(keys_new)
    cs = jnp.where(cache_mask[None, :], cs, -jnp.inf)
    ts = jnp.where(ancestry, ts, -jnp.inf)
    row_top = jnp.maximum(
        jnp.max(ps, axis=-1), jnp.maximum(jnp.max(cs, axis=-1), jnp.max(ts, axis=-1))
    )[:, None]
    pw, cw, tw = jnp.exp(ps - row_top), jnp.exp(cs - row_top), jnp.exp(ts - row_top)
    row_total = jnp.sum(pw, axis=-1) + jnp.sum(cw, axis=-1) + jnp.sum(tw, axis=-1)

    def weigh(wt, v):
        return jnp.dot(wt.astype(BF16), v, preferred_element_type=F32)

    weighted = weigh(pw, group_values) + weigh(cw, own_values) + weigh(tw, values_new)
    attended = (weighted / row_total[:, None]).astype(BF16)
    part = lax.dot_general(
        go.reshape(nn, slice_width, HD), attended, (((2,), (1,)), ((), ())), preferred_element_type=F32
    )
    part = jnp.transpose(part, (0, 2, 1)).astype(BF16)
    hid_slice = lax.dynamic_slice_in_dim(hidden, n * slice_width, slice_width, 1)
    mixed_all = proj_call(nn, part, hid_slice)
    mixed = jnp.transpose(mixed_all, (1, 0, 2)).reshape(tok, width)
    mixed_part = lax.dynamic_index_in_dim(mixed_all, n, 0, keepdims=False)
    normed_moe = rms_scale(mixed, expert_gain)
    logits = jnp.dot(normed_moe, router_weight, preferred_element_type=F32)
    expert_range = jnp.arange(E, dtype=jnp.int32)
    matches = expert_ids[:, :, None] == expert_range
    chosen = jnp.sum(jnp.where(matches, logits[:, None, :], 0.0), axis=-1)
    shares = jax.nn.softmax(chosen, axis=-1)
    named = jnp.any(matches, axis=1)
    tok_ids = jnp.arange(tok, dtype=jnp.int32)
    before = (tok_ids[:, None] > tok_ids[None, :]).astype(BF16)
    earlier = jnp.dot(before, named.astype(BF16), preferred_element_type=F32)
    ranks = jnp.sum(jnp.where(matches, earlier[:, None, :], 0.0), axis=-1).astype(jnp.int32)
    targets = expert_ids * CAP + ranks
    slot_range = jnp.arange(slots_all, dtype=jnp.int32)
    hit = targets[:, :, None] == slot_range
    place = jnp.any(hit, axis=1).astype(BF16)
    normed_slice = lax.dynamic_slice_in_dim(normed_moe, n * slice_width, slice_width, 1)
    send = lax.dot_general(
        place, normed_slice, (((0,), (0,)), ((), ())), preferred_element_type=F32
    ).astype(BF16)
    routed = swap_call(nw, send.reshape(nw, per_dev // 2, 2, slice_width), 2, "dispatch")
    rows = spread_call(routed.reshape(slots_all, slice_width))
    rows = rows.reshape(nn, slots_all, slice_width)
    fw = gate_weight.shape[2]
    both = jnp.concatenate([gate_weight[0], gate_weight[1], up_weight[0], up_weight[1]], axis=1)
    hidden_units = jnp.einsum(
        "nrd,ndf->rf", rows, both.reshape(nn, slice_width, 4 * fw), preferred_element_type=F32
    )
    act = jax.nn.silu(hidden_units[:, : 2 * fw]) * hidden_units[:, 2 * fw :]
    second = (slot_range % per_dev) >= CAP
    cols = jnp.arange(2 * fw, dtype=jnp.int32) >= fw
    act = jnp.where(second[:, None] == cols[None, :], act, 0.0).astype(BF16)
    down = down_weight.reshape(2 * fw, nn, slice_width)
    pieces = jnp.einsum("rf,fnd->nrd", act, down, preferred_element_type=F32).astype(BF16)
    folded = fold_call(pieces.reshape(NY, NX, slots_all, slice_width))
    back = swap_call(nw, folded.reshape(nw, per_dev // 2, 2, slice_width), 5, "return")
    back = back.reshape(slots_all, slice_width)
    mix = jnp.sum(jnp.where(hit, shares[:, :, None], 0.0), axis=1)
    moe_part = jnp.dot(mix, back.astype(F32), precision=lax.Precision.HIGHEST)
    layer_out = (mixed_part.astype(F32) + moe_part).astype(BF16)
    on_path = lax.dynamic_index_in_dim(ancestry, accepted[0], 0, keepdims=False)
    slots = jnp.where(on_path, length + depths, cache_size)
    put = slot_ids[:, None] == slots[None, :]
    written = jnp.any(put, axis=1)[:, None]
    put = put.astype(BF16)

    def compact(cache, fresh):
        moved = jnp.dot(put, fresh, preferred_element_type=F32).astype(BF16)
        return jnp.where(written, moved, cache)[None]

    new_keys = compact(own_keys, keys_new)
    new_values = compact(own_values, values_new)
    return (layer_out, new_keys, new_values)


def solution(mesh):
    in_specs = (
        P("wide", None),
        P(),
        P(),
        P("wide", "narrow"),
        P("wide", "narrow"),
        P("wide", "narrow"),
        P("wide", "narrow"),
        P(),
        P("wide", None, "narrow"),
        P("wide", None, "narrow"),
        P("wide", "narrow", None),
        P("wide", None, "narrow"),
        P("wide", None, "narrow"),
        P("wide", None, "narrow"),
        P("wide", None, "narrow"),
        P("wide", None),
        P("wide"),
        P(),
        P("wide", None),
        P("wide"),
    )
    out_specs = (P("wide", "narrow"), P("wide", None, "narrow"), P("wide", None, "narrow"))
    return jax.shard_map(body, mesh=mesh, in_specs=in_specs, out_specs=out_specs, check_vma=False)
```

```python
import math

import jax
import jax.numpy as jnp
from jax import lax
from jax.experimental import pallas as pl
from jax.experimental.pallas import tpu as pltpu
from jax.sharding import PartitionSpec as P

HD = 128
E = 64
SINK = 4
WIN = 512
CAP = 9
NX = 4
NY = 4
MESH = pl.DeviceIdType.MESH
F32 = jnp.float32
BF16 = jnp.bfloat16

norm_eps = 1e-06


def rms_scale(rows, row_gain):
    widened = rows.astype(F32)
    power_mean = jnp.mean(widened * widened, axis=-1, keepdims=True)
    return (widened * lax.rsqrt(power_mean + norm_eps) * row_gain).astype(BF16)


DIMS0 = (((0,), (0,)), ((), ()))
DIMS1 = (((1,), (1,)), ((), ()))
CHUNKS = 4
ORDER = (2, 1, 3, 0)
LOW = 80
NEG = -1e30


def rcopy(src, dst, ssem, rsem, dev):
    return pltpu.make_async_remote_copy(
        src_ref=src, dst_ref=dst, send_sem=ssem, recv_sem=rsem, device_id=dev, device_id_type=MESH
    )


def iota(shape, dim):
    return lax.broadcasted_iota(jnp.int32, shape, dim)


def mm(a, b, dims=(((1,), (0,)), ((), ()))):
    return lax.dot_general(a, b, dims, preferred_element_type=F32)


def layer_kernel(
    lens, acc_node, hidden, attn_gain, expert_gain, q_in, k_in, v_in, o_in, router, gate, up, down,
    pk, pv, cache_k, cache_v, parents, groups, ids,
    layer_out, new_k, new_v,
    normed, g, go, ps, pr, qs, ks, vs, cs, ts, anc, put, part, rbuf, mx, ssb, wgt, tgt, place, mix,
    dbuf, r, xs, src, r1, f1, t1, m2, r2, f2, t2, bbuf, bk,
    ls, rs, rr, fs, fr, os, orr, ofs, ofr, pss, psr, s1, r1s, s2, r2s, s3, r3s, ds, dr, ss, rrs, us, ur, es, er,
):
    nz, nn, nw = g.shape[0], part.shape[0], pr.shape[0]
    tok = hidden.shape[0]
    w = lax.axis_index("wide")
    n = lax.axis_index("narrow")
    z = w // 2
    c = lax.rem(w, 2)
    y = n // NX
    x = lax.rem(n, NX)
    sg = 1 - 2 * c
    sib_w = w + sg
    sib = (sib_w, n)

    def chip(off):
        return lax.rem(z + off + nz, nz)

    nxt = (chip(sg) * 2 + c, n)

    barrier = pltpu.get_barrier_semaphore()
    for t in (sib, (chip(1) * 2 + c, n), (chip(nz - 1) * 2 + c, n)):
        pl.semaphore_signal(barrier, inc=1, device_id=t, device_id_type=MESH)

    def greet(d, _):
        pl.semaphore_signal(barrier, inc=1, device_id=(w, lax.rem(n + d, nn)), device_id_type=MESH)
        return 0

    lax.fori_loop(1, nn, greet, 0)
    local = [
        pltpu.make_async_copy(a, b, ls.at[i])
        for i, (a, b) in enumerate(
            ((q_in, g.at[z, c, 0]), (k_in, g.at[z, c, 1]), (v_in, g.at[z, c, 2]), (o_in, go.at[z, c]))
        )
    ]
    for cp in local:
        cp.start()
    for cp in local:
        cp.wait()
    pl.semaphore_wait(barrier, nn + 2)

    def ring(s, sub):
        ref = g.at[chip(-sg * s), sub]
        return rcopy(ref, ref, rs.at[s, sub], rr.at[s, sub], nxt)

    def got(s, sub):
        ref = g.at[chip(-sg * (s + 1)), sub]
        return rcopy(ref, ref, rs.at[s, sub], rr.at[s, sub], nxt)

    def side(chip_id, sub):
        ref = g.at[chip_id, sub]
        return rcopy(ref, ref, fs.at[chip_id, sub], fr.at[chip_id, sub], sib)

    side(z, c).start()
    oref = go.at[z, c]
    o_side = rcopy(oref, oref, ofs.at[nz], ofr.at[nz], sib)
    o_side.start()
    ring(0, c).start()
    osib = go.at[z, 1 - c]
    side(z, 1 - c).wait_recv()
    ring(0, 1 - c).start()

    hv = hidden[...].astype(F32)
    power = jnp.mean(hv * hv, axis=-1, keepdims=True)
    normed[...] = (hv * lax.rsqrt(power + norm_eps) * attn_gain[...]).astype(BF16)

    def fill_prefix():
        rows, cols = nw * 16, 64
        it = iota((rows, nw), 0) // 16
        gid = jnp.sum(jnp.where(it == iota((rows, nw), 1), groups[...], 0), axis=1, keepdims=True)
        r_id = lax.rem(iota((rows, cols), 0), 16)
        c_id = iota((rows, cols), 1)
        same = lax.rem(c_id, 8) == gid
        one_k = (same & (c_id // 8 == r_id)).astype(F32).astype(BF16)
        one_v = (same & (c_id // 8 + 8 == r_id)).astype(F32).astype(BF16)
        picked = mm(one_k, pk[...].reshape(cols, HD)) + mm(one_v, pv[...].reshape(cols, HD))
        ps[...] = picked.astype(BF16).reshape(ps.shape)

    def fill_tree():
        size = parents.shape[1]
        a, b = iota((size, size), 0), iota((size, size), 1)
        eye = (a == b).astype(F32)
        up_t = jnp.maximum(eye, (parents[...] == a).astype(F32))
        for _ in range(6):
            m = up_t.astype(BF16)
            up_t = (mm(m, m) > 0.5).astype(F32)
        depth = jnp.sum(up_t, axis=0, keepdims=True) - 1.0
        full = mm(up_t.astype(BF16), eye.astype(BF16), DIMS0)
        anc[...] = full
        on_path = jnp.sum(jnp.where(a == acc_node[0], full, 0.0), axis=0, keepdims=True)
        slot = jnp.where(on_path > 0.5, lens[0] + depth.astype(jnp.int32), put.shape[0])
        put[...] = (iota(put.shape, 0) == slot).astype(F32).astype(BF16)

    def fill_slots():
        a, b = iota((tok, E), 0), iota((tok, E), 1)
        idv = ids[...]
        named = jnp.zeros((tok, E), F32)
        for k in range(idv.shape[1]):
            named = named + (idv[:, k : k + 1] == b).astype(F32)
        earlier = mm((b < a).astype(F32).astype(BF16), named.astype(BF16))
        hit = jnp.zeros(place.shape, F32)
        cols = iota(place.shape, 1)
        for k in range(idv.shape[1]):
            idk = idv[:, k : k + 1]
            rank = jnp.sum(jnp.where(idk == b, earlier, 0.0), axis=1, keepdims=True)
            t = idk * CAP + rank.astype(jnp.int32)
            tgt[k] = jnp.broadcast_to(t, tgt.shape[1:])
            hit = hit + (cols == t).astype(F32)
        place[...] = hit.astype(BF16)

    fw = gate.shape[2]

    def fill_weights(part_id):
        for i, ref in ((0, gate), (2, up)):
            for e in range(2):
                lo = part_id * 512
                wgt[lo : lo + 512, (i + e) * fw : (i + e + 1) * fw] = ref[e, lo : lo + 512, :]

    fillers = {
        1: fill_prefix, 2: fill_tree, 3: fill_slots,
        4: lambda: fill_weights(0), 5: lambda: fill_weights(1), 6: lambda: fill_weights(2), 7: lambda: fill_weights(3),
    }
    for s in range(1, nz // 2):
        for i in range(2):
            sub = c if i == 0 else 1 - c
            got(s - 1, sub).wait_recv()
            if s < nz // 2 - 1 or i == 0:
                ring(s, sub).start()
            side(chip(-sg * s), sub).start()
        fillers[s]()
    got(nz // 2 - 1, c).wait_recv()
    side(chip(nz // 2), c).start()
    for s in range(1, nz // 2):
        for sub in range(2):
            side(chip(sg * s), sub).wait_recv()
    side(chip(nz // 2), 1 - c).wait_recv()

    def psend(d, _):
        t = lax.rem(w + d, nw)
        rcopy(ps.at[t], pr.at[w], pss.at[t], psr.at[w], (t, n)).start()
        return 0

    lax.fori_loop(1, nw, psend, 0)
    cp_own = pltpu.make_async_copy(ps.at[w], pr.at[w], psr.at[w])
    cp_own.start()

    rcopy(osib, osib, ofs.at[nz], ofr.at[nz], sib).wait_recv()

    def oring(s):
        k = chip(-sg * s)
        ref = go.at[k] if s < nz // 2 - 1 else go.at[k, c]
        return rcopy(ref, ref, os.at[s], orr.at[s], nxt)

    def ogot(s):
        k = chip(-sg * (s + 1))
        ref = go.at[k] if s < nz // 2 - 1 else go.at[k, c]
        return rcopy(ref, ref, os.at[s], orr.at[s], nxt)

    def oside(s, mine):
        k = chip(-sg * s) if mine else chip(sg * s)
        ref = go.at[k] if s < nz // 2 else go.at[k, c if mine else 1 - c]
        return rcopy(ref, ref, ofs.at[k], ofr.at[k], sib)

    oring(0).start()
    scale = 1.0 / math.sqrt(HD)

    def fill_qkv(i, ref):
        def run():
            ref[...] = mm(normed[...], g[:, :, i].reshape(-1, HD)).astype(BF16)
        return run

    def fill_cache():
        pos = iota(cs.shape, 1)
        ln = lens[0]
        ok = (pos < ln) & ((pos < SINK) | (pos >= ln - WIN))
        cs[...] = jnp.where(ok, mm(qs[...], cache_k[0], DIMS1) * scale, NEG)
        ts[...] = jnp.where(anc[...] > 0.5, mm(qs[...], ks[...], DIMS1) * scale, NEG)

    def fill_compact(fresh, cache, out):
        def run():
            moved = mm(put[...], fresh[...])
            written = jnp.sum(put[...].astype(F32), axis=1, keepdims=True) > 0.5
            out[0] = jnp.where(written, moved.astype(BF16), cache[0])
        return run

    fillers = {
        1: fill_qkv(0, qs), 2: fill_qkv(1, ks), 3: fill_qkv(2, vs), 4: fill_cache,
        5: fill_compact(ks, cache_k, new_k), 6: fill_compact(vs, cache_v, new_v), 7: lambda: None,
    }
    for s in range(1, nz // 2):
        ogot(s - 1).wait_recv()
        oring(s).start()
        oside(s, True).start()
        fillers[s]()
    ogot(nz // 2 - 1).wait_recv()
    oside(nz // 2, True).start()

    cp_own.wait()

    def pwait(d, _):
        t = lax.rem(w + d, nw)
        rcopy(pr.at[t], pr.at[t], pss.at[t], psr.at[t], sib).wait_recv()
        return 0

    lax.fori_loop(1, nw, pwait, 0)
    prows = pr[...].reshape(-1, HD)
    is_key = lax.rem(iota((tok, nw * 16), 1), 16) < 8
    psc = jnp.where(is_key, mm(qs[...], prows, DIMS1) * scale, NEG)
    csc, tsc = cs[...], ts[...]
    top = jnp.maximum(
        jnp.max(psc, axis=1, keepdims=True),
        jnp.maximum(jnp.max(csc, axis=1, keepdims=True), jnp.max(tsc, axis=1, keepdims=True)),
    )
    pw = jnp.where(is_key, jnp.exp(psc - top), 0.0)
    pos = iota(cs.shape, 1)
    ok = (pos < lens[0]) & ((pos < SINK) | (pos >= lens[0] - WIN))
    cw = jnp.where(ok, jnp.exp(csc - top), 0.0)
    tw = jnp.where(anc[...] > 0.5, jnp.exp(tsc - top), 0.0)
    total = (
        jnp.sum(pw, axis=1, keepdims=True) + jnp.sum(cw, axis=1, keepdims=True) + jnp.sum(tw, axis=1, keepdims=True)
    )
    weighted = (
        mm(pltpu.roll(pw, 8, 1).astype(BF16), prows)
        + mm(cw.astype(BF16), cache_v[0])
        + mm(tw.astype(BF16), vs[...])
    )
    attended = (weighted / total).astype(BF16)
    for s in range(1, nz // 2 + 1):
        oside(s, False).wait_recv()
    for i in range(4):
        four = go[i * 4 : i * 4 + 4].reshape(512, HD)
        terms = mm(attended, four, DIMS1)
        for j in range(4):
            part[i * 4 + j] = terms[:, j * HD : (j + 1) * HD].astype(BF16)

    def send1(d, _):
        t = lax.rem(n + d, nn)
        rcopy(part.at[t], rbuf.at[n], s1.at[t], r1s.at[n], (w, t)).start()
        return 0

    lax.fori_loop(1, nn, send1, 0)
    col = pl.multiple_of(n * HD, HD)

    def add1(d, acc):
        t = lax.rem(n + d, nn)
        rcopy(rbuf.at[t], rbuf.at[t], s1.at[t], r1s.at[t], (w, t)).wait_recv()
        return acc + rbuf[t].astype(F32)

    summed = lax.fori_loop(1, nn, add1, part[n].astype(F32))
    mixed = (hidden[:, pl.ds(col, HD)].astype(F32) + summed).astype(BF16)
    mx[n] = mixed
    mf = mixed.astype(F32)
    sq = jnp.sum(mf * mf, axis=1, keepdims=True)
    eye = iota((tok, HD), 0) == iota((tok, HD), 1)
    ssb[n] = jnp.broadcast_to(jnp.sum(jnp.where(eye, sq, 0.0), axis=0, keepdims=True), (8, HD))

    def send3(d, _):
        t = lax.rem(n + d, nn)
        rcopy(ssb.at[n], ssb.at[n], s3.at[t], r3s.at[n], (w, t)).start()
        return 0

    lax.fori_loop(1, nn, send3, 0)

    def send2(d, _):
        t = lax.rem(n + d, nn)
        rcopy(mx.at[n], mx.at[n], s2.at[t], r2s.at[n], (w, t)).start()
        return 0

    lax.fori_loop(1, nn, send2, 0)

    def wait3(d, _):
        t = lax.rem(n + d, nn)
        rcopy(ssb.at[t], ssb.at[t], s3.at[t], r3s.at[t], (w, t)).wait_recv()
        return 0

    lax.fori_loop(1, nn, wait3, 0)
    sums = jnp.sum(ssb[...], axis=0)[0:1]
    sq_all = jnp.sum(jnp.where(eye, sums, 0.0), axis=1, keepdims=True)
    inv = lax.rsqrt(sq_all / (nn * HD) + norm_eps)
    mine = (mf * inv * expert_gain[:, pl.ds(col, HD)]).astype(BF16)
    slots = mm(place[...], mine, DIMS0)
    dflat = dbuf.reshape(place.shape[1], HD)
    dflat[...] = slots.astype(BF16)

    def slot_of(dz):
        return lax.rem(nz + nz // 2 - dz, nz) * 2 + c

    def send_d(dz, core):
        t = chip(dz) * 2 + core
        rcopy(dbuf.at[t], r.at[slot_of(dz)], ds.at[t], dr.at[slot_of(dz)], (t, n)).start()

    cp_d = pltpu.make_async_copy(dbuf.at[w], r.at[nz + c], dr.at[nz + c])
    cp_d.start()
    send_d(0, 1 - c)
    for k in range(1, nz // 2):
        for dz in (k, -k):
            for core in range(2):
                send_d(dz, core)
    for core in range(2):
        send_d(nz // 2, core)

    def wait2(d, _):
        t = lax.rem(n + d, nn)
        rcopy(mx.at[t], mx.at[t], s2.at[t], r2s.at[t], (w, t)).wait_recv()
        return 0

    def fill_router():
        lax.fori_loop(1, nn, wait2, 0)
        logits = jnp.zeros((tok, E), F32)
        for t in range(nn):
            row = (mx[t].astype(F32) * inv * expert_gain[:, t * HD : (t + 1) * HD]).astype(BF16)
            logits = logits + mm(row, router[t * HD : (t + 1) * HD, :])
        b = iota((tok, E), 1)
        idv = ids[...]
        picks = [
            jnp.sum(jnp.where(idv[:, k : k + 1] == b, logits, 0.0), axis=1, keepdims=True)
            for k in range(idv.shape[1])
        ]
        best = picks[0]
        for p in picks[1:]:
            best = jnp.maximum(best, p)
        exps = [jnp.exp(p - best) for p in picks]
        den = exps[0]
        for e in exps[1:]:
            den = den + e
        cols = iota(mix.shape, 1)
        m = jnp.zeros(mix.shape, F32)
        for k, e in enumerate(exps):
            m = m + jnp.where(cols == tgt[k][:, 0:1], e / den, 0.0)
        mix[...] = m

    rflat = r.reshape(place.shape[1], HD)
    size = place.shape[1] // CHUNKS
    high = size - LOW

    def dev(axis, off):
        if axis == 0:
            return (w, y * NX + lax.rem(x + off + NX, NX))
        return (w, lax.rem(y + off + NY, NY) * NX + x)

    def pos_of(axis, off):
        if axis == 0:
            return lax.rem(x + off + NX, NX)
        return lax.rem(y + off + NY, NY)

    def xref(axis, b, o, lo, ln):
        if axis == 0:
            return xs.at[o, b, pl.ds(lo, ln), :]
        return xs.at[b, o, pl.ds(lo, ln), :]

    def hop(p, slot, b_off, o_off, half, to):
        axis, lo = p % 2, ORDER[p] * size
        lo, ln = {0: (lo, size), 1: (lo, LOW), 2: (lo + LOW, high)}[half]
        ref = xref(axis, pos_of(axis, b_off), pos_of(1 - axis, o_off), lo, ln)
        return rcopy(ref, ref, ss.at[p, slot], rrs.at[p, slot], to)

    def stage0(p):
        j, axis = ORDER[p], p % 2
        for i in range(nw // CHUNKS):
            ref = r.at[j * (nw // CHUNKS) + i]
            rcopy(ref, ref, ds.at[0], dr.at[j * (nw // CHUNKS) + i], sib).wait_recv()
        xs[y, x, pl.ds(j * size, size), :] = rflat[pl.ds(j * size, size), :]
        hop(p, 0, 0, 0, 0, dev(axis, 1)).start()
        hop(p, 1, 0, 0, 0, dev(axis, -1)).start()
        hop(p, 4, 0, 0, 0, dev(1 - axis, 1)).start()
        hop(p, 5, 0, 0, 0, dev(1 - axis, -1)).start()

    def stage1(p):
        axis = p % 2
        for slot, off, half in ((0, -1, 1), (1, 1, 2)):
            hop(p, slot, off, 0, 0, sib).wait_recv()
            hop(p, slot + 2, off, 0, half, dev(axis, -off)).start()
            hop(p, 8 + 4 * slot, off, 0, 0, dev(1 - axis, 1)).start()
            hop(p, 9 + 4 * slot, off, 0, 0, dev(1 - axis, -1)).start()

    def second(p, base, b_off):
        axis = p % 2
        hop(p, base, b_off, -1, 0, sib).wait_recv()
        hop(p, base + 2, b_off, -1, 1, dev(1 - axis, 1)).start()
        hop(p, base + 1, b_off, 1, 0, sib).wait_recv()
        hop(p, base + 3, b_off, 1, 2, dev(1 - axis, -1)).start()

    def stage2(p):
        axis = p % 2
        second(p, 4, 0)
        hop(p, 2, 2, 0, 1, sib).wait_recv()
        hop(p, 3, 2, 0, 2, sib).wait_recv()
        hop(p, 16, 2, 0, 0, dev(1 - axis, 1)).start()
        hop(p, 17, 2, 0, 0, dev(1 - axis, -1)).start()
        second(p, 8, -1)
        second(p, 12, 1)

    def stage3(p):
        second(p, 16, 2)

    def sref(axis, b, lo, ln):
        if axis == 0:
            return src.at[:, b, pl.ds(lo, ln), :]
        return src.at[b, :, pl.ds(lo, ln), :]

    def val(axis, b, lo, ln):
        return sref(axis, b, lo, ln)[...].astype(F32)

    def f1d(p, slot, lo, ln, to):
        ref = f1.at[p, :, pl.ds(lo, ln), :]
        return rcopy(ref, ref, us.at[p, slot], ur.at[p, slot], to)

    def f2d(p, slot, lo, ln, to):
        ref = f2.at[p, pl.ds(lo, ln), :]
        return rcopy(ref, ref, us.at[p, slot], ur.at[p, slot], to)

    def stage4(p):
        axis, lo = p % 2, ORDER[p] * size
        for base, b_off in ((4, 0), (8, -1), (12, 1), (16, 2)):
            hop(p, base + 2, b_off, 2, 1, sib).wait_recv()
            hop(p, base + 3, b_off, 2, 2, sib).wait_recv()
        units = jnp.zeros((size, 4 * fw), F32)
        for t in range(nn):
            units = units + mm(xs[t // NX, t % NX, lo : lo + size, :], wgt[t * HD : (t + 1) * HD, :])
        gt = units[:, : 2 * fw]
        act = gt / (1.0 + jnp.exp(-gt)) * units[:, 2 * fw :]
        row = lax.rem(iota(act.shape, 0), 2 * CAP)
        keep = (row >= CAP) == (iota(act.shape, 1) >= fw)
        act = jnp.where(keep, act, 0.0).astype(BF16)
        dn = down[...].reshape(2 * fw, -1)
        for t in range(nn):
            src[t // NX, t % NX, lo : lo + size, :] = mm(act, dn[:, t * HD : (t + 1) * HD]).astype(BF16)
        b2 = pos_of(axis, 2)
        rcopy(sref(axis, b2, lo, LOW), f1.at[p, :, pl.ds(0, LOW), :], us.at[p, 0], ur.at[p, 0], dev(axis, 1)).start()
        rcopy(
            sref(axis, b2, lo + LOW, high), f1.at[p, :, pl.ds(LOW, high), :], us.at[p, 1], ur.at[p, 1], dev(axis, -1)
        ).start()

    def t1d(p, k, to):
        return rcopy(t1.at[p, k], r1.at[p, k], us.at[p, 2 + k], ur.at[p, 2 + k], to)

    def t2d(p, k, to):
        return rcopy(t2.at[p, k], r2.at[p, k], us.at[p, 6 + k], ur.at[p, 6 + k], to)

    def stage5(p):
        axis, lo = p % 2, ORDER[p] * size
        bp, bm = pos_of(axis, 1), pos_of(axis, -1)
        t1[p, 0, :, LOW:, :] = sref(axis, bp, lo + LOW, high)[...]
        t1[p, 1, :, :LOW, :] = sref(axis, bm, lo, LOW)[...]
        f1d(p, 0, 0, LOW, sib).wait_recv()
        t1[p, 0, :, :LOW, :] = (val(axis, bp, lo, LOW) + f1[p, :, :LOW, :].astype(F32)).astype(BF16)
        t1d(p, 0, dev(axis, 1)).start()
        f1d(p, 1, LOW, high, sib).wait_recv()
        t1[p, 1, :, LOW:, :] = (val(axis, bm, lo + LOW, high) + f1[p, :, LOW:, :].astype(F32)).astype(BF16)
        t1d(p, 1, dev(axis, -1)).start()

    def stage6(p):
        axis, lo = p % 2, ORDER[p] * size
        t1d(p, 0, sib).wait_recv()
        t1d(p, 1, sib).wait_recv()
        m2[p] = (val(axis, pos_of(axis, 0), lo, size) + r1[p, 0].astype(F32) + r1[p, 1].astype(F32)).astype(BF16)
        b2 = pos_of(1 - axis, 2)
        rcopy(m2.at[p, b2, pl.ds(0, LOW), :], f2.at[p, pl.ds(0, LOW), :], us.at[p, 4], ur.at[p, 4], dev(1 - axis, 1)).start()
        rcopy(
            m2.at[p, b2, pl.ds(LOW, high), :], f2.at[p, pl.ds(LOW, high), :], us.at[p, 5], ur.at[p, 5], dev(1 - axis, -1)
        ).start()

    def stage7(p):
        axis = p % 2
        bp, bm = pos_of(1 - axis, 1), pos_of(1 - axis, -1)
        t2[p, 0, LOW:, :] = m2[p, bp, LOW:, :]
        t2[p, 1, :LOW, :] = m2[p, bm, :LOW, :]
        f2d(p, 4, 0, LOW, sib).wait_recv()
        t2[p, 0, :LOW, :] = (m2[p, bp, :LOW, :].astype(F32) + f2[p, :LOW, :].astype(F32)).astype(BF16)
        t2d(p, 0, dev(1 - axis, 1)).start()
        f2d(p, 5, LOW, high, sib).wait_recv()
        t2[p, 1, LOW:, :] = (m2[p, bm, LOW:, :].astype(F32) + f2[p, LOW:, :].astype(F32)).astype(BF16)
        t2d(p, 1, dev(1 - axis, -1)).start()

    bflat = bbuf.reshape(place.shape[1], HD)

    def stage8(p):
        j, axis = ORDER[p], p % 2
        t2d(p, 0, sib).wait_recv()
        t2d(p, 1, sib).wait_recv()
        bflat[pl.ds(j * size, size), :] = (
            m2[p, pos_of(1 - axis, 0)].astype(F32) + r2[p, 0].astype(F32) + r2[p, 1].astype(F32)
        ).astype(BF16)
        for i in range(nz // CHUNKS):
            rel = j * (nz // CHUNKS) + i
            for core in range(2):
                t = chip(rel - nz // 2) * 2 + core
                a = bbuf.at[rel * 2 + core]
                if rel == nz // 2:
                    if core == 0:
                        pltpu.make_async_copy(bbuf.at[nz + c], bk.at[w], er.at[w]).start()
                        rcopy(bbuf.at[nz + 1 - c], bk.at[w], es.at[nz + 1 - c], er.at[w], sib).start()
                else:
                    rcopy(a, bk.at[w], es.at[rel * 2 + core], er.at[w], (t, n)).start()

    stages = (stage0, stage1, stage2, stage3, stage4, stage5, stage6, stage7, stage8)
    for t in range(CHUNKS + len(stages) - 1):
        for k in reversed(range(len(stages))):
            if 0 <= t - k < CHUNKS:
                stages[k](t - k)
        if t == 0:
            fill_router()

    def wait_b(d, _):
        t = lax.rem(w + d, nw)
        rcopy(bk.at[t], bk.at[t], es.at[t], er.at[t], sib).wait_recv()
        return 0

    lax.fori_loop(0, nw, wait_b, 0)
    moe = lax.dot_general(
        mix[...], bk.reshape(place.shape[1], HD)[...].astype(F32), (((1,), (0,)), ((), ())),
        precision=lax.Precision.HIGHEST, preferred_element_type=F32,
    )
    layer_out[...] = (mx[n].astype(F32) + moe).astype(BF16)

    for s in range(nz // 2):
        for i in range(2):
            if s < nz // 2 - 1 or i == 0:
                ring(s, c if i == 0 else 1 - c).wait_send()
        oring(s).wait_send()
    side(z, c).wait_send()
    o_side.wait_send()
    for s in range(1, nz // 2):
        for sub in range(2):
            side(chip(-sg * s), sub).wait_send()
        oside(s, True).wait_send()
    side(chip(nz // 2), c).wait_send()
    oside(nz // 2, True).wait_send()

    def sent_w(d, _):
        t = lax.rem(w + d, nw)
        rcopy(ps.at[t], pr.at[w], pss.at[t], psr.at[w], sib).wait_send()
        rcopy(dbuf.at[t], r.at[0], ds.at[t], dr.at[0], sib).wait_send()
        return 0

    lax.fori_loop(1, nw, sent_w, 0)

    def sent_b(d, _):
        t = lax.rem(nz + c + d, nw)
        rcopy(bbuf.at[t], bk.at[w], es.at[t], er.at[w], sib).wait_send()
        return 0

    lax.fori_loop(1, nw, sent_b, 0)

    def sent_n(d, _):
        t = lax.rem(n + d, nn)
        rcopy(part.at[t], rbuf.at[n], s1.at[t], r1s.at[n], sib).wait_send()
        rcopy(ssb.at[n], ssb.at[n], s3.at[t], r3s.at[n], sib).wait_send()
        rcopy(mx.at[n], mx.at[n], s2.at[t], r2s.at[n], sib).wait_send()
        return 0

    lax.fori_loop(1, nn, sent_n, 0)
    for p in range(CHUNKS):
        for slot in range(20):
            half = 0 if slot < 2 or slot % 4 < 2 else slot % 4 - 1
            hop(p, slot, 0, 0, half, sib).wait_send()
        f1d(p, 0, 0, LOW, sib).wait_send()
        f1d(p, 1, LOW, high, sib).wait_send()
        f2d(p, 4, 0, LOW, sib).wait_send()
        f2d(p, 5, LOW, high, sib).wait_send()
        for k in range(2):
            t1d(p, k, sib).wait_send()
            t2d(p, k, sib).wait_send()


def body(
    hidden, attn_gain, expert_gain, query_weight, key_weight, value_weight, output_weight, router_weight,
    gate_weight, up_weight, down_weight, prefix_keys, prefix_values, cache_keys, cache_values, parents,
    cache_lengths, group_ids, expert_ids, accepted,
):
    tok, width = hidden.shape
    nn = lax.axis_size("narrow")
    nw = lax.axis_size("wide")
    nz = nw // 2
    rows = nw * gate_weight.shape[0] * CAP
    size = rows // CHUNKS
    cache = cache_keys.shape[1]
    vm = pl.BlockSpec(memory_space=pltpu.VMEM)
    sm = pl.BlockSpec(memory_space=pltpu.SMEM)
    dma = pltpu.SemaphoreType.DMA

    def v(*shape, t=BF16):
        return pltpu.VMEM(shape, t)

    pair = rows // nw // 2
    scratch = [
        v(tok, width), v(nz, 2, 3, 64, HD), v(nz, 2, 64, HD), v(nw, 16, HD), v(nw, 16, HD),
        v(tok, HD), v(tok, HD), v(tok, HD), v(tok, cache, t=F32), v(tok, tok, t=F32), v(tok, tok, t=F32),
        v(cache, tok), v(nn, tok, HD), v(nn, tok, HD), v(nn, tok, HD), v(nn, 8, HD, t=F32),
        v(width, 4 * gate_weight.shape[2]), v(expert_ids.shape[1], tok, HD, t=jnp.int32), v(tok, rows), v(tok, rows, t=F32),
        v(nw, pair, 2, HD), v(nw, pair, 2, HD), v(NY, NX, rows, HD), v(NY, NX, rows, HD),
        v(CHUNKS, 2, 4, size, HD), v(CHUNKS, 4, size, HD), v(CHUNKS, 2, 4, size, HD), v(CHUNKS, 4, size, HD),
        v(CHUNKS, 2, size, HD), v(CHUNKS, size, HD), v(CHUNKS, 2, size, HD), v(nw, pair, 2, HD), v(nw, pair, 2, HD),
        dma((4,)), dma((nz // 2, 2)), dma((nz // 2, 2)), dma((nz, 2)), dma((nz, 2)),
        dma((nz // 2,)), dma((nz // 2,)), dma((nz + 1,)), dma((nz + 1,)), dma((nw,)), dma((nw,)),
        dma((nn,)), dma((nn,)), dma((nn,)), dma((nn,)), dma((nn,)), dma((nn,)), dma((nw,)), dma((nw,)),
        dma((CHUNKS, 20)), dma((CHUNKS, 20)), dma((CHUNKS, 8)), dma((CHUNKS, 8)), dma((nw,)), dma((nw,)),
    ]
    return pl.pallas_call(
        layer_kernel,
        out_shape=(
            jax.ShapeDtypeStruct((tok, HD), BF16),
            jax.ShapeDtypeStruct(cache_keys.shape, BF16),
            jax.ShapeDtypeStruct(cache_values.shape, BF16),
        ),
        in_specs=[sm, sm] + [vm] * 18,
        out_specs=(vm, vm, vm),
        scratch_shapes=scratch,
        compiler_params=pltpu.CompilerParams(
            collective_id=0, has_side_effects=True, vmem_limit_bytes=60 * 1024 * 1024
        ),
        name="layer",
    )(
        cache_lengths, accepted, hidden, attn_gain[None], expert_gain[None], query_weight, key_weight, value_weight,
        output_weight, router_weight, gate_weight, up_weight, down_weight, prefix_keys, prefix_values,
        cache_keys, cache_values, parents, group_ids[None], expert_ids,
    )


def solution(mesh):
    in_specs = (
        P("wide", None),
        P(),
        P(),
        P("wide", "narrow"),
        P("wide", "narrow"),
        P("wide", "narrow"),
        P("wide", "narrow"),
        P(),
        P("wide", None, "narrow"),
        P("wide", None, "narrow"),
        P("wide", "narrow", None),
        P("wide", None, "narrow"),
        P("wide", None, "narrow"),
        P("wide", None, "narrow"),
        P("wide", None, "narrow"),
        P("wide", None),
        P("wide"),
        P(),
        P("wide", None),
        P("wide"),
    )
    out_specs = (P("wide", "narrow"), P("wide", None, "narrow"), P("wide", None, "narrow"))
    return jax.shard_map(body, mesh=mesh, in_specs=in_specs, out_specs=out_specs, check_vma=False)
```

```python
import math

import jax
import jax.numpy as jnp
from jax import lax
from jax.experimental import pallas as pl
from jax.experimental.pallas import tpu as pltpu
from jax.sharding import PartitionSpec as P

HD = 128
E = 64
SINK = 4
WIN = 512
CAP = 9
NX = 4
NY = 4
MESH = pl.DeviceIdType.MESH
F32 = jnp.float32
BF16 = jnp.bfloat16

norm_eps = 1e-06


def rms_scale(rows, row_gain):
    widened = rows.astype(F32)
    power_mean = jnp.mean(widened * widened, axis=-1, keepdims=True)
    return (widened * lax.rsqrt(power_mean + norm_eps) * row_gain).astype(BF16)


DIMS0 = (((0,), (0,)), ((), ()))
DIMS1 = (((1,), (1,)), ((), ()))
CHUNKS = 4
ORDER = (2, 1, 3, 0)
LOW = 80
NEG = -1e30


def rcopy(src, dst, ssem, rsem, dev):
    return pltpu.make_async_remote_copy(
        src_ref=src, dst_ref=dst, send_sem=ssem, recv_sem=rsem, device_id=dev, device_id_type=MESH
    )


def iota(shape, dim):
    return lax.broadcasted_iota(jnp.int32, shape, dim)


def mm(a, b, dims=(((1,), (0,)), ((), ()))):
    return lax.dot_general(a, b, dims, preferred_element_type=F32)


def layer_kernel(
    lens, acc_node, attn_gain, expert_gain, parents, groups, ids,
    hidden_in, q_in, k_in, v_in, o_in, router_in, gate, up, down, pk_in, pv_in, ck_in, cv_in,
    layer_out, new_k, new_v,
    hidden, router, wgt, dn, cache_k, cache_v, pk, pv, proj,
    normed, g, go, ps, pr, qs, ks, vs, cs, ts, anc, put, part, rbuf, mx, tgt, place, mix,
    dbuf, r, xs, src, r1, f1, t1, m2, r2, f2, t2, bbuf, bk,
    ls, rs, rr, fs, fr, os, orr, ofs, ofr, pss, psr, s1, r1s, s2, r2s, ds, dr, ss, rrs, us, ur, es, er,
):
    nz, nn, nw = g.shape[0], part.shape[0], pr.shape[0]
    tok = hidden.shape[0]
    w = lax.axis_index("wide")
    n = lax.axis_index("narrow")
    z = w // 2
    c = lax.rem(w, 2)
    y = n // NX
    x = lax.rem(n, NX)
    sg = 1 - 2 * c
    sib_w = w + sg
    sib = (sib_w, n)

    def chip(off):
        return lax.rem(z + off + nz, nz)

    nxt = (chip(sg) * 2 + c, n)

    barrier = pltpu.get_barrier_semaphore()
    for t in (sib, (chip(1) * 2 + c, n), (chip(nz - 1) * 2 + c, n)):
        pl.semaphore_signal(barrier, inc=1, device_id=t, device_id_type=MESH)

    def greet(d, _):
        pl.semaphore_signal(barrier, inc=1, device_id=(w, lax.rem(n + d, nn)), device_id_type=MESH)
        return 0

    lax.fori_loop(1, nn, greet, 0)
    fw = gate.shape[1]
    moves = (
        (q_in, g.at[z, c, 0]), (k_in, g.at[z, c, 1]), (v_in, g.at[z, c, 2]), (o_in, go.at[z, c]),
        (hidden_in, hidden), (pk_in, pk), (pv_in, pv), (ck_in.at[0], cache_k), (cv_in.at[0], cache_v),
        (gate.at[0], wgt.at[pl.ds(0, fw), :]), (gate.at[1], wgt.at[pl.ds(fw, fw), :]),
        (up.at[0], wgt.at[pl.ds(2 * fw, fw), :]), (up.at[1], wgt.at[pl.ds(3 * fw, fw), :]),
        (down.at[0], dn.at[pl.ds(0, fw), :]), (down.at[1], dn.at[pl.ds(fw, fw), :]), (router_in, router),
    )
    local = [pltpu.make_async_copy(a, b, ls.at[i]) for i, (a, b) in enumerate(moves)]
    for cp in local:
        cp.start()
    for cp in local[:4]:
        cp.wait()
    pl.semaphore_wait(barrier, nn + 2)

    def ring(s, sub):
        ref = g.at[chip(-sg * s), sub]
        return rcopy(ref, ref, rs.at[s, sub], rr.at[s, sub], nxt)

    def got(s, sub):
        ref = g.at[chip(-sg * (s + 1)), sub]
        return rcopy(ref, ref, rs.at[s, sub], rr.at[s, sub], nxt)

    def side(chip_id, sub):
        ref = g.at[chip_id, sub]
        return rcopy(ref, ref, fs.at[chip_id, sub], fr.at[chip_id, sub], sib)

    side(z, c).start()
    oref = go.at[z, c]
    o_side = rcopy(oref, oref, ofs.at[nz], ofr.at[nz], sib)
    o_side.start()
    ring(0, c).start()
    osib = go.at[z, 1 - c]
    side(z, 1 - c).wait_recv()
    ring(0, 1 - c).start()

    local[4].wait()
    hv = hidden[...].astype(F32)
    power = jnp.mean(hv * hv, axis=-1, keepdims=True)
    normed[...] = (hv * lax.rsqrt(power + norm_eps) * attn_gain[...]).astype(BF16)
    proj[...] = jnp.zeros_like(proj)

    def fill_prefix():
        local[5].wait()
        local[6].wait()
        rows, cols = nw * 16, 64
        it = iota((rows, nw), 0) // 16
        gid = jnp.sum(jnp.where(it == iota((rows, nw), 1), groups[...], 0), axis=1, keepdims=True)
        r_id = lax.rem(iota((rows, cols), 0), 16)
        c_id = iota((rows, cols), 1)
        same = lax.rem(c_id, 8) == gid
        one_k = (same & (c_id // 8 == r_id)).astype(F32).astype(BF16)
        one_v = (same & (c_id // 8 + 8 == r_id)).astype(F32).astype(BF16)
        picked = mm(one_k, pk[...].reshape(cols, HD)) + mm(one_v, pv[...].reshape(cols, HD))
        ps[...] = picked.astype(BF16).reshape(ps.shape)

    def fill_tree():
        size = parents.shape[1]
        a, b = iota((size, size), 0), iota((size, size), 1)
        eye = (a == b).astype(F32)
        up_t = jnp.maximum(eye, (parents[...] == a).astype(F32))
        for _ in range(6):
            m = up_t.astype(BF16)
            up_t = (mm(m, m) > 0.5).astype(F32)
        depth = jnp.sum(up_t, axis=0, keepdims=True) - 1.0
        full = mm(up_t.astype(BF16), eye.astype(BF16), DIMS0)
        anc[...] = full
        on_path = jnp.sum(jnp.where(a == acc_node[0], full, 0.0), axis=0, keepdims=True)
        slot = jnp.where(on_path > 0.5, lens[0] + depth.astype(jnp.int32), put.shape[0])
        put[...] = (iota(put.shape, 0) == slot).astype(F32).astype(BF16)

    def fill_slots():
        a, b = iota((E, tok), 0), iota((E, tok), 1)
        named = jnp.zeros((E, tok), F32)
        for k in range(ids.shape[0]):
            named = named + (ids[k : k + 1, :] == a).astype(F32)
        earlier = mm(named.astype(BF16), (iota((tok, tok), 0) < iota((tok, tok), 1)).astype(F32).astype(BF16))
        hit = jnp.zeros(place.shape, F32)
        rows = iota(place.shape, 0)
        for k in range(ids.shape[0]):
            idk = ids[k : k + 1, :]
            rank = jnp.sum(jnp.where(idk == a, earlier, 0.0), axis=0, keepdims=True)
            t = idk * CAP + rank.astype(jnp.int32)
            tgt[k : k + 1, :] = t
            hit = hit + (rows == t).astype(F32)
        place[...] = hit.astype(BF16)

    def oring(s):
        k = chip(-sg * s)
        ref = go.at[k] if s < nz // 2 - 1 else go.at[k, c]
        return rcopy(ref, ref, os.at[s], orr.at[s], nxt)

    def ogot(s):
        k = chip(-sg * (s + 1))
        ref = go.at[k] if s < nz // 2 - 1 else go.at[k, c]
        return rcopy(ref, ref, os.at[s], orr.at[s], nxt)

    def oside(s, mine):
        k = chip(-sg * s) if mine else chip(sg * s)
        ref = go.at[k] if s < nz // 2 else go.at[k, c if mine else 1 - c]
        return rcopy(ref, ref, ofs.at[k], ofr.at[k], sib)

    def send_prefix(k):
        for core in range(2):
            t = k * 2 + core
            rcopy(ps.at[t], pr.at[w], pss.at[t], psr.at[w], (t, n)).start()

    def project(k):
        cols = pl.ds(pl.multiple_of(k * HD, HD), HD)
        a = normed[:, cols]
        for i in range(3):
            b = jnp.concatenate([g[k, 0, i], g[k, 1, i]], axis=0)
            proj[:, i * HD : (i + 1) * HD] += mm(a, b)

    fill_prefix()
    rcopy(osib, osib, ofs.at[nz], ofr.at[nz], sib).wait_recv()
    oring(0).start()
    cp_own = pltpu.make_async_copy(ps.at[w], pr.at[w], psr.at[w])
    cp_own.start()
    rcopy(ps.at[sib_w], pr.at[w], pss.at[sib_w], psr.at[w], sib).start()
    project(z)
    fillers = {1: fill_tree, 2: fill_slots}
    for s in range(1, nz // 2):
        for i in range(2):
            sub = c if i == 0 else 1 - c
            got(s - 1, sub).wait_recv()
            if s < nz // 2 - 1 or i == 0:
                ring(s, sub).start()
            side(chip(-sg * s), sub).start()
        ogot(s - 1).wait_recv()
        oring(s).start()
        oside(s, True).start()
        send_prefix(chip(-sg * s))
        if s > 1:
            for sub in range(2):
                side(chip(sg * (s - 1)), sub).wait_recv()
            send_prefix(chip(sg * (s - 1)))
            project(chip(sg * (s - 1)))
        project(chip(-sg * s))
        if s in fillers:
            fillers[s]()
    got(nz // 2 - 1, c).wait_recv()
    side(chip(nz // 2), c).start()
    ogot(nz // 2 - 1).wait_recv()
    oside(nz // 2, True).start()
    for sub in range(2):
        side(chip(sg * (nz // 2 - 1)), sub).wait_recv()
    send_prefix(chip(sg * (nz // 2 - 1)))
    side(chip(nz // 2), 1 - c).wait_recv()
    send_prefix(chip(nz // 2))
    project(chip(sg * (nz // 2 - 1)))
    project(chip(nz // 2))
    for i, ref in enumerate((qs, ks, vs)):
        ref[...] = proj[:, i * HD : (i + 1) * HD].astype(BF16)

    def drain_ring():
        for s in range(nz // 2):
            for i in range(2):
                if s < nz // 2 - 1 or i == 0:
                    ring(s, c if i == 0 else 1 - c).wait_send()
        side(z, c).wait_send()
        o_side.wait_send()
        for s in range(1, nz // 2):
            for sub in range(2):
                side(chip(-sg * s), sub).wait_send()
        side(chip(nz // 2), c).wait_send()

    scale = 1.0 / math.sqrt(HD)
    local[7].wait()
    pos = iota(cs.shape, 1)
    ok = (pos < lens[0]) & ((pos < SINK) | (pos >= lens[0] - WIN))
    cs[...] = jnp.where(ok, mm(qs[...], cache_k[...], DIMS1) * scale, NEG)
    ts[...] = jnp.where(anc[...] > 0.5, mm(qs[...], ks[...], DIMS1) * scale, NEG)

    def compact(fresh, cache, out):
        moved = mm(put[...], fresh[...])
        written = jnp.sum(put[...].astype(F32), axis=1, keepdims=True) > 0.5
        out[0] = jnp.where(written, moved.astype(BF16), cache[...])

    cp_own.wait()

    def pwait(d, _):
        t = lax.rem(w + d, nw)
        rcopy(pr.at[t], pr.at[t], pss.at[t], psr.at[t], sib).wait_recv()
        return 0

    lax.fori_loop(1, nw, pwait, 0)
    def drain_out():
        for s in range(nz // 2):
            oring(s).wait_send()
        for s in range(1, nz // 2 + 1):
            oside(s, True).wait_send()

        def sent_p(d, _):
            t = lax.rem(w + d, nw)
            rcopy(ps.at[t], pr.at[w], pss.at[t], psr.at[w], sib).wait_send()
            return 0

        lax.fori_loop(1, nw, sent_p, 0)

    prows = pr[...].reshape(-1, HD)
    is_key = lax.rem(iota((tok, nw * 16), 1), 16) < 8
    psc = jnp.where(is_key, mm(qs[...], prows, DIMS1) * scale, NEG)
    csc, tsc = cs[...], ts[...]
    top = jnp.maximum(
        jnp.max(psc, axis=1, keepdims=True),
        jnp.maximum(jnp.max(csc, axis=1, keepdims=True), jnp.max(tsc, axis=1, keepdims=True)),
    )
    pw = jnp.where(is_key, jnp.exp(psc - top), 0.0)
    pos = iota(cs.shape, 1)
    ok = (pos < lens[0]) & ((pos < SINK) | (pos >= lens[0] - WIN))
    cw = jnp.where(ok, jnp.exp(csc - top), 0.0)
    tw = jnp.where(anc[...] > 0.5, jnp.exp(tsc - top), 0.0)
    total = (
        jnp.sum(pw, axis=1, keepdims=True) + jnp.sum(cw, axis=1, keepdims=True) + jnp.sum(tw, axis=1, keepdims=True)
    )
    local[8].wait()
    weighted = (
        mm(pltpu.roll(pw, 8, 1).astype(BF16), prows)
        + mm(cw.astype(BF16), cache_v[...])
        + mm(tw.astype(BF16), vs[...])
    )
    attended = (weighted / total).astype(BF16)
    for s in range(1, nz // 2 + 1):
        oside(s, False).wait_recv()
    for i in range(4):
        four = go[i * 4 : i * 4 + 4].reshape(512, HD)
        terms = mm(attended, four, DIMS1)
        for j in range(4):
            part[i * 4 + j] = terms[:, j * HD : (j + 1) * HD].astype(BF16)

    def send1(d, _):
        t = lax.rem(n + d, nn)
        rcopy(part.at[t], rbuf.at[n], s1.at[t], r1s.at[n], (w, t)).start()
        return 0

    lax.fori_loop(1, nn, send1, 0)
    col = pl.multiple_of(n * HD, HD)

    def add1(d, acc):
        t = lax.rem(n + d, nn)
        rcopy(rbuf.at[t], rbuf.at[t], s1.at[t], r1s.at[t], (w, t)).wait_recv()
        return acc + rbuf[t].astype(F32)

    summed = lax.fori_loop(1, nn, add1, part[n].astype(F32))
    mixed = (hidden[:, pl.ds(col, HD)].astype(F32) + summed).astype(BF16)
    mx[n] = mixed
    slots = mm(place[...], mixed)
    dflat = dbuf.reshape(place.shape[0], HD)
    dflat[...] = slots.astype(BF16)


    def drain_plane():
        def sent_n(d, _):
            t = lax.rem(n + d, nn)
            rcopy(part.at[t], rbuf.at[n], s1.at[t], r1s.at[n], sib).wait_send()
            rcopy(mx.at[n], mx.at[n], s2.at[t], r2s.at[n], sib).wait_send()
            return 0

        lax.fori_loop(1, nn, sent_n, 0)

    def slot_of(dz):
        return lax.rem(nz + nz // 2 - dz, nz) * 2 + c

    def send_d(dz, core):
        t = chip(dz) * 2 + core
        rcopy(dbuf.at[t], r.at[slot_of(dz)], ds.at[t], dr.at[slot_of(dz)], (t, n)).start()

    cp_d = pltpu.make_async_copy(dbuf.at[w], r.at[nz + c], dr.at[nz + c])
    cp_d.start()
    send_d(0, 1 - c)
    for k in range(1, nz // 2):
        for dz in (k, -k):
            for core in range(2):
                send_d(dz, core)
    for core in range(2):
        send_d(nz // 2, core)
    def send2(d, _):
        t = lax.rem(n + d, nn)
        rcopy(mx.at[n], mx.at[n], s2.at[t], r2s.at[n], (w, t)).start()
        return 0

    lax.fori_loop(1, nn, send2, 0)
    compact(ks, cache_k, new_k)
    compact(vs, cache_v, new_v)

    def wait2(d, _):
        t = lax.rem(n + d, nn)
        rcopy(mx.at[t], mx.at[t], s2.at[t], r2s.at[t], (w, t)).wait_recv()
        return 0

    def fill_router():
        lax.fori_loop(1, nn, wait2, 0)
        local[15].wait()
        power = jnp.zeros((tok, 1), F32)
        for t in range(nn):
            m = mx[t].astype(F32)
            power = power + jnp.sum(m * m, axis=1, keepdims=True)
        inv = lax.rsqrt(power / (nn * HD) + norm_eps)
        logits = jnp.zeros((E, tok), F32)
        for t in range(nn):
            row = (mx[t].astype(F32) * inv * expert_gain[:, t * HD : (t + 1) * HD]).astype(BF16)
            logits = logits + mm(router[:, t * HD : (t + 1) * HD], row, DIMS1)
        a = iota((E, tok), 0)
        picks = [
            jnp.sum(jnp.where(ids[k : k + 1, :] == a, logits, 0.0), axis=0, keepdims=True)
            for k in range(ids.shape[0])
        ]
        best = picks[0]
        for p in picks[1:]:
            best = jnp.maximum(best, p)
        exps = [jnp.exp(p - best) for p in picks]
        den = exps[0]
        for e in exps[1:]:
            den = den + e
        rows = iota(mix.shape, 0)
        m = jnp.zeros(mix.shape, F32)
        for k, e in enumerate(exps):
            m = m + jnp.where(rows == tgt[k : k + 1, :], e / den, 0.0)
        mix[...] = m

    def drain_dispatch():
        def sent_d(d, _):
            t = lax.rem(w + d, nw)
            rcopy(dbuf.at[t], r.at[0], ds.at[t], dr.at[0], sib).wait_send()
            return 0

        lax.fori_loop(1, nw, sent_d, 0)

    rflat = r.reshape(place.shape[0], HD)
    size = place.shape[0] // CHUNKS
    high = size - LOW

    def dev(axis, off):
        if axis == 0:
            return (w, y * NX + lax.rem(x + off + NX, NX))
        return (w, lax.rem(y + off + NY, NY) * NX + x)

    def pos_of(axis, off):
        if axis == 0:
            return lax.rem(x + off + NX, NX)
        return lax.rem(y + off + NY, NY)

    def xref(axis, b, o, lo, ln):
        if axis == 0:
            return xs.at[o, b, pl.ds(lo, ln), :]
        return xs.at[b, o, pl.ds(lo, ln), :]

    def hop(p, slot, b_off, o_off, half, to):
        axis, lo = p % 2, ORDER[p] * size
        lo, ln = {0: (lo, size), 1: (lo, LOW), 2: (lo + LOW, high)}[half]
        ref = xref(axis, pos_of(axis, b_off), pos_of(1 - axis, o_off), lo, ln)
        return rcopy(ref, ref, ss.at[p, slot], rrs.at[p, slot], to)

    def stage0(p):
        j, axis = ORDER[p], p % 2
        for i in range(nw // CHUNKS):
            ref = r.at[j * (nw // CHUNKS) + i]
            rcopy(ref, ref, ds.at[0], dr.at[j * (nw // CHUNKS) + i], sib).wait_recv()
        xs[y, x, pl.ds(j * size, size), :] = rflat[pl.ds(j * size, size), :]
        hop(p, 0, 0, 0, 0, dev(axis, 1)).start()
        hop(p, 1, 0, 0, 0, dev(axis, -1)).start()
        hop(p, 4, 0, 0, 0, dev(1 - axis, 1)).start()
        hop(p, 5, 0, 0, 0, dev(1 - axis, -1)).start()

    def stage1(p):
        axis = p % 2
        for slot, off, half in ((0, -1, 1), (1, 1, 2)):
            hop(p, slot, off, 0, 0, sib).wait_recv()
            hop(p, slot + 2, off, 0, half, dev(axis, -off)).start()
            hop(p, 8 + 4 * slot, off, 0, 0, dev(1 - axis, 1)).start()
            hop(p, 9 + 4 * slot, off, 0, 0, dev(1 - axis, -1)).start()

    def second(p, base, b_off):
        axis = p % 2
        hop(p, base, b_off, -1, 0, sib).wait_recv()
        hop(p, base + 2, b_off, -1, 1, dev(1 - axis, 1)).start()
        hop(p, base + 1, b_off, 1, 0, sib).wait_recv()
        hop(p, base + 3, b_off, 1, 2, dev(1 - axis, -1)).start()

    def stage2(p):
        axis = p % 2
        second(p, 4, 0)
        hop(p, 2, 2, 0, 1, sib).wait_recv()
        hop(p, 3, 2, 0, 2, sib).wait_recv()
        hop(p, 16, 2, 0, 0, dev(1 - axis, 1)).start()
        hop(p, 17, 2, 0, 0, dev(1 - axis, -1)).start()
        second(p, 8, -1)
        second(p, 12, 1)

    def stage3(p):
        second(p, 16, 2)

    def sref(axis, b, lo, ln):
        if axis == 0:
            return src.at[:, b, pl.ds(lo, ln), :]
        return src.at[b, :, pl.ds(lo, ln), :]

    def val(axis, b, lo, ln):
        return sref(axis, b, lo, ln)[...].astype(F32)

    def f1d(p, slot, lo, ln, to):
        ref = f1.at[p, :, pl.ds(lo, ln), :]
        return rcopy(ref, ref, us.at[p, slot], ur.at[p, slot], to)

    def f2d(p, slot, lo, ln, to):
        ref = f2.at[p, pl.ds(lo, ln), :]
        return rcopy(ref, ref, us.at[p, slot], ur.at[p, slot], to)

    def stage4(p):
        axis, lo = p % 2, ORDER[p] * size
        for base, b_off in ((4, 0), (8, -1), (12, 1), (16, 2)):
            hop(p, base + 2, b_off, 2, 1, sib).wait_recv()
            hop(p, base + 3, b_off, 2, 2, sib).wait_recv()
        if p == 0:
            for cp in local[9:15]:
                cp.wait()
        power = jnp.zeros((size, 1), F32)
        for t in range(nn):
            m = xs[t // NX, t % NX, lo : lo + size, :].astype(F32)
            power = power + jnp.sum(m * m, axis=1, keepdims=True)
        inv = lax.rsqrt(power / (nn * HD) + norm_eps)
        units = jnp.zeros((size, 4 * fw), F32)
        for t in range(nn):
            m = xs[t // NX, t % NX, lo : lo + size, :].astype(F32)
            m = (m * inv * expert_gain[:, t * HD : (t + 1) * HD]).astype(BF16)
            units = units + mm(m, wgt[:, t * HD : (t + 1) * HD], DIMS1)
        gt = units[:, : 2 * fw]
        act = gt / (1.0 + jnp.exp(-gt)) * units[:, 2 * fw :]
        row = lax.rem(iota(act.shape, 0), 2 * CAP)
        keep = (row >= CAP) == (iota(act.shape, 1) >= fw)
        act = jnp.where(keep, act, 0.0).astype(BF16)
        for t in range(nn):
            src[t // NX, t % NX, lo : lo + size, :] = mm(act, dn[:, t * HD : (t + 1) * HD]).astype(BF16)
        b2 = pos_of(axis, 2)
        rcopy(sref(axis, b2, lo, LOW), f1.at[p, :, pl.ds(0, LOW), :], us.at[p, 0], ur.at[p, 0], dev(axis, 1)).start()
        rcopy(
            sref(axis, b2, lo + LOW, high), f1.at[p, :, pl.ds(LOW, high), :], us.at[p, 1], ur.at[p, 1], dev(axis, -1)
        ).start()

    def t1d(p, k, to):
        return rcopy(t1.at[p, k], r1.at[p, k], us.at[p, 2 + k], ur.at[p, 2 + k], to)

    def t2d(p, k, to):
        return rcopy(t2.at[p, k], r2.at[p, k], us.at[p, 6 + k], ur.at[p, 6 + k], to)

    def stage5(p):
        axis, lo = p % 2, ORDER[p] * size
        bp, bm = pos_of(axis, 1), pos_of(axis, -1)
        t1[p, 0, :, LOW:, :] = sref(axis, bp, lo + LOW, high)[...]
        t1[p, 1, :, :LOW, :] = sref(axis, bm, lo, LOW)[...]
        f1d(p, 0, 0, LOW, sib).wait_recv()
        t1[p, 0, :, :LOW, :] = (val(axis, bp, lo, LOW) + f1[p, :, :LOW, :].astype(F32)).astype(BF16)
        t1d(p, 0, dev(axis, 1)).start()
        f1d(p, 1, LOW, high, sib).wait_recv()
        t1[p, 1, :, LOW:, :] = (val(axis, bm, lo + LOW, high) + f1[p, :, LOW:, :].astype(F32)).astype(BF16)
        t1d(p, 1, dev(axis, -1)).start()

    def stage6(p):
        axis, lo = p % 2, ORDER[p] * size
        t1d(p, 0, sib).wait_recv()
        t1d(p, 1, sib).wait_recv()
        m2[p] = (val(axis, pos_of(axis, 0), lo, size) + r1[p, 0].astype(F32) + r1[p, 1].astype(F32)).astype(BF16)
        b2 = pos_of(1 - axis, 2)
        rcopy(m2.at[p, b2, pl.ds(0, LOW), :], f2.at[p, pl.ds(0, LOW), :], us.at[p, 4], ur.at[p, 4], dev(1 - axis, 1)).start()
        rcopy(
            m2.at[p, b2, pl.ds(LOW, high), :], f2.at[p, pl.ds(LOW, high), :], us.at[p, 5], ur.at[p, 5], dev(1 - axis, -1)
        ).start()

    def stage7(p):
        axis = p % 2
        bp, bm = pos_of(1 - axis, 1), pos_of(1 - axis, -1)
        t2[p, 0, LOW:, :] = m2[p, bp, LOW:, :]
        t2[p, 1, :LOW, :] = m2[p, bm, :LOW, :]
        f2d(p, 4, 0, LOW, sib).wait_recv()
        t2[p, 0, :LOW, :] = (m2[p, bp, :LOW, :].astype(F32) + f2[p, :LOW, :].astype(F32)).astype(BF16)
        t2d(p, 0, dev(1 - axis, 1)).start()
        f2d(p, 5, LOW, high, sib).wait_recv()
        t2[p, 1, LOW:, :] = (m2[p, bm, LOW:, :].astype(F32) + f2[p, LOW:, :].astype(F32)).astype(BF16)
        t2d(p, 1, dev(1 - axis, -1)).start()

    bflat = bbuf.reshape(place.shape[0], HD)

    def stage8(p):
        j, axis = ORDER[p], p % 2
        t2d(p, 0, sib).wait_recv()
        t2d(p, 1, sib).wait_recv()
        bflat[pl.ds(j * size, size), :] = (
            m2[p, pos_of(1 - axis, 0)].astype(F32) + r2[p, 0].astype(F32) + r2[p, 1].astype(F32)
        ).astype(BF16)
        for i in range(nz // CHUNKS):
            rel = j * (nz // CHUNKS) + i
            for core in range(2):
                t = chip(rel - nz // 2) * 2 + core
                a = bbuf.at[rel * 2 + core]
                if rel == nz // 2:
                    if core == 0:
                        pltpu.make_async_copy(bbuf.at[nz + c], bk.at[w], er.at[w]).start()
                        rcopy(bbuf.at[nz + 1 - c], bk.at[w], es.at[nz + 1 - c], er.at[w], sib).start()
                else:
                    rcopy(a, bk.at[w], es.at[rel * 2 + core], er.at[w], (t, n)).start()

    def drain_pipe():
        def sent_b(d, _):
            t = lax.rem(nz + c + d, nw)
            rcopy(bbuf.at[t], bk.at[w], es.at[t], er.at[w], sib).wait_send()
            return 0

        lax.fori_loop(1, nw, sent_b, 0)
        for p in range(CHUNKS):
            for slot in range(20):
                half = 0 if slot < 2 or slot % 4 < 2 else slot % 4 - 1
                hop(p, slot, 0, 0, half, sib).wait_send()
            f1d(p, 0, 0, LOW, sib).wait_send()
            f1d(p, 1, LOW, high, sib).wait_send()
            f2d(p, 4, 0, LOW, sib).wait_send()
            f2d(p, 5, LOW, high, sib).wait_send()
            for k in range(2):
                t1d(p, k, sib).wait_send()
                t2d(p, k, sib).wait_send()

    stages = (stage0, stage1, stage2, stage3, stage4, stage5, stage6, stage7, stage8)
    for t in range(CHUNKS + len(stages) - 1):
        for k in reversed(range(len(stages))):
            if 0 <= t - k < CHUNKS:
                stages[k](t - k)
        if t == 3:
            fill_router()

    def wait_b(d, _):
        t = lax.rem(w + d, nw)
        rcopy(bk.at[t], bk.at[t], es.at[t], er.at[t], sib).wait_recv()
        return 0

    lax.fori_loop(0, nw, wait_b, 0)
    moe = lax.dot_general(
        mix[...], bk.reshape(place.shape[0], HD)[...].astype(F32), DIMS0,
        precision=lax.Precision.HIGHEST, preferred_element_type=F32,
    )
    layer_out[...] = (mx[n].astype(F32) + moe).astype(BF16)

    drain_ring()
    drain_out()
    drain_plane()
    drain_dispatch()
    drain_pipe()


def body(
    hidden, attn_gain, expert_gain, query_weight, key_weight, value_weight, output_weight, router_weight,
    gate_weight, up_weight, down_weight, prefix_keys, prefix_values, cache_keys, cache_values, parents,
    cache_lengths, group_ids, expert_ids, accepted,
):
    tok, width = hidden.shape
    nn = lax.axis_size("narrow")
    nw = lax.axis_size("wide")
    nz = nw // 2
    rows = nw * gate_weight.shape[0] * CAP
    size = rows // CHUNKS
    cache = cache_keys.shape[1]
    vm = pl.BlockSpec(memory_space=pltpu.VMEM)
    sm = pl.BlockSpec(memory_space=pltpu.SMEM)
    hbm = pl.BlockSpec(memory_space=pl.ANY)
    dma = pltpu.SemaphoreType.DMA

    def v(*shape, t=BF16):
        return pltpu.VMEM(shape, t)

    pair = rows // nw // 2
    fw = gate_weight.shape[2]
    scratch = [
        v(tok, width), v(E, width), v(4 * fw, width), v(2 * fw, width), v(cache, HD), v(cache, HD),
        v(*prefix_keys.shape), v(*prefix_values.shape), v(tok, 3 * HD, t=F32),
        v(tok, width), v(nz, 2, 3, 64, HD), v(nz, 2, 64, HD), v(nw, 16, HD), v(nw, 16, HD),
        v(tok, HD), v(tok, HD), v(tok, HD), v(tok, cache, t=F32), v(tok, tok, t=F32), v(tok, tok, t=F32),
        v(cache, tok), v(nn, tok, HD), v(nn, tok, HD), v(nn, tok, HD),
        v(expert_ids.shape[1], tok, t=jnp.int32), v(rows, tok), v(rows, tok, t=F32),
        v(nw, pair, 2, HD), v(nw, pair, 2, HD), v(NY, NX, rows, HD), v(NY, NX, rows, HD),
        v(CHUNKS, 2, 4, size, HD), v(CHUNKS, 4, size, HD), v(CHUNKS, 2, 4, size, HD), v(CHUNKS, 4, size, HD),
        v(CHUNKS, 2, size, HD), v(CHUNKS, size, HD), v(CHUNKS, 2, size, HD), v(nw, pair, 2, HD), v(nw, pair, 2, HD),
        dma((16,)), dma((nz // 2, 2)), dma((nz // 2, 2)), dma((nz, 2)), dma((nz, 2)),
        dma((nz // 2,)), dma((nz // 2,)), dma((nz + 1,)), dma((nz + 1,)), dma((nw,)), dma((nw,)),
        dma((nn,)), dma((nn,)), dma((nn,)), dma((nn,)), dma((nw,)), dma((nw,)),
        dma((CHUNKS, 20)), dma((CHUNKS, 20)), dma((CHUNKS, 8)), dma((CHUNKS, 8)), dma((nw,)), dma((nw,)),
    ]
    return pl.pallas_call(
        layer_kernel,
        out_shape=(
            jax.ShapeDtypeStruct((tok, HD), BF16),
            jax.ShapeDtypeStruct(cache_keys.shape, BF16),
            jax.ShapeDtypeStruct(cache_values.shape, BF16),
        ),
        in_specs=[sm, sm] + [vm] * 5 + [hbm] * 13,
        out_specs=(vm, vm, vm),
        scratch_shapes=scratch,
        compiler_params=pltpu.CompilerParams(
            collective_id=0, has_side_effects=True, vmem_limit_bytes=60 * 1024 * 1024
        ),
        name="layer",
    )(
        cache_lengths, accepted, attn_gain[None], expert_gain[None], parents, group_ids[None], expert_ids.T,
        hidden, query_weight, key_weight, value_weight, output_weight, router_weight.T,
        jnp.swapaxes(gate_weight, 1, 2), jnp.swapaxes(up_weight, 1, 2), down_weight,
        prefix_keys, prefix_values, cache_keys, cache_values,
    )


def solution(mesh):
    in_specs = (
        P("wide", None),
        P(),
        P(),
        P("wide", "narrow"),
        P("wide", "narrow"),
        P("wide", "narrow"),
        P("wide", "narrow"),
        P(),
        P("wide", None, "narrow"),
        P("wide", None, "narrow"),
        P("wide", "narrow", None),
        P("wide", None, "narrow"),
        P("wide", None, "narrow"),
        P("wide", None, "narrow"),
        P("wide", None, "narrow"),
        P("wide", None),
        P("wide"),
        P(),
        P("wide", None),
        P("wide"),
    )
    out_specs = (P("wide", "narrow"), P("wide", None, "narrow"), P("wide", None, "narrow"))
    return jax.shard_map(body, mesh=mesh, in_specs=in_specs, out_specs=out_specs, check_vma=False)
```

```python
import math

import jax
import jax.numpy as jnp
from jax import lax
from jax.experimental import pallas as pl
from jax.experimental.pallas import tpu as pltpu
from jax.sharding import PartitionSpec as P

HD = 128
E = 64
SINK = 4
WIN = 512
CAP = 9
NX = 4
NY = 4
MESH = pl.DeviceIdType.MESH
F32 = jnp.float32
BF16 = jnp.bfloat16

norm_eps = 1e-06


def rms_scale(rows, row_gain):
    widened = rows.astype(F32)
    power_mean = jnp.mean(widened * widened, axis=-1, keepdims=True)
    return (widened * lax.rsqrt(power_mean + norm_eps) * row_gain).astype(BF16)


DIMS0 = (((0,), (0,)), ((), ()))
DIMS1 = (((1,), (1,)), ((), ()))
CHUNKS = 4
ORDER = (2, 1, 3, 0)
LOW = 80
NEG = -1e30


def rcopy(src, dst, ssem, rsem, dev):
    return pltpu.make_async_remote_copy(
        src_ref=src, dst_ref=dst, send_sem=ssem, recv_sem=rsem, device_id=dev, device_id_type=MESH
    )


def iota(shape, dim):
    return lax.broadcasted_iota(jnp.int32, shape, dim)


def mm(a, b, dims=(((1,), (0,)), ((), ()))):
    return lax.dot_general(a, b, dims, preferred_element_type=F32)


def layer_kernel(
    lens, acc_node, attn_gain, expert_gain, parents, groups, ids,
    hidden_in, q_in, k_in, v_in, o_in, router_in, gate, up, down, pk_in, pv_in, ck_in, cv_in,
    layer_out, new_k, new_v,
    hidden, router, wgt, dn, cache_k, cache_v, pk, pv, proj,
    normed, g, go, ps, pr, qs, ks, vs, cs, ts, anc, put, part, rbuf, mx, tgt, place, mix,
    dbuf, r, xs, src, r1, f1, t1, m2, r2, f2, t2, bbuf, bk,
    ls, rs, rr, fs, fr, os, orr, ofs, ofr, pss, psr, s1, r1s, s2, r2s, ds, dr, ss, rrs, us, ur, es, er,
):
    nz, nn, nw = g.shape[0], part.shape[0], pr.shape[0]
    tok = hidden.shape[0]
    w = lax.axis_index("wide")
    n = lax.axis_index("narrow")
    z = w // 2
    c = lax.rem(w, 2)
    y = n // NX
    x = lax.rem(n, NX)
    sg = 1 - 2 * c
    sib_w = w + sg
    sib = (sib_w, n)

    def chip(off):
        return lax.rem(z + off + nz, nz)

    nxt = (chip(sg) * 2 + c, n)

    barrier = pltpu.get_barrier_semaphore()
    for t in (sib, (chip(1) * 2 + c, n), (chip(nz - 1) * 2 + c, n)):
        pl.semaphore_signal(barrier, inc=1, device_id=t, device_id_type=MESH)

    def greet(d, _):
        pl.semaphore_signal(barrier, inc=1, device_id=(w, lax.rem(n + d, nn)), device_id_type=MESH)
        return 0

    lax.fori_loop(1, nn, greet, 0)
    fw = gate.shape[1]
    moves = (
        (q_in, g.at[z, c, 0]), (k_in, g.at[z, c, 1]), (v_in, g.at[z, c, 2]), (o_in, go.at[z, c]),
        (hidden_in, hidden), (pk_in, pk), (pv_in, pv), (ck_in.at[0], cache_k), (cv_in.at[0], cache_v),
        (gate.at[0], wgt.at[pl.ds(0, fw), :]), (gate.at[1], wgt.at[pl.ds(fw, fw), :]),
        (up.at[0], wgt.at[pl.ds(2 * fw, fw), :]), (up.at[1], wgt.at[pl.ds(3 * fw, fw), :]),
        (down.at[0], dn.at[pl.ds(0, fw), :]), (down.at[1], dn.at[pl.ds(fw, fw), :]), (router_in, router),
    )
    local = [pltpu.make_async_copy(a, b, ls.at[i]) for i, (a, b) in enumerate(moves)]
    for cp in local:
        cp.start()
    for cp in local[:4]:
        cp.wait()
    pl.semaphore_wait(barrier, nn + 2)

    def ring(s, sub):
        ref = g.at[chip(-sg * s), sub]
        return rcopy(ref, ref, rs.at[s, sub], rr.at[s, sub], nxt)

    def got(s, sub):
        ref = g.at[chip(-sg * (s + 1)), sub]
        return rcopy(ref, ref, rs.at[s, sub], rr.at[s, sub], nxt)

    def side(chip_id, sub):
        ref = g.at[chip_id, sub]
        return rcopy(ref, ref, fs.at[chip_id, sub], fr.at[chip_id, sub], sib)

    side(z, c).start()
    oref = go.at[z, c]
    o_side = rcopy(oref, oref, ofs.at[nz], ofr.at[nz], sib)
    o_side.start()
    ring(0, c).start()
    osib = go.at[z, 1 - c]
    side(z, 1 - c).wait_recv()
    ring(0, 1 - c).start()

    def fill_norm():
        local[4].wait()
        hv = hidden[...].astype(F32)
        power = jnp.mean(hv * hv, axis=-1, keepdims=True)
        normed[...] = (hv * lax.rsqrt(power + norm_eps) * attn_gain[...]).astype(BF16)
        proj[...] = jnp.zeros_like(proj)

    def fill_prefix():
        local[5].wait()
        local[6].wait()
        rows, cols = nw * 16, 64
        it = iota((rows, nw), 0) // 16
        gid = jnp.sum(jnp.where(it == iota((rows, nw), 1), groups[...], 0), axis=1, keepdims=True)
        r_id = lax.rem(iota((rows, cols), 0), 16)
        c_id = iota((rows, cols), 1)
        same = lax.rem(c_id, 8) == gid
        one_k = (same & (c_id // 8 == r_id)).astype(F32).astype(BF16)
        one_v = (same & (c_id // 8 + 8 == r_id)).astype(F32).astype(BF16)
        picked = mm(one_k, pk[...].reshape(cols, HD)) + mm(one_v, pv[...].reshape(cols, HD))
        ps[...] = picked.astype(BF16).reshape(ps.shape)

    def fill_tree():
        size = parents.shape[1]
        a, b = iota((size, size), 0), iota((size, size), 1)
        eye = (a == b).astype(F32)
        up_t = jnp.maximum(eye, (parents[...] == a).astype(F32))
        for _ in range(6):
            m = up_t.astype(BF16)
            up_t = (mm(m, m) > 0.5).astype(F32)
        depth = jnp.sum(up_t, axis=0, keepdims=True) - 1.0
        full = mm(up_t.astype(BF16), eye.astype(BF16), DIMS0)
        anc[...] = full
        on_path = jnp.sum(jnp.where(a == acc_node[0], full, 0.0), axis=0, keepdims=True)
        slot = jnp.where(on_path > 0.5, lens[0] + depth.astype(jnp.int32), put.shape[0])
        put[...] = (iota(put.shape, 0) == slot).astype(F32).astype(BF16)

    def fill_slots():
        a, b = iota((E, tok), 0), iota((E, tok), 1)
        named = jnp.zeros((E, tok), F32)
        for k in range(ids.shape[0]):
            named = named + (ids[k : k + 1, :] == a).astype(F32)
        earlier = mm(named.astype(BF16), (iota((tok, tok), 0) < iota((tok, tok), 1)).astype(F32).astype(BF16))
        hit = jnp.zeros(place.shape, F32)
        rows = iota(place.shape, 0)
        for k in range(ids.shape[0]):
            idk = ids[k : k + 1, :]
            rank = jnp.sum(jnp.where(idk == a, earlier, 0.0), axis=0, keepdims=True)
            t = idk * CAP + rank.astype(jnp.int32)
            tgt[k : k + 1, :] = t
            hit = hit + (rows == t).astype(F32)
        place[...] = hit.astype(BF16)

    def oring(s):
        k = chip(-sg * s)
        ref = go.at[k] if s < nz // 2 - 1 else go.at[k, c]
        return rcopy(ref, ref, os.at[s], orr.at[s], nxt)

    def ogot(s):
        k = chip(-sg * (s + 1))
        ref = go.at[k] if s < nz // 2 - 1 else go.at[k, c]
        return rcopy(ref, ref, os.at[s], orr.at[s], nxt)

    def oside(s, mine):
        k = chip(-sg * s) if mine else chip(sg * s)
        ref = go.at[k] if s < nz // 2 else go.at[k, c if mine else 1 - c]
        return rcopy(ref, ref, ofs.at[k], ofr.at[k], sib)

    def send_prefix(k):
        for core in range(2):
            t = k * 2 + core
            rcopy(ps.at[t], pr.at[w], pss.at[t], psr.at[w], (t, n)).start()

    def project(k):
        cols = pl.ds(pl.multiple_of(k * HD, HD), HD)
        a = normed[:, cols]
        for i in range(3):
            b = jnp.concatenate([g[k, 0, i], g[k, 1, i]], axis=0)
            proj[:, i * HD : (i + 1) * HD] += mm(a, b)

    half = nz // 2
    rcopy(osib, osib, ofs.at[nz], ofr.at[nz], sib).wait_recv()
    oring(0).start()
    cp_own = pltpu.make_async_copy(ps.at[w], pr.at[w], psr.at[w])

    def seen(k):
        for sub in range(2):
            side(k, sub).wait_recv()

    for s in range(1, half + 1):
        for i in range(2 if s < half else 1):
            sub = c if i == 0 else 1 - c
            got(s - 1, sub).wait_recv()
            if s < half - 1 or (s < half and i == 0):
                ring(s, sub).start()
            side(chip(-sg * s), sub).start()
        if s == 1:
            fill_norm()
        if s == 2:
            fill_prefix()
            cp_own.start()
            rcopy(ps.at[sib_w], pr.at[w], pss.at[sib_w], psr.at[w], sib).start()
            send_prefix(chip(-sg))
        ogot(s - 1).wait_recv()
        if s < half:
            oring(s).start()
        oside(s, True).start()
        if s >= 2:
            if s < half:
                send_prefix(chip(-sg * s))
            seen(chip(sg * (s - 1)))
            send_prefix(chip(sg * (s - 1)))
            project(chip(sg * (s - 1)))
            project(chip(-sg * (s - 1)))
        if s == 3:
            project(z)
            fill_tree()
        if s == 4:
            fill_slots()
    side(chip(half), 1 - c).wait_recv()
    send_prefix(chip(half))
    project(chip(half))
    for i, ref in enumerate((qs, ks, vs)):
        ref[...] = proj[:, i * HD : (i + 1) * HD].astype(BF16)

    def drain_ring():
        for s in range(nz // 2):
            for i in range(2):
                if s < nz // 2 - 1 or i == 0:
                    ring(s, c if i == 0 else 1 - c).wait_send()
        side(z, c).wait_send()
        o_side.wait_send()
        for s in range(1, nz // 2):
            for sub in range(2):
                side(chip(-sg * s), sub).wait_send()
        side(chip(nz // 2), c).wait_send()

    scale = 1.0 / math.sqrt(HD)
    local[7].wait()
    pos = iota(cs.shape, 1)
    ok = (pos < lens[0]) & ((pos < SINK) | (pos >= lens[0] - WIN))
    cs[...] = jnp.where(ok, mm(qs[...], cache_k[...], DIMS1) * scale, NEG)
    ts[...] = jnp.where(anc[...] > 0.5, mm(qs[...], ks[...], DIMS1) * scale, NEG)

    def compact(fresh, cache, out):
        moved = mm(put[...], fresh[...])
        written = jnp.sum(put[...].astype(F32), axis=1, keepdims=True) > 0.5
        out[0] = jnp.where(written, moved.astype(BF16), cache[...])

    cp_own.wait()

    def pwait(d, _):
        t = lax.rem(w + d, nw)
        rcopy(pr.at[t], pr.at[t], pss.at[t], psr.at[t], sib).wait_recv()
        return 0

    lax.fori_loop(1, nw, pwait, 0)
    def drain_out():
        for s in range(nz // 2):
            oring(s).wait_send()
        for s in range(1, nz // 2 + 1):
            oside(s, True).wait_send()

        def sent_p(d, _):
            t = lax.rem(w + d, nw)
            rcopy(ps.at[t], pr.at[w], pss.at[t], psr.at[w], sib).wait_send()
            return 0

        lax.fori_loop(1, nw, sent_p, 0)

    prows = pr[...].reshape(-1, HD)
    is_key = lax.rem(iota((tok, nw * 16), 1), 16) < 8
    psc = jnp.where(is_key, mm(qs[...], prows, DIMS1) * scale, NEG)
    csc, tsc = cs[...], ts[...]
    top = jnp.maximum(
        jnp.max(psc, axis=1, keepdims=True),
        jnp.maximum(jnp.max(csc, axis=1, keepdims=True), jnp.max(tsc, axis=1, keepdims=True)),
    )
    pw = jnp.where(is_key, jnp.exp(psc - top), 0.0)
    pos = iota(cs.shape, 1)
    ok = (pos < lens[0]) & ((pos < SINK) | (pos >= lens[0] - WIN))
    cw = jnp.where(ok, jnp.exp(csc - top), 0.0)
    tw = jnp.where(anc[...] > 0.5, jnp.exp(tsc - top), 0.0)
    total = (
        jnp.sum(pw, axis=1, keepdims=True) + jnp.sum(cw, axis=1, keepdims=True) + jnp.sum(tw, axis=1, keepdims=True)
    )
    local[8].wait()
    weighted = (
        mm(pltpu.roll(pw, 8, 1).astype(BF16), prows)
        + mm(cw.astype(BF16), cache_v[...])
        + mm(tw.astype(BF16), vs[...])
    )
    attended = (weighted / total).astype(BF16)
    for s in range(1, nz // 2 + 1):
        oside(s, False).wait_recv()
    for i in range(4):
        four = go[i * 4 : i * 4 + 4].reshape(512, HD)
        terms = mm(attended, four, DIMS1)
        for j in range(4):
            part[i * 4 + j] = terms[:, j * HD : (j + 1) * HD].astype(BF16)

    def send1(d, _):
        t = lax.rem(n + d, nn)
        rcopy(part.at[t], rbuf.at[n], s1.at[t], r1s.at[n], (w, t)).start()
        return 0

    lax.fori_loop(1, nn, send1, 0)
    col = pl.multiple_of(n * HD, HD)

    def add1(d, acc):
        t = lax.rem(n + d, nn)
        rcopy(rbuf.at[t], rbuf.at[t], s1.at[t], r1s.at[t], (w, t)).wait_recv()
        return acc + rbuf[t].astype(F32)

    summed = lax.fori_loop(1, nn, add1, part[n].astype(F32))
    mixed = (hidden[:, pl.ds(col, HD)].astype(F32) + summed).astype(BF16)
    mx[n] = mixed
    slots = mm(place[...], mixed)
    dflat = dbuf.reshape(place.shape[0], HD)
    dflat[...] = slots.astype(BF16)


    def drain_plane():
        def sent_n(d, _):
            t = lax.rem(n + d, nn)
            rcopy(part.at[t], rbuf.at[n], s1.at[t], r1s.at[n], sib).wait_send()
            rcopy(mx.at[n], mx.at[n], s2.at[t], r2s.at[n], sib).wait_send()
            return 0

        lax.fori_loop(1, nn, sent_n, 0)

    def slot_of(dz):
        return lax.rem(nz + nz // 2 - dz, nz) * 2 + c

    def send_d(dz, core):
        t = chip(dz) * 2 + core
        rcopy(dbuf.at[t], r.at[slot_of(dz)], ds.at[t], dr.at[slot_of(dz)], (t, n)).start()

    cp_d = pltpu.make_async_copy(dbuf.at[w], r.at[nz + c], dr.at[nz + c])
    cp_d.start()
    send_d(0, 1 - c)
    for k in range(1, nz // 2):
        for dz in (k, -k):
            for core in range(2):
                send_d(dz, core)
    for core in range(2):
        send_d(nz // 2, core)
    def send2(d, _):
        t = lax.rem(n + d, nn)
        rcopy(mx.at[n], mx.at[n], s2.at[t], r2s.at[n], (w, t)).start()
        return 0

    lax.fori_loop(1, nn, send2, 0)
    compact(ks, cache_k, new_k)
    compact(vs, cache_v, new_v)

    def wait2(d, _):
        t = lax.rem(n + d, nn)
        rcopy(mx.at[t], mx.at[t], s2.at[t], r2s.at[t], (w, t)).wait_recv()
        return 0

    def fill_router():
        lax.fori_loop(1, nn, wait2, 0)
        local[15].wait()
        power = jnp.zeros((tok, 1), F32)
        for t in range(nn):
            m = mx[t].astype(F32)
            power = power + jnp.sum(m * m, axis=1, keepdims=True)
        inv = lax.rsqrt(power / (nn * HD) + norm_eps)
        logits = jnp.zeros((E, tok), F32)
        for t in range(nn):
            row = (mx[t].astype(F32) * inv * expert_gain[:, t * HD : (t + 1) * HD]).astype(BF16)
            logits = logits + mm(router[:, t * HD : (t + 1) * HD], row, DIMS1)
        a = iota((E, tok), 0)
        picks = [
            jnp.sum(jnp.where(ids[k : k + 1, :] == a, logits, 0.0), axis=0, keepdims=True)
            for k in range(ids.shape[0])
        ]
        best = picks[0]
        for p in picks[1:]:
            best = jnp.maximum(best, p)
        exps = [jnp.exp(p - best) for p in picks]
        den = exps[0]
        for e in exps[1:]:
            den = den + e
        rows = iota(mix.shape, 0)
        m = jnp.zeros(mix.shape, F32)
        for k, e in enumerate(exps):
            m = m + jnp.where(rows == tgt[k : k + 1, :], e / den, 0.0)
        mix[...] = m

    def drain_dispatch():
        def sent_d(d, _):
            t = lax.rem(w + d, nw)
            rcopy(dbuf.at[t], r.at[0], ds.at[t], dr.at[0], sib).wait_send()
            return 0

        lax.fori_loop(1, nw, sent_d, 0)

    rflat = r.reshape(place.shape[0], HD)
    size = place.shape[0] // CHUNKS
    high = size - LOW

    def dev(axis, off):
        if axis == 0:
            return (w, y * NX + lax.rem(x + off + NX, NX))
        return (w, lax.rem(y + off + NY, NY) * NX + x)

    def pos_of(axis, off):
        if axis == 0:
            return lax.rem(x + off + NX, NX)
        return lax.rem(y + off + NY, NY)

    def xref(axis, b, o, lo, ln):
        if axis == 0:
            return xs.at[o, b, pl.ds(lo, ln), :]
        return xs.at[b, o, pl.ds(lo, ln), :]

    def hop(p, slot, b_off, o_off, half, to):
        axis, lo = p % 2, ORDER[p] * size
        lo, ln = {0: (lo, size), 1: (lo, LOW), 2: (lo + LOW, high)}[half]
        ref = xref(axis, pos_of(axis, b_off), pos_of(1 - axis, o_off), lo, ln)
        return rcopy(ref, ref, ss.at[p, slot], rrs.at[p, slot], to)

    def stage0(p):
        j, axis = ORDER[p], p % 2
        for i in range(nw // CHUNKS):
            ref = r.at[j * (nw // CHUNKS) + i]
            rcopy(ref, ref, ds.at[0], dr.at[j * (nw // CHUNKS) + i], sib).wait_recv()
        xs[y, x, pl.ds(j * size, size), :] = rflat[pl.ds(j * size, size), :]
        hop(p, 0, 0, 0, 0, dev(axis, 1)).start()
        hop(p, 1, 0, 0, 0, dev(axis, -1)).start()
        hop(p, 4, 0, 0, 0, dev(1 - axis, 1)).start()
        hop(p, 5, 0, 0, 0, dev(1 - axis, -1)).start()

    def stage1(p):
        axis = p % 2
        for slot, off, half in ((0, -1, 1), (1, 1, 2)):
            hop(p, slot, off, 0, 0, sib).wait_recv()
            hop(p, slot + 2, off, 0, half, dev(axis, -off)).start()
            hop(p, 8 + 4 * slot, off, 0, 0, dev(1 - axis, 1)).start()
            hop(p, 9 + 4 * slot, off, 0, 0, dev(1 - axis, -1)).start()

    def second(p, base, b_off):
        axis = p % 2
        hop(p, base, b_off, -1, 0, sib).wait_recv()
        hop(p, base + 2, b_off, -1, 1, dev(1 - axis, 1)).start()
        hop(p, base + 1, b_off, 1, 0, sib).wait_recv()
        hop(p, base + 3, b_off, 1, 2, dev(1 - axis, -1)).start()

    def stage2(p):
        axis = p % 2
        second(p, 4, 0)
        hop(p, 2, 2, 0, 1, sib).wait_recv()
        hop(p, 3, 2, 0, 2, sib).wait_recv()
        hop(p, 16, 2, 0, 0, dev(1 - axis, 1)).start()
        hop(p, 17, 2, 0, 0, dev(1 - axis, -1)).start()
        second(p, 8, -1)
        second(p, 12, 1)

    def stage3(p):
        second(p, 16, 2)

    def sref(axis, b, lo, ln):
        if axis == 0:
            return src.at[:, b, pl.ds(lo, ln), :]
        return src.at[b, :, pl.ds(lo, ln), :]

    def val(axis, b, lo, ln):
        return sref(axis, b, lo, ln)[...].astype(F32)

    def f1d(p, slot, lo, ln, to):
        ref = f1.at[p, :, pl.ds(lo, ln), :]
        return rcopy(ref, ref, us.at[p, slot], ur.at[p, slot], to)

    def f2d(p, slot, lo, ln, to):
        ref = f2.at[p, pl.ds(lo, ln), :]
        return rcopy(ref, ref, us.at[p, slot], ur.at[p, slot], to)

    def stage4(p):
        axis, lo = p % 2, ORDER[p] * size
        for base, b_off in ((4, 0), (8, -1), (12, 1), (16, 2)):
            hop(p, base + 2, b_off, 2, 1, sib).wait_recv()
            hop(p, base + 3, b_off, 2, 2, sib).wait_recv()
        if p == 0:
            for cp in local[9:15]:
                cp.wait()
        power = jnp.zeros((size, 1), F32)
        for t in range(nn):
            m = xs[t // NX, t % NX, lo : lo + size, :].astype(F32)
            power = power + jnp.sum(m * m, axis=1, keepdims=True)
        inv = lax.rsqrt(power / (nn * HD) + norm_eps)
        units = jnp.zeros((size, 4 * fw), F32)
        for t in range(nn):
            m = xs[t // NX, t % NX, lo : lo + size, :].astype(F32)
            m = (m * inv * expert_gain[:, t * HD : (t + 1) * HD]).astype(BF16)
            units = units + mm(m, wgt[:, t * HD : (t + 1) * HD], DIMS1)
        gt = units[:, : 2 * fw]
        act = gt / (1.0 + jnp.exp(-gt)) * units[:, 2 * fw :]
        row = lax.rem(iota(act.shape, 0), 2 * CAP)
        keep = (row >= CAP) == (iota(act.shape, 1) >= fw)
        act = jnp.where(keep, act, 0.0).astype(BF16)
        for t in range(nn):
            src[t // NX, t % NX, lo : lo + size, :] = mm(act, dn[:, t * HD : (t + 1) * HD]).astype(BF16)
        b2 = pos_of(axis, 2)
        rcopy(sref(axis, b2, lo, LOW), f1.at[p, :, pl.ds(0, LOW), :], us.at[p, 0], ur.at[p, 0], dev(axis, 1)).start()
        rcopy(
            sref(axis, b2, lo + LOW, high), f1.at[p, :, pl.ds(LOW, high), :], us.at[p, 1], ur.at[p, 1], dev(axis, -1)
        ).start()

    def t1d(p, k, to):
        return rcopy(t1.at[p, k], r1.at[p, k], us.at[p, 2 + k], ur.at[p, 2 + k], to)

    def t2d(p, k, to):
        return rcopy(t2.at[p, k], r2.at[p, k], us.at[p, 6 + k], ur.at[p, 6 + k], to)

    def stage5(p):
        axis, lo = p % 2, ORDER[p] * size
        bp, bm = pos_of(axis, 1), pos_of(axis, -1)
        t1[p, 0, :, LOW:, :] = sref(axis, bp, lo + LOW, high)[...]
        t1[p, 1, :, :LOW, :] = sref(axis, bm, lo, LOW)[...]
        f1d(p, 0, 0, LOW, sib).wait_recv()
        t1[p, 0, :, :LOW, :] = (val(axis, bp, lo, LOW) + f1[p, :, :LOW, :].astype(F32)).astype(BF16)
        t1d(p, 0, dev(axis, 1)).start()
        f1d(p, 1, LOW, high, sib).wait_recv()
        t1[p, 1, :, LOW:, :] = (val(axis, bm, lo + LOW, high) + f1[p, :, LOW:, :].astype(F32)).astype(BF16)
        t1d(p, 1, dev(axis, -1)).start()

    def stage6(p):
        axis, lo = p % 2, ORDER[p] * size
        t1d(p, 0, sib).wait_recv()
        t1d(p, 1, sib).wait_recv()
        m2[p] = (val(axis, pos_of(axis, 0), lo, size) + r1[p, 0].astype(F32) + r1[p, 1].astype(F32)).astype(BF16)
        b2 = pos_of(1 - axis, 2)
        rcopy(m2.at[p, b2, pl.ds(0, LOW), :], f2.at[p, pl.ds(0, LOW), :], us.at[p, 4], ur.at[p, 4], dev(1 - axis, 1)).start()
        rcopy(
            m2.at[p, b2, pl.ds(LOW, high), :], f2.at[p, pl.ds(LOW, high), :], us.at[p, 5], ur.at[p, 5], dev(1 - axis, -1)
        ).start()

    def stage7(p):
        axis = p % 2
        bp, bm = pos_of(1 - axis, 1), pos_of(1 - axis, -1)
        t2[p, 0, LOW:, :] = m2[p, bp, LOW:, :]
        t2[p, 1, :LOW, :] = m2[p, bm, :LOW, :]
        f2d(p, 4, 0, LOW, sib).wait_recv()
        t2[p, 0, :LOW, :] = (m2[p, bp, :LOW, :].astype(F32) + f2[p, :LOW, :].astype(F32)).astype(BF16)
        t2d(p, 0, dev(1 - axis, 1)).start()
        f2d(p, 5, LOW, high, sib).wait_recv()
        t2[p, 1, LOW:, :] = (m2[p, bm, LOW:, :].astype(F32) + f2[p, LOW:, :].astype(F32)).astype(BF16)
        t2d(p, 1, dev(1 - axis, -1)).start()

    bflat = bbuf.reshape(place.shape[0], HD)

    def stage8(p):
        j, axis = ORDER[p], p % 2
        t2d(p, 0, sib).wait_recv()
        t2d(p, 1, sib).wait_recv()
        bflat[pl.ds(j * size, size), :] = (
            m2[p, pos_of(1 - axis, 0)].astype(F32) + r2[p, 0].astype(F32) + r2[p, 1].astype(F32)
        ).astype(BF16)
        for i in range(nz // CHUNKS):
            rel = j * (nz // CHUNKS) + i
            for core in range(2):
                t = chip(rel - nz // 2) * 2 + core
                a = bbuf.at[rel * 2 + core]
                if rel == nz // 2:
                    if core == 0:
                        pltpu.make_async_copy(bbuf.at[nz + c], bk.at[w], er.at[w]).start()
                        rcopy(bbuf.at[nz + 1 - c], bk.at[w], es.at[nz + 1 - c], er.at[w], sib).start()
                else:
                    rcopy(a, bk.at[w], es.at[rel * 2 + core], er.at[w], (t, n)).start()

    def drain_pipe():
        def sent_b(d, _):
            t = lax.rem(nz + c + d, nw)
            rcopy(bbuf.at[t], bk.at[w], es.at[t], er.at[w], sib).wait_send()
            return 0

        lax.fori_loop(1, nw, sent_b, 0)
        for p in range(CHUNKS):
            for slot in range(20):
                half = 0 if slot < 2 or slot % 4 < 2 else slot % 4 - 1
                hop(p, slot, 0, 0, half, sib).wait_send()
            f1d(p, 0, 0, LOW, sib).wait_send()
            f1d(p, 1, LOW, high, sib).wait_send()
            f2d(p, 4, 0, LOW, sib).wait_send()
            f2d(p, 5, LOW, high, sib).wait_send()
            for k in range(2):
                t1d(p, k, sib).wait_send()
                t2d(p, k, sib).wait_send()

    stages = (stage0, stage1, stage2, stage3, stage4, stage5, stage6, stage7, stage8)
    for k in range(len(stages)):
        for p in range(CHUNKS):
            stages[k](p)
        if k == 1:
            fill_router()

    def wait_b(d, _):
        t = lax.rem(w + d, nw)
        rcopy(bk.at[t], bk.at[t], es.at[t], er.at[t], sib).wait_recv()
        return 0

    lax.fori_loop(0, nw, wait_b, 0)
    moe = lax.dot_general(
        mix[...], bk.reshape(place.shape[0], HD)[...].astype(F32), DIMS0,
        precision=lax.Precision.HIGHEST, preferred_element_type=F32,
    )
    layer_out[...] = (mx[n].astype(F32) + moe).astype(BF16)

    drain_ring()
    drain_out()
    drain_plane()
    drain_dispatch()
    drain_pipe()


def body(
    hidden, attn_gain, expert_gain, query_weight, key_weight, value_weight, output_weight, router_weight,
    gate_weight, up_weight, down_weight, prefix_keys, prefix_values, cache_keys, cache_values, parents,
    cache_lengths, group_ids, expert_ids, accepted,
):
    tok, width = hidden.shape
    nn = lax.axis_size("narrow")
    nw = lax.axis_size("wide")
    nz = nw // 2
    rows = nw * gate_weight.shape[0] * CAP
    size = rows // CHUNKS
    cache = cache_keys.shape[1]
    vm = pl.BlockSpec(memory_space=pltpu.VMEM)
    sm = pl.BlockSpec(memory_space=pltpu.SMEM)
    hbm = pl.BlockSpec(memory_space=pl.ANY)
    dma = pltpu.SemaphoreType.DMA

    def v(*shape, t=BF16):
        return pltpu.VMEM(shape, t)

    pair = rows // nw // 2
    fw = gate_weight.shape[2]
    scratch = [
        v(tok, width), v(E, width), v(4 * fw, width), v(2 * fw, width), v(cache, HD), v(cache, HD),
        v(*prefix_keys.shape), v(*prefix_values.shape), v(tok, 3 * HD, t=F32),
        v(tok, width), v(nz, 2, 3, 64, HD), v(nz, 2, 64, HD), v(nw, 16, HD), v(nw, 16, HD),
        v(tok, HD), v(tok, HD), v(tok, HD), v(tok, cache, t=F32), v(tok, tok, t=F32), v(tok, tok, t=F32),
        v(cache, tok), v(nn, tok, HD), v(nn, tok, HD), v(nn, tok, HD),
        v(expert_ids.shape[1], tok, t=jnp.int32), v(rows, tok), v(rows, tok, t=F32),
        v(nw, pair, 2, HD), v(nw, pair, 2, HD), v(NY, NX, rows, HD), v(NY, NX, rows, HD),
        v(CHUNKS, 2, 4, size, HD), v(CHUNKS, 4, size, HD), v(CHUNKS, 2, 4, size, HD), v(CHUNKS, 4, size, HD),
        v(CHUNKS, 2, size, HD), v(CHUNKS, size, HD), v(CHUNKS, 2, size, HD), v(nw, pair, 2, HD), v(nw, pair, 2, HD),
        dma((16,)), dma((nz // 2, 2)), dma((nz // 2, 2)), dma((nz, 2)), dma((nz, 2)),
        dma((nz // 2,)), dma((nz // 2,)), dma((nz + 1,)), dma((nz + 1,)), dma((nw,)), dma((nw,)),
        dma((nn,)), dma((nn,)), dma((nn,)), dma((nn,)), dma((nw,)), dma((nw,)),
        dma((CHUNKS, 20)), dma((CHUNKS, 20)), dma((CHUNKS, 8)), dma((CHUNKS, 8)), dma((nw,)), dma((nw,)),
    ]
    return pl.pallas_call(
        layer_kernel,
        out_shape=(
            jax.ShapeDtypeStruct((tok, HD), BF16),
            jax.ShapeDtypeStruct(cache_keys.shape, BF16),
            jax.ShapeDtypeStruct(cache_values.shape, BF16),
        ),
        in_specs=[sm, sm] + [vm] * 5 + [hbm] * 13,
        out_specs=(vm, vm, vm),
        scratch_shapes=scratch,
        compiler_params=pltpu.CompilerParams(
            collective_id=0, has_side_effects=True, vmem_limit_bytes=60 * 1024 * 1024
        ),
        name="layer",
    )(
        cache_lengths, accepted, attn_gain[None], expert_gain[None], parents, group_ids[None], expert_ids.T,
        hidden, query_weight, key_weight, value_weight, output_weight, router_weight.T,
        jnp.swapaxes(gate_weight, 1, 2), jnp.swapaxes(up_weight, 1, 2), down_weight,
        prefix_keys, prefix_values, cache_keys, cache_values,
    )


def solution(mesh):
    in_specs = (
        P("wide", None),
        P(),
        P(),
        P("wide", "narrow"),
        P("wide", "narrow"),
        P("wide", "narrow"),
        P("wide", "narrow"),
        P(),
        P("wide", None, "narrow"),
        P("wide", None, "narrow"),
        P("wide", "narrow", None),
        P("wide", None, "narrow"),
        P("wide", None, "narrow"),
        P("wide", None, "narrow"),
        P("wide", None, "narrow"),
        P("wide", None),
        P("wide"),
        P(),
        P("wide", None),
        P("wide"),
    )
    out_specs = (P("wide", "narrow"), P("wide", None, "narrow"), P("wide", None, "narrow"))
    return jax.shard_map(body, mesh=mesh, in_specs=in_specs, out_specs=out_specs, check_vma=False)
```

```python
import math

import jax
import jax.numpy as jnp
from jax import lax
from jax.experimental import pallas as pl
from jax.experimental.pallas import tpu as pltpu
from jax.sharding import PartitionSpec as P

HD = 128
E = 64
SINK = 4
WIN = 512
CAP = 9
NX = 4
NY = 4
MESH = pl.DeviceIdType.MESH
F32 = jnp.float32
BF16 = jnp.bfloat16

norm_eps = 1e-06


def rms_scale(rows, row_gain):
    widened = rows.astype(F32)
    power_mean = jnp.mean(widened * widened, axis=-1, keepdims=True)
    return (widened * lax.rsqrt(power_mean + norm_eps) * row_gain).astype(BF16)


DIMS0 = (((0,), (0,)), ((), ()))
DIMS1 = (((1,), (1,)), ((), ()))
CHUNKS = 4
ORDER = (2, 1, 3, 0)
LOW = 80
NEG = -1e30


def rcopy(src, dst, ssem, rsem, dev):
    return pltpu.make_async_remote_copy(
        src_ref=src, dst_ref=dst, send_sem=ssem, recv_sem=rsem, device_id=dev, device_id_type=MESH
    )


def iota(shape, dim):
    return lax.broadcasted_iota(jnp.int32, shape, dim)


def mm(a, b, dims=(((1,), (0,)), ((), ()))):
    return lax.dot_general(a, b, dims, preferred_element_type=F32)


def layer_kernel(
    lens, acc_node, attn_gain, expert_gain, parents, groups, ids,
    hidden_in, q_in, k_in, v_in, o_in, router_in, gate, up, down, pk_in, pv_in, ck_in, cv_in,
    layer_out, new_k, new_v,
    hidden, router, wgt, dn, cache_k, cache_v, pk, pv, proj,
    normed, g, go, ps, pr, qs, ks, vs, cs, ts, anc, put, part, rbuf, mx, tgt, place, mix,
    dbuf, r, xs, src, r1, f1, t1, m2, r2, bbuf, bk,
    ls, rs, rr, fs, fr, os, orr, ofs, ofr, pss, psr, s1, r1s, s2, r2s, ds, dr, ss, rrs, us, ur, es, er,
):
    nz, nn, nw = g.shape[0], part.shape[0], pr.shape[0]
    tok = hidden.shape[0]
    w = lax.axis_index("wide")
    n = lax.axis_index("narrow")
    z = w // 2
    c = lax.rem(w, 2)
    y = n // NX
    x = lax.rem(n, NX)
    sg = 1 - 2 * c
    sib_w = w + sg
    sib = (sib_w, n)

    def chip(off):
        return lax.rem(z + off + nz, nz)

    nxt = (chip(sg) * 2 + c, n)

    barrier = pltpu.get_barrier_semaphore()
    for t in (sib, (chip(1) * 2 + c, n), (chip(nz - 1) * 2 + c, n)):
        pl.semaphore_signal(barrier, inc=1, device_id=t, device_id_type=MESH)

    def greet(d, _):
        pl.semaphore_signal(barrier, inc=1, device_id=(w, lax.rem(n + d, nn)), device_id_type=MESH)
        return 0

    lax.fori_loop(1, nn, greet, 0)
    fw = gate.shape[1]
    moves = (
        (q_in, g.at[z, c, 0]), (k_in, g.at[z, c, 1]), (v_in, g.at[z, c, 2]), (o_in, go.at[z, c]),
        (hidden_in, hidden), (pk_in, pk), (pv_in, pv), (ck_in.at[0], cache_k), (cv_in.at[0], cache_v),
        (gate.at[0], wgt.at[pl.ds(0, fw), :]), (gate.at[1], wgt.at[pl.ds(fw, fw), :]),
        (up.at[0], wgt.at[pl.ds(2 * fw, fw), :]), (up.at[1], wgt.at[pl.ds(3 * fw, fw), :]),
        (down.at[0], dn.at[pl.ds(0, fw), :]), (down.at[1], dn.at[pl.ds(fw, fw), :]), (router_in, router),
    )
    local = [pltpu.make_async_copy(a, b, ls.at[i]) for i, (a, b) in enumerate(moves)]
    for cp in local:
        cp.start()
    for cp in local[:4]:
        cp.wait()
    pl.semaphore_wait(barrier, nn + 2)

    def ring(s, sub):
        ref = g.at[chip(-sg * s), sub]
        return rcopy(ref, ref, rs.at[s, sub], rr.at[s, sub], nxt)

    def got(s, sub):
        ref = g.at[chip(-sg * (s + 1)), sub]
        return rcopy(ref, ref, rs.at[s, sub], rr.at[s, sub], nxt)

    def side(chip_id, sub):
        ref = g.at[chip_id, sub]
        return rcopy(ref, ref, fs.at[chip_id, sub], fr.at[chip_id, sub], sib)

    side(z, c).start()
    oref = go.at[z, c]
    o_side = rcopy(oref, oref, ofs.at[nz], ofr.at[nz], sib)
    o_side.start()
    ring(0, c).start()
    osib = go.at[z, 1 - c]
    side(z, 1 - c).wait_recv()
    ring(0, 1 - c).start()

    def fill_norm():
        local[4].wait()
        hv = hidden[...].astype(F32)
        power = jnp.mean(hv * hv, axis=-1, keepdims=True)
        normed[...] = (hv * lax.rsqrt(power + norm_eps) * attn_gain[...]).astype(BF16)
        proj[...] = jnp.zeros_like(proj)

    def fill_prefix():
        local[5].wait()
        local[6].wait()
        rows, cols = nw * 16, 64
        it = iota((rows, nw), 0) // 16
        gid = jnp.sum(jnp.where(it == iota((rows, nw), 1), groups[...], 0), axis=1, keepdims=True)
        r_id = lax.rem(iota((rows, cols), 0), 16)
        c_id = iota((rows, cols), 1)
        same = lax.rem(c_id, 8) == gid
        one_k = (same & (c_id // 8 == r_id)).astype(F32).astype(BF16)
        one_v = (same & (c_id // 8 + 8 == r_id)).astype(F32).astype(BF16)
        picked = mm(one_k, pk[...].reshape(cols, HD)) + mm(one_v, pv[...].reshape(cols, HD))
        ps[...] = picked.astype(BF16).reshape(ps.shape)

    def fill_tree():
        size = parents.shape[1]
        a, b = iota((size, size), 0), iota((size, size), 1)
        eye = (a == b).astype(F32)
        up_t = jnp.maximum(eye, (parents[...] == a).astype(F32))
        for _ in range(6):
            m = up_t.astype(BF16)
            up_t = (mm(m, m) > 0.5).astype(F32)
        depth = jnp.sum(up_t, axis=0, keepdims=True) - 1.0
        full = mm(up_t.astype(BF16), eye.astype(BF16), DIMS0)
        anc[...] = full
        on_path = jnp.sum(jnp.where(a == acc_node[0], full, 0.0), axis=0, keepdims=True)
        slot = jnp.where(on_path > 0.5, lens[0] + depth.astype(jnp.int32), put.shape[0])
        put[...] = (iota(put.shape, 0) == slot).astype(F32).astype(BF16)

    def fill_slots():
        a, b = iota((E, tok), 0), iota((E, tok), 1)
        named = jnp.zeros((E, tok), F32)
        for k in range(ids.shape[0]):
            named = named + (ids[k : k + 1, :] == a).astype(F32)
        earlier = mm(named.astype(BF16), (iota((tok, tok), 0) < iota((tok, tok), 1)).astype(F32).astype(BF16))
        hit = jnp.zeros(place.shape, F32)
        rows = iota(place.shape, 0)
        for k in range(ids.shape[0]):
            idk = ids[k : k + 1, :]
            rank = jnp.sum(jnp.where(idk == a, earlier, 0.0), axis=0, keepdims=True)
            t = idk * CAP + rank.astype(jnp.int32)
            tgt[k : k + 1, :] = t
            hit = hit + (rows == t).astype(F32)
        place[...] = hit.astype(BF16)

    def oring(s):
        k = chip(-sg * s)
        ref = go.at[k] if s < nz // 2 - 1 else go.at[k, c]
        return rcopy(ref, ref, os.at[s], orr.at[s], nxt)

    def ogot(s):
        k = chip(-sg * (s + 1))
        ref = go.at[k] if s < nz // 2 - 1 else go.at[k, c]
        return rcopy(ref, ref, os.at[s], orr.at[s], nxt)

    def oside(s, mine):
        k = chip(-sg * s) if mine else chip(sg * s)
        ref = go.at[k] if s < nz // 2 else go.at[k, c if mine else 1 - c]
        return rcopy(ref, ref, ofs.at[k], ofr.at[k], sib)

    def send_prefix(k):
        for core in range(2):
            t = k * 2 + core
            rcopy(ps.at[t], pr.at[w], pss.at[t], psr.at[w], (t, n)).start()

    def project(k):
        cols = pl.ds(pl.multiple_of(k * HD, HD), HD)
        a = normed[:, cols]
        for i in range(3):
            b = jnp.concatenate([g[k, 0, i], g[k, 1, i]], axis=0)
            proj[:, i * HD : (i + 1) * HD] += mm(a, b)

    half = nz // 2
    rcopy(osib, osib, ofs.at[nz], ofr.at[nz], sib).wait_recv()
    oring(0).start()
    cp_own = pltpu.make_async_copy(ps.at[w], pr.at[w], psr.at[w])

    def seen(k):
        for sub in range(2):
            side(k, sub).wait_recv()

    for s in range(1, half + 1):
        for i in range(2 if s < half else 1):
            sub = c if i == 0 else 1 - c
            got(s - 1, sub).wait_recv()
            if s < half - 1 or (s < half and i == 0):
                ring(s, sub).start()
            side(chip(-sg * s), sub).start()
        if s == 1:
            fill_norm()
        if s == 2:
            fill_prefix()
            cp_own.start()
            rcopy(ps.at[sib_w], pr.at[w], pss.at[sib_w], psr.at[w], sib).start()
            send_prefix(chip(-sg))
        ogot(s - 1).wait_recv()
        if s < half:
            oring(s).start()
        oside(s, True).start()
        if s >= 2:
            if s < half:
                send_prefix(chip(-sg * s))
            seen(chip(sg * (s - 1)))
            send_prefix(chip(sg * (s - 1)))
            project(chip(sg * (s - 1)))
            project(chip(-sg * (s - 1)))
        if s == 3:
            project(z)
            fill_tree()
        if s == 4:
            fill_slots()
    side(chip(half), 1 - c).wait_recv()
    send_prefix(chip(half))
    project(chip(half))
    for i, ref in enumerate((qs, ks, vs)):
        ref[...] = proj[:, i * HD : (i + 1) * HD].astype(BF16)

    def drain_ring():
        for s in range(nz // 2):
            for i in range(2):
                if s < nz // 2 - 1 or i == 0:
                    ring(s, c if i == 0 else 1 - c).wait_send()
        side(z, c).wait_send()
        o_side.wait_send()
        for s in range(1, nz // 2):
            for sub in range(2):
                side(chip(-sg * s), sub).wait_send()
        side(chip(nz // 2), c).wait_send()

    scale = 1.0 / math.sqrt(HD)
    local[7].wait()
    pos = iota(cs.shape, 1)
    ok = (pos < lens[0]) & ((pos < SINK) | (pos >= lens[0] - WIN))
    cs[...] = jnp.where(ok, mm(qs[...], cache_k[...], DIMS1) * scale, NEG)
    ts[...] = jnp.where(anc[...] > 0.5, mm(qs[...], ks[...], DIMS1) * scale, NEG)

    def compact(fresh, cache, out):
        moved = mm(put[...], fresh[...])
        written = jnp.sum(put[...].astype(F32), axis=1, keepdims=True) > 0.5
        out[0] = jnp.where(written, moved.astype(BF16), cache[...])

    cp_own.wait()

    def pwait(d, _):
        t = lax.rem(w + d, nw)
        rcopy(pr.at[t], pr.at[t], pss.at[t], psr.at[t], sib).wait_recv()
        return 0

    lax.fori_loop(1, nw, pwait, 0)
    def drain_out():
        for s in range(nz // 2):
            oring(s).wait_send()
        for s in range(1, nz // 2 + 1):
            oside(s, True).wait_send()

        def sent_p(d, _):
            t = lax.rem(w + d, nw)
            rcopy(ps.at[t], pr.at[w], pss.at[t], psr.at[w], sib).wait_send()
            return 0

        lax.fori_loop(1, nw, sent_p, 0)

    prows = pr[...].reshape(-1, HD)
    is_key = lax.rem(iota((tok, nw * 16), 1), 16) < 8
    psc = jnp.where(is_key, mm(qs[...], prows, DIMS1) * scale, NEG)
    csc, tsc = cs[...], ts[...]
    top = jnp.maximum(
        jnp.max(psc, axis=1, keepdims=True),
        jnp.maximum(jnp.max(csc, axis=1, keepdims=True), jnp.max(tsc, axis=1, keepdims=True)),
    )
    pw = jnp.where(is_key, jnp.exp(psc - top), 0.0)
    pos = iota(cs.shape, 1)
    ok = (pos < lens[0]) & ((pos < SINK) | (pos >= lens[0] - WIN))
    cw = jnp.where(ok, jnp.exp(csc - top), 0.0)
    tw = jnp.where(anc[...] > 0.5, jnp.exp(tsc - top), 0.0)
    total = (
        jnp.sum(pw, axis=1, keepdims=True) + jnp.sum(cw, axis=1, keepdims=True) + jnp.sum(tw, axis=1, keepdims=True)
    )
    local[8].wait()
    weighted = (
        mm(pltpu.roll(pw, 8, 1).astype(BF16), prows)
        + mm(cw.astype(BF16), cache_v[...])
        + mm(tw.astype(BF16), vs[...])
    )
    attended = (weighted / total).astype(BF16)
    for s in range(1, nz // 2 + 1):
        oside(s, False).wait_recv()
    for i in range(4):
        four = go[i * 4 : i * 4 + 4].reshape(512, HD)
        terms = mm(attended, four, DIMS1)
        for j in range(4):
            part[i * 4 + j] = terms[:, j * HD : (j + 1) * HD].astype(BF16)

    def send1(d, _):
        t = lax.rem(n + d, nn)
        rcopy(part.at[t], rbuf.at[n], s1.at[t], r1s.at[n], (w, t)).start()
        return 0

    lax.fori_loop(1, nn, send1, 0)
    col = pl.multiple_of(n * HD, HD)

    def add1(d, acc):
        t = lax.rem(n + d, nn)
        rcopy(rbuf.at[t], rbuf.at[t], s1.at[t], r1s.at[t], (w, t)).wait_recv()
        return acc + rbuf[t].astype(F32)

    summed = lax.fori_loop(1, nn, add1, part[n].astype(F32))
    mixed = (hidden[:, pl.ds(col, HD)].astype(F32) + summed).astype(BF16)
    mx[n] = mixed
    slots = mm(place[...], mixed)
    dflat = dbuf.reshape(place.shape[0], HD)
    dflat[...] = slots.astype(BF16)


    def drain_plane():
        def sent_n(d, _):
            t = lax.rem(n + d, nn)
            rcopy(part.at[t], rbuf.at[n], s1.at[t], r1s.at[n], sib).wait_send()
            rcopy(mx.at[n], mx.at[n], s2.at[t], r2s.at[n], sib).wait_send()
            return 0

        lax.fori_loop(1, nn, sent_n, 0)

    def slot_of(dz):
        return lax.rem(nz + nz // 2 - dz, nz) * 2 + c

    def send_d(dz, core):
        t = chip(dz) * 2 + core
        rcopy(dbuf.at[t], r.at[slot_of(dz)], ds.at[t], dr.at[slot_of(dz)], (t, n)).start()

    cp_d = pltpu.make_async_copy(dbuf.at[w], r.at[nz + c], dr.at[nz + c])
    cp_d.start()
    send_d(0, 1 - c)
    for dz in (1, -1, 2, -2, 3, -3, 4):
        for core in range(2):
            send_d(dz, core)
    for dz in (nz // 2, -7, 7, -6, 6, -5, 5, -4):
        for core in range(2):
            send_d(dz, core)

    def send2(d, _):
        t = lax.rem(n + d, nn)
        rcopy(mx.at[n], mx.at[n], s2.at[t], r2s.at[n], (w, t)).start()
        return 0

    def wait2(d, _):
        t = lax.rem(n + d, nn)
        rcopy(mx.at[t], mx.at[t], s2.at[t], r2s.at[t], (w, t)).wait_recv()
        return 0

    def fill_router():
        lax.fori_loop(1, nn, wait2, 0)
        local[15].wait()
        power = jnp.zeros((tok, 1), F32)
        for t in range(nn):
            m = mx[t].astype(F32)
            power = power + jnp.sum(m * m, axis=1, keepdims=True)
        inv = lax.rsqrt(power / (nn * HD) + norm_eps)
        logits = jnp.zeros((E, tok), F32)
        for t in range(nn):
            row = (mx[t].astype(F32) * inv * expert_gain[:, t * HD : (t + 1) * HD]).astype(BF16)
            logits = logits + mm(router[:, t * HD : (t + 1) * HD], row, DIMS1)
        a = iota((E, tok), 0)
        picks = [
            jnp.sum(jnp.where(ids[k : k + 1, :] == a, logits, 0.0), axis=0, keepdims=True)
            for k in range(ids.shape[0])
        ]
        best = picks[0]
        for p in picks[1:]:
            best = jnp.maximum(best, p)
        exps = [jnp.exp(p - best) for p in picks]
        den = exps[0]
        for e in exps[1:]:
            den = den + e
        rows = iota(mix.shape, 0)
        m = jnp.zeros(mix.shape, F32)
        for k, e in enumerate(exps):
            m = m + jnp.where(rows == tgt[k : k + 1, :], e / den, 0.0)
        mix[...] = m

    def drain_dispatch():
        def sent_d(d, _):
            t = lax.rem(w + d, nw)
            rcopy(dbuf.at[t], r.at[0], ds.at[t], dr.at[0], sib).wait_send()
            return 0

        lax.fori_loop(1, nw, sent_d, 0)

    rflat = r.reshape(place.shape[0], HD)
    size = place.shape[0] // CHUNKS
    high = size - LOW

    def dev(axis, off):
        if axis == 0:
            return (w, y * NX + lax.rem(x + off + NX, NX))
        return (w, lax.rem(y + off + NY, NY) * NX + x)

    def pos_of(axis, off):
        if axis == 0:
            return lax.rem(x + off + NX, NX)
        return lax.rem(y + off + NY, NY)

    def xref(axis, b, o, lo, ln):
        if axis == 0:
            return xs.at[o, b, pl.ds(lo, ln), :]
        return xs.at[b, o, pl.ds(lo, ln), :]

    def hop(p, slot, b_off, o_off, half, to):
        axis, lo = p % 2, ORDER[p] * size
        lo, ln = {0: (lo, size), 1: (lo, LOW), 2: (lo + LOW, high)}[half]
        ref = xref(axis, pos_of(axis, b_off), pos_of(1 - axis, o_off), lo, ln)
        return rcopy(ref, ref, ss.at[p, slot], rrs.at[p, slot], to)

    def stage0(p):
        j, axis = ORDER[p], p % 2
        for i in range(nw // CHUNKS):
            ref = r.at[j * (nw // CHUNKS) + i]
            rcopy(ref, ref, ds.at[0], dr.at[j * (nw // CHUNKS) + i], sib).wait_recv()
        xs[y, x, pl.ds(j * size, size), :] = rflat[pl.ds(j * size, size), :]
        hop(p, 0, 0, 0, 0, dev(axis, 1)).start()
        hop(p, 1, 0, 0, 0, dev(axis, -1)).start()
        hop(p, 2, 0, 0, 0, dev(axis, 2)).start()
        hop(p, 4, 0, 0, 0, dev(1 - axis, 1)).start()
        hop(p, 5, 0, 0, 0, dev(1 - axis, -1)).start()

    def stage1(p):
        axis = p % 2
        for slot, off in ((0, -1), (1, 1)):
            hop(p, slot, off, 0, 0, sib).wait_recv()
            hop(p, 8 + 4 * slot, off, 0, 0, dev(1 - axis, 1)).start()
            hop(p, 9 + 4 * slot, off, 0, 0, dev(1 - axis, -1)).start()

    def second(p, base, b_off):
        axis = p % 2
        hop(p, base, b_off, -1, 0, sib).wait_recv()
        hop(p, base + 2, b_off, -1, 1, dev(1 - axis, 1)).start()
        hop(p, base + 1, b_off, 1, 0, sib).wait_recv()
        hop(p, base + 3, b_off, 1, 2, dev(1 - axis, -1)).start()

    def stage2(p):
        axis = p % 2
        second(p, 4, 0)
        hop(p, 2, 2, 0, 0, sib).wait_recv()
        hop(p, 16, 2, 0, 0, dev(1 - axis, 1)).start()
        hop(p, 17, 2, 0, 0, dev(1 - axis, -1)).start()
        second(p, 8, -1)
        second(p, 12, 1)

    def stage3(p):
        second(p, 16, 2)

    def sref(axis, b, lo, ln):
        if axis == 0:
            return src.at[:, b, pl.ds(lo, ln), :]
        return src.at[b, :, pl.ds(lo, ln), :]

    def val(axis, b, lo, ln):
        return sref(axis, b, lo, ln)[...].astype(F32)

    def f1d(p, slot, lo, ln, to):
        ref = f1.at[p, :, pl.ds(lo, ln), :]
        return rcopy(ref, ref, us.at[p, slot], ur.at[p, slot], to)

    def stage4(p):
        axis, lo = p % 2, ORDER[p] * size
        for base, b_off in ((4, 0), (8, -1), (12, 1), (16, 2)):
            hop(p, base + 2, b_off, 2, 1, sib).wait_recv()
            hop(p, base + 3, b_off, 2, 2, sib).wait_recv()
        if p == 0:
            for cp in local[9:15]:
                cp.wait()
        power = jnp.zeros((size, 1), F32)
        for t in range(nn):
            m = xs[t // NX, t % NX, lo : lo + size, :].astype(F32)
            power = power + jnp.sum(m * m, axis=1, keepdims=True)
        inv = lax.rsqrt(power / (nn * HD) + norm_eps)
        units = jnp.zeros((size, 4 * fw), F32)
        for t in range(nn):
            m = xs[t // NX, t % NX, lo : lo + size, :].astype(F32)
            m = (m * inv * expert_gain[:, t * HD : (t + 1) * HD]).astype(BF16)
            units = units + mm(m, wgt[:, t * HD : (t + 1) * HD], DIMS1)
        gt = units[:, : 2 * fw]
        act = gt / (1.0 + jnp.exp(-gt)) * units[:, 2 * fw :]
        row = lax.rem(iota(act.shape, 0), 2 * CAP)
        keep = (row >= CAP) == (iota(act.shape, 1) >= fw)
        act = jnp.where(keep, act, 0.0).astype(BF16)
        for t in range(nn):
            src[t // NX, t % NX, lo : lo + size, :] = mm(act, dn[:, t * HD : (t + 1) * HD]).astype(BF16)
        b2 = pos_of(axis, 2)
        rcopy(sref(axis, b2, lo, LOW), f1.at[p, :, pl.ds(0, LOW), :], us.at[p, 0], ur.at[p, 0], dev(axis, 1)).start()
        rcopy(
            sref(axis, b2, lo + LOW, high), f1.at[p, :, pl.ds(LOW, high), :], us.at[p, 1], ur.at[p, 1], dev(axis, -1)
        ).start()

    def t1d(p, k, to):
        return rcopy(t1.at[p, k], r1.at[p, k], us.at[p, 2 + k], ur.at[p, 2 + k], to)

    def last(p, k, b, to):
        return rcopy(m2.at[p, b], r2.at[p, k], us.at[p, 4 + k], ur.at[p, 4 + k], to)

    def stage5(p):
        axis, lo = p % 2, ORDER[p] * size
        bp, bm = pos_of(axis, 1), pos_of(axis, -1)
        t1[p, 0, :, LOW:, :] = sref(axis, bp, lo + LOW, high)[...]
        t1[p, 1, :, :LOW, :] = sref(axis, bm, lo, LOW)[...]
        f1d(p, 0, 0, LOW, sib).wait_recv()
        t1[p, 0, :, :LOW, :] = (val(axis, bp, lo, LOW) + f1[p, :, :LOW, :].astype(F32)).astype(BF16)
        t1d(p, 0, dev(axis, 1)).start()
        f1d(p, 1, LOW, high, sib).wait_recv()
        t1[p, 1, :, LOW:, :] = (val(axis, bm, lo + LOW, high) + f1[p, :, LOW:, :].astype(F32)).astype(BF16)
        t1d(p, 1, dev(axis, -1)).start()

    def stage6(p):
        axis, lo = p % 2, ORDER[p] * size
        t1d(p, 0, sib).wait_recv()
        t1d(p, 1, sib).wait_recv()
        m2[p] = (val(axis, pos_of(axis, 0), lo, size) + r1[p, 0].astype(F32) + r1[p, 1].astype(F32)).astype(BF16)
        for k, off in enumerate((1, -1, 2)):
            last(p, k, pos_of(1 - axis, off), dev(1 - axis, off)).start()

    bflat = bbuf.reshape(place.shape[0], HD)

    def stage8(p):
        j, axis = ORDER[p], p % 2
        for k in range(3):
            last(p, k, 0, sib).wait_recv()
        bflat[pl.ds(j * size, size), :] = (
            (m2[p, pos_of(1 - axis, 0)].astype(F32) + r2[p, 0].astype(F32))
            + (r2[p, 1].astype(F32) + r2[p, 2].astype(F32))
        ).astype(BF16)
        for i in range(nz // CHUNKS):
            rel = j * (nz // CHUNKS) + i
            for core in range(2):
                t = chip(rel - nz // 2) * 2 + core
                a = bbuf.at[rel * 2 + core]
                if rel == nz // 2:
                    if core == 0:
                        pltpu.make_async_copy(bbuf.at[nz + c], bk.at[w], er.at[w]).start()
                        rcopy(bbuf.at[nz + 1 - c], bk.at[w], es.at[nz + 1 - c], er.at[w], sib).start()
                else:
                    rcopy(a, bk.at[w], es.at[rel * 2 + core], er.at[w], (t, n)).start()

    def drain_pipe():
        def sent_b(d, _):
            t = lax.rem(nz + c + d, nw)
            rcopy(bbuf.at[t], bk.at[w], es.at[t], er.at[w], sib).wait_send()
            return 0

        lax.fori_loop(1, nw, sent_b, 0)
        for p in range(CHUNKS):
            for slot in range(20):
                if slot == 3:
                    continue
                half = 0 if slot < 3 or slot % 4 < 2 else slot % 4 - 1
                hop(p, slot, 0, 0, half, sib).wait_send()
            f1d(p, 0, 0, LOW, sib).wait_send()
            f1d(p, 1, LOW, high, sib).wait_send()
            for k in range(2):
                t1d(p, k, sib).wait_send()
            for k in range(3):
                last(p, k, 0, sib).wait_send()

    stages = (stage0, stage1, stage2, stage3, stage4, stage5, stage6, stage8)
    for k in range(len(stages)):
        for p in range(CHUNKS):
            stages[k](p)
        if k == 4:
            compact(ks, cache_k, new_k)
            compact(vs, cache_v, new_v)
        if k == 6:
            lax.fori_loop(1, nn, send2, 0)
    fill_router()

    def wait_b(d, _):
        t = lax.rem(w + d, nw)
        rcopy(bk.at[t], bk.at[t], es.at[t], er.at[t], sib).wait_recv()
        return 0

    lax.fori_loop(0, nw, wait_b, 0)
    moe = lax.dot_general(
        mix[...], bk.reshape(place.shape[0], HD)[...].astype(F32), DIMS0,
        precision=lax.Precision.HIGHEST, preferred_element_type=F32,
    )
    layer_out[...] = (mx[n].astype(F32) + moe).astype(BF16)

    drain_ring()
    drain_out()
    drain_plane()
    drain_dispatch()
    drain_pipe()


def body(
    hidden, attn_gain, expert_gain, query_weight, key_weight, value_weight, output_weight, router_weight,
    gate_weight, up_weight, down_weight, prefix_keys, prefix_values, cache_keys, cache_values, parents,
    cache_lengths, group_ids, expert_ids, accepted,
):
    tok, width = hidden.shape
    nn = lax.axis_size("narrow")
    nw = lax.axis_size("wide")
    nz = nw // 2
    rows = nw * gate_weight.shape[0] * CAP
    size = rows // CHUNKS
    cache = cache_keys.shape[1]
    vm = pl.BlockSpec(memory_space=pltpu.VMEM)
    sm = pl.BlockSpec(memory_space=pltpu.SMEM)
    hbm = pl.BlockSpec(memory_space=pl.ANY)
    dma = pltpu.SemaphoreType.DMA

    def v(*shape, t=BF16):
        return pltpu.VMEM(shape, t)

    pair = rows // nw // 2
    fw = gate_weight.shape[2]
    scratch = [
        v(tok, width), v(E, width), v(4 * fw, width), v(2 * fw, width), v(cache, HD), v(cache, HD),
        v(*prefix_keys.shape), v(*prefix_values.shape), v(tok, 3 * HD, t=F32),
        v(tok, width), v(nz, 2, 3, 64, HD), v(nz, 2, 64, HD), v(nw, 16, HD), v(nw, 16, HD),
        v(tok, HD), v(tok, HD), v(tok, HD), v(tok, cache, t=F32), v(tok, tok, t=F32), v(tok, tok, t=F32),
        v(cache, tok), v(nn, tok, HD), v(nn, tok, HD), v(nn, tok, HD),
        v(expert_ids.shape[1], tok, t=jnp.int32), v(rows, tok), v(rows, tok, t=F32),
        v(nw, pair, 2, HD), v(nw, pair, 2, HD), v(NY, NX, rows, HD), v(NY, NX, rows, HD),
        v(CHUNKS, 2, 4, size, HD), v(CHUNKS, 4, size, HD), v(CHUNKS, 2, 4, size, HD), v(CHUNKS, 4, size, HD),
        v(CHUNKS, 3, size, HD), v(nw, pair, 2, HD), v(nw, pair, 2, HD),
        dma((16,)), dma((nz // 2, 2)), dma((nz // 2, 2)), dma((nz, 2)), dma((nz, 2)),
        dma((nz // 2,)), dma((nz // 2,)), dma((nz + 1,)), dma((nz + 1,)), dma((nw,)), dma((nw,)),
        dma((nn,)), dma((nn,)), dma((nn,)), dma((nn,)), dma((nw,)), dma((nw,)),
        dma((CHUNKS, 20)), dma((CHUNKS, 20)), dma((CHUNKS, 8)), dma((CHUNKS, 8)), dma((nw,)), dma((nw,)),
    ]
    return pl.pallas_call(
        layer_kernel,
        out_shape=(
            jax.ShapeDtypeStruct((tok, HD), BF16),
            jax.ShapeDtypeStruct(cache_keys.shape, BF16),
            jax.ShapeDtypeStruct(cache_values.shape, BF16),
        ),
        in_specs=[sm, sm] + [vm] * 5 + [hbm] * 13,
        out_specs=(vm, vm, vm),
        scratch_shapes=scratch,
        compiler_params=pltpu.CompilerParams(
            collective_id=0, has_side_effects=True, vmem_limit_bytes=60 * 1024 * 1024
        ),
        name="layer",
    )(
        cache_lengths, accepted, attn_gain[None], expert_gain[None], parents, group_ids[None], expert_ids.T,
        hidden, query_weight, key_weight, value_weight, output_weight, router_weight.T,
        jnp.swapaxes(gate_weight, 1, 2), jnp.swapaxes(up_weight, 1, 2), down_weight,
        prefix_keys, prefix_values, cache_keys, cache_values,
    )


def solution(mesh):
    in_specs = (
        P("wide", None),
        P(),
        P(),
        P("wide", "narrow"),
        P("wide", "narrow"),
        P("wide", "narrow"),
        P("wide", "narrow"),
        P(),
        P("wide", None, "narrow"),
        P("wide", None, "narrow"),
        P("wide", "narrow", None),
        P("wide", None, "narrow"),
        P("wide", None, "narrow"),
        P("wide", None, "narrow"),
        P("wide", None, "narrow"),
        P("wide", None),
        P("wide"),
        P(),
        P("wide", None),
        P("wide"),
    )
    out_specs = (P("wide", "narrow"), P("wide", None, "narrow"), P("wide", None, "narrow"))
    return jax.shard_map(body, mesh=mesh, in_specs=in_specs, out_specs=out_specs, check_vma=False)
```

```python
import math

import jax
import jax.numpy as jnp
from jax import lax
from jax.experimental import pallas as pl
from jax.experimental.pallas import tpu as pltpu
from jax.sharding import PartitionSpec as P

HD = 128
E = 64
SINK = 4
WIN = 512
CAP = 9
NX = 4
NY = 4
MESH = pl.DeviceIdType.MESH
F32 = jnp.float32
BF16 = jnp.bfloat16

norm_eps = 1e-06


def rms_scale(rows, row_gain):
    widened = rows.astype(F32)
    power_mean = jnp.mean(widened * widened, axis=-1, keepdims=True)
    return (widened * lax.rsqrt(power_mean + norm_eps) * row_gain).astype(BF16)


DIMS0 = (((0,), (0,)), ((), ()))
DIMS1 = (((1,), (1,)), ((), ()))
CHUNKS = 4
ORDER = (2, 1, 3, 0)
LOW = 80
NEG = -1e30


def rcopy(src, dst, ssem, rsem, dev):
    return pltpu.make_async_remote_copy(
        src_ref=src, dst_ref=dst, send_sem=ssem, recv_sem=rsem, device_id=dev, device_id_type=MESH
    )


def iota(shape, dim):
    return lax.broadcasted_iota(jnp.int32, shape, dim)


def mm(a, b, dims=(((1,), (0,)), ((), ()))):
    return lax.dot_general(a, b, dims, preferred_element_type=F32)


def layer_kernel(
    lens, acc_node, attn_gain, expert_gain, parents, groups, ids,
    hidden_in, q_in, k_in, v_in, o_in, router_in, gate, up, down, pk_in, pv_in, ck_in, cv_in,
    layer_out, new_k, new_v,
    hidden, router, wgt, dn, cache_k, cache_v, pk, pv, proj,
    normed, g, go, ps, pr, qs, ks, vs, cs, ts, anc, put, part, rbuf, mx, tgt, place, mix,
    dbuf, r, xs, src, r1, f1, t1, m2, r2, bbuf, bk,
    ls, rs, rr, fs, fr, os, orr, ofs, ofr, pss, psr, s1, r1s, s2, r2s, ds, dr, ss, rrs, us, ur, es, er,
):
    nz, nn, nw = g.shape[0], part.shape[0], pr.shape[0]
    tok = hidden.shape[0]
    w = lax.axis_index("wide")
    n = lax.axis_index("narrow")
    z = w // 2
    c = lax.rem(w, 2)
    y = n // NX
    x = lax.rem(n, NX)
    sg = 1 - 2 * c
    sib_w = w + sg
    sib = (sib_w, n)

    def chip(off):
        return lax.rem(z + off + nz, nz)

    nxt = (chip(sg) * 2 + c, n)

    barrier = pltpu.get_barrier_semaphore()
    for t in (sib, (chip(1) * 2 + c, n), (chip(nz - 1) * 2 + c, n)):
        pl.semaphore_signal(barrier, inc=1, device_id=t, device_id_type=MESH)

    def greet(d, _):
        pl.semaphore_signal(barrier, inc=1, device_id=(w, lax.rem(n + d, nn)), device_id_type=MESH)
        return 0

    lax.fori_loop(1, nn, greet, 0)
    fw = gate.shape[1]
    moves = (
        (q_in, g.at[z, c, 0]), (k_in, g.at[z, c, 1]), (v_in, g.at[z, c, 2]), (o_in, go.at[z, c]),
        (hidden_in, hidden), (pk_in, pk), (pv_in, pv), (ck_in.at[0], cache_k), (cv_in.at[0], cache_v),
        (gate.at[0], wgt.at[pl.ds(0, fw), :]), (gate.at[1], wgt.at[pl.ds(fw, fw), :]),
        (up.at[0], wgt.at[pl.ds(2 * fw, fw), :]), (up.at[1], wgt.at[pl.ds(3 * fw, fw), :]),
        (down.at[0], dn.at[pl.ds(0, fw), :]), (down.at[1], dn.at[pl.ds(fw, fw), :]), (router_in, router),
    )
    local = [pltpu.make_async_copy(a, b, ls.at[i]) for i, (a, b) in enumerate(moves)]
    for cp in local:
        cp.start()
    for cp in local[:4]:
        cp.wait()
    pl.semaphore_wait(barrier, nn + 2)

    def ring(s, sub):
        ref = g.at[chip(-sg * s), sub]
        return rcopy(ref, ref, rs.at[s, sub], rr.at[s, sub], nxt)

    def got(s, sub):
        ref = g.at[chip(-sg * (s + 1)), sub]
        return rcopy(ref, ref, rs.at[s, sub], rr.at[s, sub], nxt)

    def side(chip_id, sub):
        ref = g.at[chip_id, sub]
        return rcopy(ref, ref, fs.at[chip_id, sub], fr.at[chip_id, sub], sib)

    side(z, c).start()
    oref = go.at[z, c]
    o_side = rcopy(oref, oref, ofs.at[nz], ofr.at[nz], sib)
    o_side.start()
    ring(0, c).start()
    osib = go.at[z, 1 - c]
    side(z, 1 - c).wait_recv()
    ring(0, 1 - c).start()

    def fill_norm():
        local[4].wait()
        hv = hidden[...].astype(F32)
        power = jnp.mean(hv * hv, axis=-1, keepdims=True)
        normed[...] = (hv * lax.rsqrt(power + norm_eps) * attn_gain[...]).astype(BF16)
        proj[...] = jnp.zeros_like(proj)

    def fill_prefix():
        local[5].wait()
        local[6].wait()
        rows, cols = nw * 16, 64
        it = iota((rows, nw), 0) // 16
        gid = jnp.sum(jnp.where(it == iota((rows, nw), 1), groups[...], 0), axis=1, keepdims=True)
        r_id = lax.rem(iota((rows, cols), 0), 16)
        c_id = iota((rows, cols), 1)
        same = lax.rem(c_id, 8) == gid
        one_k = (same & (c_id // 8 == r_id)).astype(F32).astype(BF16)
        one_v = (same & (c_id // 8 + 8 == r_id)).astype(F32).astype(BF16)
        picked = mm(one_k, pk[...].reshape(cols, HD)) + mm(one_v, pv[...].reshape(cols, HD))
        ps[...] = picked.astype(BF16).reshape(ps.shape)

    def fill_tree():
        size = parents.shape[1]
        a, b = iota((size, size), 0), iota((size, size), 1)
        eye = (a == b).astype(F32)
        up_t = jnp.maximum(eye, (parents[...] == a).astype(F32))
        for _ in range(6):
            m = up_t.astype(BF16)
            up_t = (mm(m, m) > 0.5).astype(F32)
        depth = jnp.sum(up_t, axis=0, keepdims=True) - 1.0
        full = mm(up_t.astype(BF16), eye.astype(BF16), DIMS0)
        anc[...] = full
        on_path = jnp.sum(jnp.where(a == acc_node[0], full, 0.0), axis=0, keepdims=True)
        slot = jnp.where(on_path > 0.5, lens[0] + depth.astype(jnp.int32), put.shape[0])
        put[...] = (iota(put.shape, 0) == slot).astype(F32).astype(BF16)

    def fill_slots():
        a, b = iota((E, tok), 0), iota((E, tok), 1)
        named = jnp.zeros((E, tok), F32)
        for k in range(ids.shape[0]):
            named = named + (ids[k : k + 1, :] == a).astype(F32)
        earlier = mm(named.astype(BF16), (iota((tok, tok), 0) < iota((tok, tok), 1)).astype(F32).astype(BF16))
        hit = jnp.zeros(place.shape, F32)
        rows = iota(place.shape, 0)
        for k in range(ids.shape[0]):
            idk = ids[k : k + 1, :]
            rank = jnp.sum(jnp.where(idk == a, earlier, 0.0), axis=0, keepdims=True)
            t = idk * CAP + rank.astype(jnp.int32)
            tgt[k : k + 1, :] = t
            hit = hit + (rows == t).astype(F32)
        place[...] = hit.astype(BF16)

    def oring(s):
        k = chip(-sg * s)
        ref = go.at[k] if s < nz // 2 - 1 else go.at[k, c]
        return rcopy(ref, ref, os.at[s], orr.at[s], nxt)

    def ogot(s):
        k = chip(-sg * (s + 1))
        ref = go.at[k] if s < nz // 2 - 1 else go.at[k, c]
        return rcopy(ref, ref, os.at[s], orr.at[s], nxt)

    def oside(s, mine):
        k = chip(-sg * s) if mine else chip(sg * s)
        ref = go.at[k] if s < nz // 2 else go.at[k, c if mine else 1 - c]
        return rcopy(ref, ref, ofs.at[k], ofr.at[k], sib)

    def send_prefix(k):
        for core in range(2):
            t = k * 2 + core
            rcopy(ps.at[t], pr.at[w], pss.at[t], psr.at[w], (t, n)).start()

    def project(k):
        cols = pl.ds(pl.multiple_of(k * HD, HD), HD)
        a = normed[:, cols]
        for i in range(3):
            b = jnp.concatenate([g[k, 0, i], g[k, 1, i]], axis=0)
            proj[:, i * HD : (i + 1) * HD] += mm(a, b)

    half = nz // 2
    rcopy(osib, osib, ofs.at[nz], ofr.at[nz], sib).wait_recv()
    oring(0).start()
    cp_own = pltpu.make_async_copy(ps.at[w], pr.at[w], psr.at[w])

    def seen(k):
        for sub in range(2):
            side(k, sub).wait_recv()

    for s in range(1, half + 1):
        for i in range(2 if s < half else 1):
            sub = c if i == 0 else 1 - c
            got(s - 1, sub).wait_recv()
            if s < half - 1 or (s < half and i == 0):
                ring(s, sub).start()
            side(chip(-sg * s), sub).start()
        if s == 1:
            fill_norm()
        if s == 2:
            fill_prefix()
            cp_own.start()
            rcopy(ps.at[sib_w], pr.at[w], pss.at[sib_w], psr.at[w], sib).start()
            send_prefix(chip(-sg))
        ogot(s - 1).wait_recv()
        if s < half:
            oring(s).start()
        oside(s, True).start()
        if s >= 2:
            if s < half:
                send_prefix(chip(-sg * s))
            seen(chip(sg * (s - 1)))
            send_prefix(chip(sg * (s - 1)))
            project(chip(sg * (s - 1)))
            project(chip(-sg * (s - 1)))
        if s == 3:
            project(z)
            fill_tree()
        if s == 4:
            fill_slots()
    side(chip(half), 1 - c).wait_recv()
    send_prefix(chip(half))
    project(chip(half))
    for i, ref in enumerate((qs, ks, vs)):
        ref[...] = proj[:, i * HD : (i + 1) * HD].astype(BF16)

    def drain_ring():
        for s in range(nz // 2):
            for i in range(2):
                if s < nz // 2 - 1 or i == 0:
                    ring(s, c if i == 0 else 1 - c).wait_send()
        side(z, c).wait_send()
        o_side.wait_send()
        for s in range(1, nz // 2):
            for sub in range(2):
                side(chip(-sg * s), sub).wait_send()
        side(chip(nz // 2), c).wait_send()

    scale = 1.0 / math.sqrt(HD)
    local[7].wait()
    pos = iota(cs.shape, 1)
    ok = (pos < lens[0]) & ((pos < SINK) | (pos >= lens[0] - WIN))
    cs[...] = jnp.where(ok, mm(qs[...], cache_k[...], DIMS1) * scale, NEG)
    ts[...] = jnp.where(anc[...] > 0.5, mm(qs[...], ks[...], DIMS1) * scale, NEG)

    def compact(fresh, cache, out):
        moved = mm(put[...], fresh[...])
        written = jnp.sum(put[...].astype(F32), axis=1, keepdims=True) > 0.5
        out[0] = jnp.where(written, moved.astype(BF16), cache[...])

    cp_own.wait()

    def pwait(d, _):
        t = lax.rem(w + d, nw)
        rcopy(pr.at[t], pr.at[t], pss.at[t], psr.at[t], sib).wait_recv()
        return 0

    lax.fori_loop(1, nw, pwait, 0)
    def drain_out():
        for s in range(nz // 2):
            oring(s).wait_send()
        for s in range(1, nz // 2 + 1):
            oside(s, True).wait_send()

        def sent_p(d, _):
            t = lax.rem(w + d, nw)
            rcopy(ps.at[t], pr.at[w], pss.at[t], psr.at[w], sib).wait_send()
            return 0

        lax.fori_loop(1, nw, sent_p, 0)

    prows = pr[...].reshape(-1, HD)
    is_key = lax.rem(iota((tok, nw * 16), 1), 16) < 8
    psc = jnp.where(is_key, mm(qs[...], prows, DIMS1) * scale, NEG)
    csc, tsc = cs[...], ts[...]
    top = jnp.maximum(
        jnp.max(psc, axis=1, keepdims=True),
        jnp.maximum(jnp.max(csc, axis=1, keepdims=True), jnp.max(tsc, axis=1, keepdims=True)),
    )
    pw = jnp.where(is_key, jnp.exp(psc - top), 0.0)
    pos = iota(cs.shape, 1)
    ok = (pos < lens[0]) & ((pos < SINK) | (pos >= lens[0] - WIN))
    cw = jnp.where(ok, jnp.exp(csc - top), 0.0)
    tw = jnp.where(anc[...] > 0.5, jnp.exp(tsc - top), 0.0)
    total = (
        jnp.sum(pw, axis=1, keepdims=True) + jnp.sum(cw, axis=1, keepdims=True) + jnp.sum(tw, axis=1, keepdims=True)
    )
    local[8].wait()
    weighted = (
        mm(pltpu.roll(pw, 8, 1).astype(BF16), prows)
        + mm(cw.astype(BF16), cache_v[...])
        + mm(tw.astype(BF16), vs[...])
    )
    attended = (weighted / total).astype(BF16)
    for s in range(1, nz // 2 + 1):
        oside(s, False).wait_recv()
    for i in range(4):
        four = go[i * 4 : i * 4 + 4].reshape(512, HD)
        terms = mm(attended, four, DIMS1)
        for j in range(4):
            part[i * 4 + j] = terms[:, j * HD : (j + 1) * HD].astype(BF16)

    def send1(d, _):
        t = lax.rem(n + d, nn)
        rcopy(part.at[t], rbuf.at[n], s1.at[t], r1s.at[n], (w, t)).start()
        return 0

    lax.fori_loop(1, nn, send1, 0)
    col = pl.multiple_of(n * HD, HD)

    def add1(d, acc):
        t = lax.rem(n + d, nn)
        rcopy(rbuf.at[t], rbuf.at[t], s1.at[t], r1s.at[t], (w, t)).wait_recv()
        return acc + rbuf[t].astype(F32)

    summed = lax.fori_loop(1, nn, add1, part[n].astype(F32))
    mixed = (hidden[:, pl.ds(col, HD)].astype(F32) + summed).astype(BF16)
    mx[n] = mixed
    slots = mm(place[...], mixed)
    dflat = dbuf.reshape(place.shape[0], HD)
    dflat[...] = slots.astype(BF16)


    def drain_plane():
        def sent_n(d, _):
            t = lax.rem(n + d, nn)
            rcopy(part.at[t], rbuf.at[n], s1.at[t], r1s.at[n], sib).wait_send()
            rcopy(mx.at[n], mx.at[n], s2.at[t], r2s.at[n], sib).wait_send()
            return 0

        lax.fori_loop(1, nn, sent_n, 0)

    def slot_of(dz):
        return lax.rem(nz + nz // 2 - dz, nz) * 2 + c

    def send_d(dz, core):
        t = chip(dz) * 2 + core
        rcopy(dbuf.at[t], r.at[slot_of(dz)], ds.at[t], dr.at[slot_of(dz)], (t, n)).start()

    cp_d = pltpu.make_async_copy(dbuf.at[w], r.at[nz + c], dr.at[nz + c])
    cp_d.start()
    send_d(0, 1 - c)
    for dz in (1, -1, 2, -2, 3, -3, 4):
        for core in range(2):
            send_d(dz, core)
    for dz in (nz // 2, -7, 7, -6, 6, -5, 5, -4):
        for core in range(2):
            send_d(dz, core)
    compact(ks, cache_k, new_k)
    compact(vs, cache_v, new_v)

    def send2(d, _):
        t = lax.rem(n + d, nn)
        rcopy(mx.at[n], mx.at[n], s2.at[t], r2s.at[n], (w, t)).start()
        return 0

    def wait2(d, _):
        t = lax.rem(n + d, nn)
        rcopy(mx.at[t], mx.at[t], s2.at[t], r2s.at[t], (w, t)).wait_recv()
        return 0

    def fill_router():
        lax.fori_loop(1, nn, wait2, 0)
        local[15].wait()
        power = jnp.zeros((tok, 1), F32)
        for t in range(nn):
            m = mx[t].astype(F32)
            power = power + jnp.sum(m * m, axis=1, keepdims=True)
        inv = lax.rsqrt(power / (nn * HD) + norm_eps)
        logits = jnp.zeros((E, tok), F32)
        for t in range(nn):
            row = (mx[t].astype(F32) * inv * expert_gain[:, t * HD : (t + 1) * HD]).astype(BF16)
            logits = logits + mm(router[:, t * HD : (t + 1) * HD], row, DIMS1)
        a = iota((E, tok), 0)
        picks = [
            jnp.sum(jnp.where(ids[k : k + 1, :] == a, logits, 0.0), axis=0, keepdims=True)
            for k in range(ids.shape[0])
        ]
        best = picks[0]
        for p in picks[1:]:
            best = jnp.maximum(best, p)
        exps = [jnp.exp(p - best) for p in picks]
        den = exps[0]
        for e in exps[1:]:
            den = den + e
        rows = iota(mix.shape, 0)
        m = jnp.zeros(mix.shape, F32)
        for k, e in enumerate(exps):
            m = m + jnp.where(rows == tgt[k : k + 1, :], e / den, 0.0)
        mix[...] = m

    def drain_dispatch():
        def sent_d(d, _):
            t = lax.rem(w + d, nw)
            rcopy(dbuf.at[t], r.at[0], ds.at[t], dr.at[0], sib).wait_send()
            return 0

        lax.fori_loop(1, nw, sent_d, 0)

    rflat = r.reshape(place.shape[0], HD)
    size = place.shape[0] // CHUNKS
    high = size - LOW

    def dev(axis, off):
        if axis == 0:
            return (w, y * NX + lax.rem(x + off + NX, NX))
        return (w, lax.rem(y + off + NY, NY) * NX + x)

    def pos_of(axis, off):
        if axis == 0:
            return lax.rem(x + off + NX, NX)
        return lax.rem(y + off + NY, NY)

    def xref(axis, b, o, lo, ln):
        if axis == 0:
            return xs.at[o, b, pl.ds(lo, ln), :]
        return xs.at[b, o, pl.ds(lo, ln), :]

    def hop(p, slot, b_off, o_off, half, to):
        axis, lo = p % 2, ORDER[p] * size
        lo, ln = {0: (lo, size), 1: (lo, LOW), 2: (lo + LOW, high)}[half]
        ref = xref(axis, pos_of(axis, b_off), pos_of(1 - axis, o_off), lo, ln)
        return rcopy(ref, ref, ss.at[p, slot], rrs.at[p, slot], to)

    def stage0(p):
        j, axis = ORDER[p], p % 2
        for i in range(nw // CHUNKS):
            ref = r.at[j * (nw // CHUNKS) + i]
            rcopy(ref, ref, ds.at[0], dr.at[j * (nw // CHUNKS) + i], sib).wait_recv()
        xs[y, x, pl.ds(j * size, size), :] = rflat[pl.ds(j * size, size), :]
        hop(p, 0, 0, 0, 0, dev(axis, 1)).start()
        hop(p, 1, 0, 0, 0, dev(axis, -1)).start()
        hop(p, 2, 0, 0, 0, dev(axis, 2)).start()
        hop(p, 4, 0, 0, 0, dev(1 - axis, 1)).start()
        hop(p, 5, 0, 0, 0, dev(1 - axis, -1)).start()

    def stage1(p):
        axis = p % 2
        for slot, off in ((0, -1), (1, 1)):
            hop(p, slot, off, 0, 0, sib).wait_recv()
            hop(p, 8 + 4 * slot, off, 0, 0, dev(1 - axis, 1)).start()
            hop(p, 9 + 4 * slot, off, 0, 0, dev(1 - axis, -1)).start()

    def second(p, base, b_off):
        axis = p % 2
        hop(p, base, b_off, -1, 0, sib).wait_recv()
        hop(p, base + 2, b_off, -1, 1, dev(1 - axis, 1)).start()
        hop(p, base + 1, b_off, 1, 0, sib).wait_recv()
        hop(p, base + 3, b_off, 1, 2, dev(1 - axis, -1)).start()

    def stage2(p):
        axis = p % 2
        second(p, 4, 0)
        hop(p, 2, 2, 0, 0, sib).wait_recv()
        hop(p, 16, 2, 0, 0, dev(1 - axis, 1)).start()
        hop(p, 17, 2, 0, 0, dev(1 - axis, -1)).start()
        second(p, 8, -1)
        second(p, 12, 1)

    def stage3(p):
        second(p, 16, 2)

    def sref(axis, b, lo, ln):
        if axis == 0:
            return src.at[:, b, pl.ds(lo, ln), :]
        return src.at[b, :, pl.ds(lo, ln), :]

    def val(axis, b, lo, ln):
        return sref(axis, b, lo, ln)[...].astype(F32)

    def f1d(p, slot, lo, ln, to):
        ref = f1.at[p, :, pl.ds(lo, ln), :]
        return rcopy(ref, ref, us.at[p, slot], ur.at[p, slot], to)

    def stage4(p):
        axis, lo = p % 2, ORDER[p] * size
        for base, b_off in ((4, 0), (8, -1), (12, 1), (16, 2)):
            hop(p, base + 2, b_off, 2, 1, sib).wait_recv()
            hop(p, base + 3, b_off, 2, 2, sib).wait_recv()
        if p == 0:
            for cp in local[9:15]:
                cp.wait()
        power = jnp.zeros((size, 1), F32)
        for t in range(nn):
            m = xs[t // NX, t % NX, lo : lo + size, :].astype(F32)
            power = power + jnp.sum(m * m, axis=1, keepdims=True)
        inv = lax.rsqrt(power / (nn * HD) + norm_eps)
        units = jnp.zeros((size, 4 * fw), F32)
        for t in range(nn):
            m = xs[t // NX, t % NX, lo : lo + size, :].astype(F32)
            m = (m * inv * expert_gain[:, t * HD : (t + 1) * HD]).astype(BF16)
            units = units + mm(m, wgt[:, t * HD : (t + 1) * HD], DIMS1)
        gt = units[:, : 2 * fw]
        act = gt / (1.0 + jnp.exp(-gt)) * units[:, 2 * fw :]
        row = lax.rem(iota(act.shape, 0), 2 * CAP)
        keep = (row >= CAP) == (iota(act.shape, 1) >= fw)
        act = jnp.where(keep, act, 0.0).astype(BF16)
        for t in range(nn):
            src[t // NX, t % NX, lo : lo + size, :] = mm(act, dn[:, t * HD : (t + 1) * HD]).astype(BF16)
        b2 = pos_of(axis, 2)
        rcopy(sref(axis, b2, lo, LOW), f1.at[p, :, pl.ds(0, LOW), :], us.at[p, 0], ur.at[p, 0], dev(axis, 1)).start()
        rcopy(
            sref(axis, b2, lo + LOW, high), f1.at[p, :, pl.ds(LOW, high), :], us.at[p, 1], ur.at[p, 1], dev(axis, -1)
        ).start()

    def t1d(p, k, to):
        return rcopy(t1.at[p, k], r1.at[p, k], us.at[p, 2 + k], ur.at[p, 2 + k], to)

    def last(p, k, b, to):
        return rcopy(m2.at[p, b], r2.at[p, k], us.at[p, 4 + k], ur.at[p, 4 + k], to)

    def stage5(p):
        axis, lo = p % 2, ORDER[p] * size
        bp, bm = pos_of(axis, 1), pos_of(axis, -1)
        t1[p, 0, :, LOW:, :] = sref(axis, bp, lo + LOW, high)[...]
        t1[p, 1, :, :LOW, :] = sref(axis, bm, lo, LOW)[...]
        f1d(p, 0, 0, LOW, sib).wait_recv()
        t1[p, 0, :, :LOW, :] = (val(axis, bp, lo, LOW) + f1[p, :, :LOW, :].astype(F32)).astype(BF16)
        t1d(p, 0, dev(axis, 1)).start()
        f1d(p, 1, LOW, high, sib).wait_recv()
        t1[p, 1, :, LOW:, :] = (val(axis, bm, lo + LOW, high) + f1[p, :, LOW:, :].astype(F32)).astype(BF16)
        t1d(p, 1, dev(axis, -1)).start()

    def stage6(p):
        axis, lo = p % 2, ORDER[p] * size
        t1d(p, 0, sib).wait_recv()
        t1d(p, 1, sib).wait_recv()
        m2[p] = (val(axis, pos_of(axis, 0), lo, size) + r1[p, 0].astype(F32) + r1[p, 1].astype(F32)).astype(BF16)
        for k, off in enumerate((1, -1, 2)):
            last(p, k, pos_of(1 - axis, off), dev(1 - axis, off)).start()

    bflat = bbuf.reshape(place.shape[0], HD)

    def stage8(p):
        j, axis = ORDER[p], p % 2
        for k in range(3):
            last(p, k, 0, sib).wait_recv()
        bflat[pl.ds(j * size, size), :] = (
            (m2[p, pos_of(1 - axis, 0)].astype(F32) + r2[p, 0].astype(F32))
            + (r2[p, 1].astype(F32) + r2[p, 2].astype(F32))
        ).astype(BF16)
        for i in range(nz // CHUNKS):
            rel = j * (nz // CHUNKS) + i
            for core in range(2):
                t = chip(rel - nz // 2) * 2 + core
                a = bbuf.at[rel * 2 + core]
                if rel == nz // 2:
                    if core == 0:
                        pltpu.make_async_copy(bbuf.at[nz + c], bk.at[w], er.at[w]).start()
                        rcopy(bbuf.at[nz + 1 - c], bk.at[w], es.at[nz + 1 - c], er.at[w], sib).start()
                else:
                    rcopy(a, bk.at[w], es.at[rel * 2 + core], er.at[w], (t, n)).start()

    def drain_pipe():
        def sent_b(d, _):
            t = lax.rem(nz + c + d, nw)
            rcopy(bbuf.at[t], bk.at[w], es.at[t], er.at[w], sib).wait_send()
            return 0

        lax.fori_loop(1, nw, sent_b, 0)
        for p in range(CHUNKS):
            for slot in range(20):
                if slot == 3:
                    continue
                half = 0 if slot < 3 or slot % 4 < 2 else slot % 4 - 1
                hop(p, slot, 0, 0, half, sib).wait_send()
            f1d(p, 0, 0, LOW, sib).wait_send()
            f1d(p, 1, LOW, high, sib).wait_send()
            for k in range(2):
                t1d(p, k, sib).wait_send()
            for k in range(3):
                last(p, k, 0, sib).wait_send()

    stages = (stage0, stage1, stage2, stage3, stage4, stage5, stage6, stage8)
    for k in range(len(stages)):
        for p in range(CHUNKS):
            stages[k](p)
        if k == 6:
            lax.fori_loop(1, nn, send2, 0)
    fill_router()

    def wait_b(d, _):
        t = lax.rem(w + d, nw)
        rcopy(bk.at[t], bk.at[t], es.at[t], er.at[t], sib).wait_recv()
        return 0

    lax.fori_loop(0, nw, wait_b, 0)
    moe = lax.dot_general(
        mix[...], bk.reshape(place.shape[0], HD)[...].astype(F32), DIMS0,
        precision=lax.Precision.HIGHEST, preferred_element_type=F32,
    )
    layer_out[...] = (mx[n].astype(F32) + moe).astype(BF16)

    drain_ring()
    drain_out()
    drain_plane()
    drain_dispatch()
    drain_pipe()


def body(
    hidden, attn_gain, expert_gain, query_weight, key_weight, value_weight, output_weight, router_weight,
    gate_weight, up_weight, down_weight, prefix_keys, prefix_values, cache_keys, cache_values, parents,
    cache_lengths, group_ids, expert_ids, accepted,
):
    tok, width = hidden.shape
    nn = lax.axis_size("narrow")
    nw = lax.axis_size("wide")
    nz = nw // 2
    rows = nw * gate_weight.shape[0] * CAP
    size = rows // CHUNKS
    cache = cache_keys.shape[1]
    vm = pl.BlockSpec(memory_space=pltpu.VMEM)
    sm = pl.BlockSpec(memory_space=pltpu.SMEM)
    hbm = pl.BlockSpec(memory_space=pl.ANY)
    dma = pltpu.SemaphoreType.DMA

    def v(*shape, t=BF16):
        return pltpu.VMEM(shape, t)

    pair = rows // nw // 2
    fw = gate_weight.shape[2]
    scratch = [
        v(tok, width), v(E, width), v(4 * fw, width), v(2 * fw, width), v(cache, HD), v(cache, HD),
        v(*prefix_keys.shape), v(*prefix_values.shape), v(tok, 3 * HD, t=F32),
        v(tok, width), v(nz, 2, 3, 64, HD), v(nz, 2, 64, HD), v(nw, 16, HD), v(nw, 16, HD),
        v(tok, HD), v(tok, HD), v(tok, HD), v(tok, cache, t=F32), v(tok, tok, t=F32), v(tok, tok, t=F32),
        v(cache, tok), v(nn, tok, HD), v(nn, tok, HD), v(nn, tok, HD),
        v(expert_ids.shape[1], tok, t=jnp.int32), v(rows, tok), v(rows, tok, t=F32),
        v(nw, pair, 2, HD), v(nw, pair, 2, HD), v(NY, NX, rows, HD), v(NY, NX, rows, HD),
        v(CHUNKS, 2, 4, size, HD), v(CHUNKS, 4, size, HD), v(CHUNKS, 2, 4, size, HD), v(CHUNKS, 4, size, HD),
        v(CHUNKS, 3, size, HD), v(nw, pair, 2, HD), v(nw, pair, 2, HD),
        dma((16,)), dma((nz // 2, 2)), dma((nz // 2, 2)), dma((nz, 2)), dma((nz, 2)),
        dma((nz // 2,)), dma((nz // 2,)), dma((nz + 1,)), dma((nz + 1,)), dma((nw,)), dma((nw,)),
        dma((nn,)), dma((nn,)), dma((nn,)), dma((nn,)), dma((nw,)), dma((nw,)),
        dma((CHUNKS, 20)), dma((CHUNKS, 20)), dma((CHUNKS, 8)), dma((CHUNKS, 8)), dma((nw,)), dma((nw,)),
    ]
    return pl.pallas_call(
        layer_kernel,
        out_shape=(
            jax.ShapeDtypeStruct((tok, HD), BF16),
            jax.ShapeDtypeStruct(cache_keys.shape, BF16),
            jax.ShapeDtypeStruct(cache_values.shape, BF16),
        ),
        in_specs=[sm, sm] + [vm] * 5 + [hbm] * 13,
        out_specs=(vm, vm, vm),
        scratch_shapes=scratch,
        compiler_params=pltpu.CompilerParams(
            collective_id=0, has_side_effects=True, vmem_limit_bytes=60 * 1024 * 1024
        ),
        name="layer",
    )(
        cache_lengths, accepted, attn_gain[None], expert_gain[None], parents, group_ids[None], expert_ids.T,
        hidden, query_weight, key_weight, value_weight, output_weight, router_weight.T,
        jnp.swapaxes(gate_weight, 1, 2), jnp.swapaxes(up_weight, 1, 2), down_weight,
        prefix_keys, prefix_values, cache_keys, cache_values,
    )


def solution(mesh):
    in_specs = (
        P("wide", None),
        P(),
        P(),
        P("wide", "narrow"),
        P("wide", "narrow"),
        P("wide", "narrow"),
        P("wide", "narrow"),
        P(),
        P("wide", None, "narrow"),
        P("wide", None, "narrow"),
        P("wide", "narrow", None),
        P("wide", None, "narrow"),
        P("wide", None, "narrow"),
        P("wide", None, "narrow"),
        P("wide", None, "narrow"),
        P("wide", None),
        P("wide"),
        P(),
        P("wide", None),
        P("wide"),
    )
    out_specs = (P("wide", "narrow"), P("wide", None, "narrow"), P("wide", None, "narrow"))
    return jax.shard_map(body, mesh=mesh, in_specs=in_specs, out_specs=out_specs, check_vma=False)
```
